32 devices in a mesh: dp: 8 (over z, y), fsdp: 4 (over x, core).
Axes of the slice: x: 2, y: 2, z: 4, core: 2. Of those that a mesh axis runs over, the one named last changes fastest.
Arguments:
- frames_in: bfloat16 [20480, 1024], P(('dp', 'fsdp')), may hold values from -6 to 6
- cotangent: bfloat16 [20480, 1024], P(('dp', 'fsdp')), may hold values from -6 to 6
- lengths: int32 [32, 3], P(('dp', 'fsdp')), may hold values from 0 to 640, as said below
- first_gain: float32 [1024], replicated, may hold values from 0.5 to 1.5
- first_up: bfloat16 [1024, 4096], P(None, 'fsdp'), may hold values from -0.1875 to 0.1875
- first_down: bfloat16 [4096, 1024], P(None, 'fsdp'), may hold values from -0.09375 to 0.09375
- attend_gain: float32 [1024], replicated, may hold values from 0.5 to 1.5
- query_proj: bfloat16 [1024, 1024], P(None, 'fsdp'), may hold values from -0.1875 to 0.1875
- key_proj: bfloat16 [1024, 1024], P(None, 'fsdp'), may hold values from -0.1875 to 0.1875
- value_proj: bfloat16 [1024, 1024], P(None, 'fsdp'), may hold values from -0.1875 to 0.1875
- output_proj: bfloat16 [1024, 1024], P(None, 'fsdp'), may hold values from -1.5 to 1.5
- conv_gain: float32 [1024], replicated, may hold values from 0.5 to 1.5
- conv_expand: bfloat16 [1024, 2048], P(None, 'fsdp'), may hold values from -0.1875 to 0.1875
- conv_kernel: float32 [5, 1024], replicated, may hold values from -2.5 to 2.5
- batch_gain: float32 [1024], replicated, may hold values from 0.5 to 1.5
- batch_shift: float32 [1024], replicated, may hold values from -3 to 3
- conv_project: bfloat16 [1024, 1024], P(None, 'fsdp'), may hold values from -0.1875 to 0.1875
- second_gain: float32 [1024], replicated, may hold values from 0.5 to 1.5
- second_up: bfloat16 [1024, 4096], P(None, 'fsdp'), may hold values from -0.1875 to 0.1875
- second_down: bfloat16 [4096, 1024], P(None, 'fsdp'), may hold values from -0.09375 to 0.09375
- final_gain: float32 [1024], replicated, may hold values from 0.5 to 1.5
Outputs:
- layer_out: bfloat16 [20480, 1024], P(('dp', 'fsdp'))
- input_grad: float32 [20480, 1024], P(('dp', 'fsdp'))
- first_up_grad: float32 [1024, 4096], P(None, 'fsdp')
- first_down_grad: float32 [4096, 1024], P(None, 'fsdp')
- query_grad: float32 [1024, 1024], P(None, 'fsdp')
- key_grad: float32 [1024, 1024], P(None, 'fsdp')
- value_grad: float32 [1024, 1024], P(None, 'fsdp')
- output_grad: float32 [1024, 1024], P(None, 'fsdp')
- expand_grad: float32 [1024, 2048], P(None, 'fsdp')
- project_grad: float32 [1024, 1024], P(None, 'fsdp')
- second_up_grad: float32 [1024, 4096], P(None, 'fsdp')
- second_down_grad: float32 [4096, 1024], P(None, 'fsdp')
- first_gain_grad: float32 [1024], replicated
- attend_gain_grad: float32 [1024], replicated
- conv_gain_grad: float32 [1024], replicated
- second_gain_grad: float32 [1024], replicated
- final_gain_grad: float32 [1024], replicated
- kernel_grad: float32 [5, 1024], replicated
- batch_gain_grad: float32 [1024], replicated
- batch_shift_grad: float32 [1024], replicated
- batch_mean: float32 [1024], replicated
- batch_variance: float32 [1024], replicated
The draws below stay inside these ranges and needn't reach their ends.
Inputs may be any that keep to these rules, and one draw needn't show every extreme that they name: Row r gives the lengths of the utterances packed from frame 0 in buffer r, zero for an empty slot; a row sums to at most 640, and at least one buffer holds a single utterance of exactly 640 frames.
All inputs are finite; a program needn't handle non-finite values.
Results may differ from the reference program's by a relative error of at most 0.018.
Values may be sent and summed in bfloat16 or wider, within the bound.
No kernel may reach another device: no remote copies, remote signals or barrier semaphores. Data moves between devices by JAX's collectives and lax.ppermute only.
A program may use at most 320 MiB of HBM per device.

```python
import jax
import jax.numpy as jnp
from jax import lax

D = 1024
FF = 4096
HEADS = 8
HEAD_DIM = 128
KERNEL = 5
FRAMES = 640
BUFFERS = 32
TOKENS = 20480


def draw_lengths(key, part):
    keys = jax.random.split(jax.random.fold_in(key, 17), 5)
    clip_low = FRAMES * 5 // 32
    clip_high = FRAMES * 25 // 64 + 1
    first = jax.random.randint(keys[0], (BUFFERS,), clip_low, clip_high)
    second = jax.random.randint(keys[1], (BUFFERS,), clip_low, clip_high)
    third = jax.random.randint(keys[2], (BUFFERS,), 0, FRAMES * 3 // 16 + 1)
    pick = jax.random.randint(keys[3], (BUFFERS,), 0, 8)
    forced = jax.random.randint(keys[4], (), 0, BUFFERS)
    rows = jnp.arange(BUFFERS)
    whole = jnp.logical_or(pick == 0, rows == forced)
    zero = jnp.zeros((BUFFERS,), jnp.int32)
    column_one = jnp.where(whole, FRAMES, first)
    column_two = jnp.where(whole, zero, second)
    column_three = jnp.where(whole, zero, third)
    return jnp.stack([column_one, column_two, column_three], axis=1).astype(jnp.int32)


def levels(key, extent, shards, low, high):
    def one(dim, blocks):
        steps = jax.random.uniform(jax.random.fold_in(jax.random.fold_in(key, 6), dim), (blocks,), jnp.float32, low / len(shards), high / len(shards))
        return jnp.repeat(jnp.exp(steps), extent[dim] // blocks).reshape((-1,) + (1,) * (len(extent) - dim - 1))

    level = one(*shards[0])
    for cut in shards[1:]:
        level = level * one(*cut)
    return level


def gaussian(own_key, shape, deviation, bound, shards=(), kind=jnp.bfloat16):
    entries = jax.random.normal(own_key, shape, jnp.float32) * deviation
    if len(shards) > 0:
        entries = levels(own_key, shape, shards, -0.22, 0.18) * entries
    return jnp.clip(entries, min=-bound, max=bound).astype(kind)


def setup_inputs(seed: int = 0) -> dict:
    arg_keys = jax.random.split(jax.random.key(seed), 22)
    return {
        "frames_in": gaussian(arg_keys[0], (TOKENS, D), 1.0, 6.0, ((0, 32),)),
        "cotangent": gaussian(arg_keys[1], (TOKENS, D), 1.0, 6.0, ((0, 32),)),
        "lengths": draw_lengths(jax.random.fold_in(arg_keys[21], 71), 0),
        "first_gain": jnp.clip(1.0 + 0.1 * jax.random.normal(arg_keys[3], (D,), jnp.float32), 0.5, 1.5),
        "first_up": gaussian(arg_keys[4], (D, FF), D ** -0.5, 0.1875, ((1, 4),)),
        "first_down": gaussian(arg_keys[5], (FF, D), FF ** -0.5, 0.09375, ((1, 4),)),
        "attend_gain": jnp.clip(1.0 + 0.1 * jax.random.normal(arg_keys[6], (D,), jnp.float32), 0.5, 1.5),
        "query_proj": gaussian(arg_keys[7], (D, D), D ** -0.5, 0.1875, ((1, 4),)),
        "key_proj": gaussian(arg_keys[8], (D, D), D ** -0.5, 0.1875, ((1, 4),)),
        "value_proj": gaussian(arg_keys[9], (D, D), D ** -0.5, 0.1875, ((1, 4),)),
        "output_proj": gaussian(arg_keys[10], (D, D), (D // 64) ** -0.5, 1.5, ((1, 4),)),
        "conv_gain": jnp.clip(1.0 + 0.1 * jax.random.normal(arg_keys[11], (D,), jnp.float32), 0.5, 1.5),
        "conv_expand": gaussian(arg_keys[12], (D, 2 * D), D ** -0.5, 0.1875, ((1, 4),)),
        "conv_kernel": gaussian(arg_keys[13], (KERNEL, D), KERNEL ** -0.5, 2.5, (), jnp.float32),
        "batch_gain": jnp.clip(1.0 + 0.1 * jax.random.normal(arg_keys[14], (D,), jnp.float32), 0.5, 1.5),
        "batch_shift": gaussian(arg_keys[15], (D,), 0.5, 3.0, (), jnp.float32),
        "conv_project": gaussian(arg_keys[16], (D, D), D ** -0.5, 0.1875, ((1, 4),)),
        "second_gain": jnp.clip(1.0 + 0.1 * jax.random.normal(arg_keys[17], (D,), jnp.float32), 0.5, 1.5),
        "second_up": gaussian(arg_keys[18], (D, FF), D ** -0.5, 0.1875, ((1, 4),)),
        "second_down": gaussian(arg_keys[19], (FF, D), FF ** -0.5, 0.09375, ((1, 4),)),
        "final_gain": jnp.clip(1.0 + 0.1 * jax.random.normal(arg_keys[20], (D,), jnp.float32), 0.5, 1.5),
    }


EXACT = lax.Precision.HIGHEST
EPSILON = 1e-05
MASKED = -1e+30

@jax.custom_vjp
def low(v):
    return lax.optimization_barrier(v.astype(jnp.bfloat16)).astype(jnp.float32)

@jax.custom_vjp
def low_back(v):
    return v

def low_keep(v):
    return (low(v), None)

def low_pass(kept, grad):
    return (grad,)

def back_keep(v):
    return (v, None)

def back_low(kept, grad):
    return (low(grad),)
low.defvjp(low_keep, low_pass)
low_back.defvjp(back_keep, back_low)

def matmul(left, right):
    return jnp.dot(left, right, precision=EXACT, preferred_element_type=jnp.float32)

def norm(value, gain):
    centre = lax.optimization_barrier(jnp.mean(value, axis=-1, keepdims=True))
    centred = value - centre
    inverse = lax.rsqrt(lax.optimization_barrier(jnp.mean(centred * centred, axis=-1, keepdims=True)) + EPSILON)
    return centred * inverse * gain

def layout(row, frames):
    ends = jnp.cumsum(row, dtype=jnp.int32)
    times = jnp.arange(frames, dtype=jnp.int32)
    reached = times[:, None] >= ends[None, :]
    segment = lax.optimization_barrier(jnp.sum(reached.astype(jnp.int32), axis=1, dtype=jnp.int32))
    start = lax.optimization_barrier(jnp.max(jnp.where(reached, ends[None, :], 0), axis=1)).astype(jnp.int32)
    position = (times - start).astype(jnp.float32)
    valid = (times < ends[-1]).astype(jnp.float32)
    return (segment, position, valid)

def rotation(position, half):
    rates = 10000.0 ** (-jnp.arange(half, dtype=jnp.float32) / half)
    angle = position[:, None] * rates[None, :]
    return (jnp.cos(angle), jnp.sin(angle))

def rotate(value, cosine, sine):
    half = value.shape[-1] // 2
    front = value[..., :half]
    behind = value[..., half:]
    cosine = cosine[:, None, :]
    sine = sine[:, None, :]
    return jnp.concatenate([front * cosine - behind * sine, front * sine + behind * cosine], axis=-1)

def depthwise(value, kernel, segment):
    frames = value.shape[0]
    reach = (kernel.shape[0] - 1) // 2
    padded = jnp.pad(value, ((reach, reach), (0, 0)))
    side_segment = jnp.pad(segment, (reach, reach), constant_values=-1)
    result = jnp.zeros(value.shape, jnp.float32)
    for shift_index in range(kernel.shape[0]):
        same = (side_segment[shift_index:shift_index + frames] == segment).astype(jnp.float32)[:, None]
        result = result + kernel[shift_index] * padded[shift_index:shift_index + frames] * same
    return result

def feed_forward(value, gain, up_weight, down_weight):
    normed = low(norm(value, gain))
    inner = low_back(matmul(normed, up_weight))
    acted = low(jax.nn.silu(inner))
    return value + 0.5 * low_back(matmul(acted, down_weight))

def attend(value, gain, query_weight, key_weight, value_weight, output_weight, segment, cosine, sine):
    frames, width = value.shape
    shape = (frames, HEADS, HEAD_DIM)
    normed = low(norm(value, gain))
    query_pre = low_back(matmul(normed, query_weight)).reshape(shape)
    key_pre = low_back(matmul(normed, key_weight)).reshape(shape)
    value_pre = low_back(matmul(normed, value_weight)).reshape(shape)
    query = low(rotate(query_pre, cosine, sine) * HEAD_DIM ** (-0.5))
    keys = low(rotate(key_pre, cosine, sine))
    values = low(value_pre)
    allowed = (segment[:, None] == segment[None, :])[None]
    raw = jnp.einsum('qhe,khe->hqk', query, keys, precision=EXACT)
    scores = low_back(jnp.where(allowed, raw, MASKED))
    highest = lax.optimization_barrier(jnp.max(scores, axis=-1, keepdims=True))
    expanded = jnp.exp(scores - highest)
    probs = low(expanded / lax.optimization_barrier(jnp.sum(expanded, axis=-1, keepdims=True)))
    mixed = jnp.einsum('hqk,khe->qhe', probs, values, precision=EXACT).reshape(frames, width)
    mixed = low(low_back(mixed))
    return value + low_back(matmul(mixed, output_weight))

def conv_front(value, gain, expand_weight, kernel, segment):
    width = value.shape[-1]
    normed = low(norm(value, gain))
    expand = low_back(matmul(normed, expand_weight))
    glued = expand[:, :width] * jax.nn.sigmoid(expand[:, width:])
    return depthwise(glued, kernel, segment)

def reference(frames_in, cotangent, lengths, first_gain, first_up, first_down, attend_gain, query_proj, key_proj, value_proj, output_proj, conv_gain, conv_expand, conv_kernel, batch_gain, batch_shift, conv_project, second_gain, second_up, second_down, final_gain):
    segment, position, valid = jax.vmap(lambda row: layout(row, FRAMES))(lengths)
    params = tuple((item.astype(jnp.float32) for item in (first_gain, first_up, first_down, attend_gain, query_proj, key_proj, value_proj, output_proj, conv_gain, conv_expand, conv_kernel, batch_gain, batch_shift, conv_project, second_gain, second_up, second_down, final_gain)))
    inputs = frames_in.astype(jnp.float32).reshape(BUFFERS, FRAMES, D)
    upstream = cotangent.astype(jnp.float32).reshape(BUFFERS, FRAMES, D)

    def forward(inputs, params):
        p_first_gain, p_first_up, p_first_down, p_attend_gain, p_query, p_key, p_value, p_output, p_conv_gain, p_expand, p_kernel, p_batch_gain, p_batch_shift, p_project, p_second_gain, p_second_up, p_second_down, p_final_gain = params

        def section_one(block):
            value, block_segment, block_position = block
            cosine, sine = rotation(block_position, HEAD_DIM // 2)
            value = feed_forward(value, p_first_gain, p_first_up, p_first_down)
            value = attend(value, p_attend_gain, p_query, p_key, p_value, p_output, block_segment, cosine, sine)
            return (value, conv_front(value, p_conv_gain, p_expand, p_kernel, block_segment))
        middle, mixed = lax.map(jax.checkpoint(section_one), (inputs, segment, position))
        column = valid[..., None]
        count = jnp.sum(valid)
        mean = lax.optimization_barrier(jnp.sum(mixed * column, axis=(0, 1))) / count
        spread = (mixed - mean) * column
        variance = lax.optimization_barrier(jnp.sum(spread * spread, axis=(0, 1))) / count

        def section_two(block):
            value, mixed_block, valid_block = block
            standard = (mixed_block - mean) * lax.rsqrt(variance + EPSILON)
            normal = standard * p_batch_gain + p_batch_shift
            acted = low(jax.nn.silu(normal))
            value = value + low_back(matmul(acted, p_project))
            value = feed_forward(value, p_second_gain, p_second_up, p_second_down)
            return norm(value, p_final_gain) * valid_block[:, None]
        result = lax.map(jax.checkpoint(section_two), (middle, mixed, valid))
        return (result, (mean, variance))
    result, pullback, moments = jax.vjp(forward, inputs, params, has_aux=True)
    input_grad, param_grads = pullback(upstream)
    pg = param_grads
    return (result.reshape(TOKENS, D).astype(jnp.bfloat16), input_grad.reshape(TOKENS, D), pg[1], pg[2], pg[4], pg[5], pg[6], pg[7], pg[9], pg[13], pg[15], pg[16], pg[0], pg[3], pg[8], pg[14], pg[17], pg[10], pg[11], pg[12], moments[0], moments[1])
```

```python
import functools

import jax
import jax.numpy as jnp
from jax import lax
from jax.experimental import pallas as pl
from jax.experimental.pallas import tpu as pltpu
from jax.sharding import PartitionSpec as P

HEADS = 8
HEAD_DIM = 128


EPSILON = 1e-05
MASKED = -1e30
SLICES = 4
VMEM_LIMIT = 60 * 1024 * 1024
COST_SCALE = 0.01
BITS = 7

F32 = jnp.float32
BF16 = jnp.bfloat16


def cost_of(flops, moved):
    return pl.CostEstimate(
        flops=int(flops * COST_SCALE),
        transcendentals=0,
        bytes_accessed=int(moved * COST_SCALE),
    )


def size_of(item):
    return item.size * item.dtype.itemsize


def normalize(value, gain):
    centre = jnp.mean(value, axis=-1, keepdims=True)
    centred = value - centre
    inverse = lax.rsqrt(jnp.mean(centred * centred, axis=-1, keepdims=True) + EPSILON)
    scaled = centred * inverse
    return (scaled * gain, scaled, inverse)


def normalize_back(upstream, scaled, inverse, gain):
    inner = upstream * gain
    first_mean = jnp.mean(inner, axis=-1, keepdims=True)
    second_mean = jnp.mean(inner * scaled, axis=-1, keepdims=True)
    return (
        inverse * (inner - first_mean - scaled * second_mean),
        jnp.sum(upstream * scaled, axis=0, keepdims=True),
    )


def sigmoid(value):
    return 0.5 * jnp.tanh(0.5 * value) + 0.5


def swish_slope(value):
    gate = sigmoid(value)
    return gate * (1.0 + value * (1.0 - gate))


def layout(row, frames):
    ends = jnp.cumsum(row, dtype=jnp.int32)
    times = jnp.arange(frames, dtype=jnp.int32)
    reached = times[:, None] >= ends[None, :]
    segment = jnp.sum(reached.astype(jnp.int32), axis=1, dtype=jnp.int32)
    start = jnp.max(jnp.where(reached, ends[None, :], 0), axis=1)
    position = (times - start).astype(jnp.float32)
    valid = (times < ends[-1]).astype(jnp.float32)
    return (segment, position, valid)


def rotation(position, half):
    rates = 10000.0 ** (-jnp.arange(half, dtype=jnp.float32) / half)
    angle = position[:, None] * rates[None, :]
    cosine, sine = jnp.cos(angle), jnp.sin(angle)
    return (
        jnp.concatenate([cosine, cosine], axis=1),
        jnp.concatenate([-sine, sine], axis=1),
    )


def rotate(value, cosine, sine):
    heads = []
    for start in range(0, value.shape[1], HEAD_DIM):
        head = value[:, start : start + HEAD_DIM]
        heads.append(head * cosine + pltpu.roll(head, HEAD_DIM // 2, 1) * sine)
    return heads[0] if len(heads) == 1 else jnp.concatenate(heads, axis=1)


def loads(spots, pieces, first, width, target, sems):
    half = pieces[2].shape[0]
    quarter = half // 2
    low = pl.multiple_of(spots[4] * half, 16)
    high = pl.multiple_of((1 - spots[4]) * half, 16)
    rows = pieces[0].shape[0]
    beside = pl.multiple_of(spots[6] * rows, 16)
    places = (
        (0, 0, rows),
        (1, 0, rows),
        (2, low, half),
        (2, high, quarter),
        (2, high + quarter, quarter),
        (3, low, half),
        (3, high, quarter),
        (3, high + quarter, quarter),
    )
    return [
        pltpu.make_async_copy(
            piece.at[pl.ds(beside if index == 1 else 0, extent), pl.ds(first, width)],
            target(place, start, extent),
            sems.at[index],
        )
        for index, (piece, (place, start, extent)) in enumerate(zip(pieces, places))
    ]


PIECES = 8
WAITS = ((0,), (1,), (2, 3, 4), (5, 6, 7))


def forward_kernel(first, width, counts, prologue, epilogue, spots, *refs):
    whole_count, block_count, full_out_count, block_out_count = counts
    refs = list(refs)

    def take(number):
        taken = refs[:number]
        del refs[:number]
        return taken

    wholes = take(whole_count)
    blocks = take(block_count)
    pieces = take(PIECES)
    full_outs = take(full_out_count)
    block_outs = take(block_out_count)
    left, weights, sems = refs
    step = pl.program_id(0)
    copies = loads(
        spots,
        pieces,
        first,
        width,
        lambda place, start, extent: weights.at[place, pl.ds(start, extent), :],
        sems,
    )

    @pl.when(step == 0)
    def _():
        for copy in copies:
            copy.start()
        left[...] = prologue(wholes, full_outs)

    for place, group in enumerate(WAITS):

        @pl.when(step == place)
        def _():
            for index in group:
                copies[index].wait()

    result = jnp.dot(left[...], weights[step], preferred_element_type=F32)
    epilogue(result, wholes, blocks, block_outs)


def forward_product(clock, pieces, first, width, wholes, blocks, full_outs, block_outs, prologue, epilogue):
    depth = pieces[0].shape[0]
    frames = wholes[0].shape[0]
    turned = lambda step, spots: (0, spots[step])
    fixed = lambda step, spots: (0, 0)
    in_specs = [pl.BlockSpec(item.shape, fixed, pipeline_mode=pl.Buffered(1)) for item in wholes]
    in_specs += [pl.BlockSpec((frames, columns), turned) for _, columns in blocks]
    in_specs += [pl.BlockSpec(memory_space=pl.ANY)] * PIECES
    out_shape = [jax.ShapeDtypeStruct(shape, kind) for shape, kind in full_outs]
    out_shape += [
        jax.ShapeDtypeStruct((frames, SLICES * columns), kind) for kind, columns in block_outs
    ]
    out_specs = [pl.BlockSpec(shape, fixed) for shape, _ in full_outs]
    out_specs += [pl.BlockSpec((frames, columns), turned) for _, columns in block_outs]
    moved = sum(size_of(item) for item in wholes) + sum(size_of(item) for item, _ in blocks)
    moved += sum(size_of(item) for item in out_shape) + depth * width * SLICES * 2
    outs = pl.pallas_call(
        functools.partial(
            forward_kernel,
            first,
            width,
            (len(wholes), len(blocks), len(full_outs), len(block_outs)),
            prologue,
            epilogue,
        ),
        out_shape=out_shape,
        grid_spec=pltpu.PrefetchScalarGridSpec(
            num_scalar_prefetch=1,
            grid=(SLICES,),
            in_specs=in_specs,
            out_specs=out_specs,
            scratch_shapes=[
                pltpu.VMEM((frames, depth), BF16),
                pltpu.VMEM((SLICES, depth, width), BF16),
                pltpu.SemaphoreType.DMA((PIECES,)),
            ],
        ),
        compiler_params=pltpu.CompilerParams(
            dimension_semantics=("arbitrary",), vmem_limit_bytes=VMEM_LIMIT
        ),
        cost_estimate=cost_of(2 * frames * depth * width * SLICES, moved),
    )(clock.spots, *wholes, *[item for item, _ in blocks], *pieces)
    return clock(*outs)


def normed_prologue(wholes, full_outs):
    value, gain = wholes[:2]
    normed = normalize(value[...].astype(F32), gain[...])[0].astype(BF16)
    full_outs[0][...] = normed
    return normed


def plain_prologue(wholes, full_outs):
    return wholes[0][...]


def up_epilogue(result, wholes, blocks, outs):
    inner, acted = outs
    inner[...] = result.astype(BF16)
    acted[...] = (result * sigmoid(result)).astype(BF16)


def up(value, gain, pieces, clock):
    frames, width = value.shape
    columns = pieces[0].shape[1]
    return forward_product(
        clock,
        pieces,
        0,
        columns,
        [value, gain],
        [],
        [((frames, width), BF16)],
        [(BF16, columns), (BF16, columns)],
        normed_prologue,
        up_epilogue,
    )


def add_epilogue(scale, result, wholes, blocks, outs):
    outs[0][...] = blocks[0][...].astype(F32) + scale * result


def added(left, value, scale, pieces, first, columns, clock):
    return forward_product(
        clock,
        pieces,
        first,
        columns,
        [left],
        [(value, columns)],
        [],
        [(F32, columns)],
        plain_prologue,
        functools.partial(add_epilogue, scale),
    )[0]


def attend_epilogue(result, wholes, blocks, outs):
    cosine, sine = wholes[2][...], wholes[3][...]
    columns = result.shape[1] // 3
    scale = HEAD_DIM ** (-0.5)
    outs[0][...] = (rotate(result[:, :columns], cosine, sine) * scale).astype(BF16)
    outs[1][...] = rotate(result[:, columns : 2 * columns], cosine, sine).astype(BF16)
    outs[2][...] = result[:, 2 * columns :].astype(BF16)


def attend_front(value, gain, cosine, sine, pieces, columns, clock):
    return forward_product(
        clock,
        pieces,
        0,
        3 * columns,
        [value, gain, cosine, sine],
        [],
        [(value.shape, BF16)],
        [(BF16, columns)] * 3,
        normed_prologue,
        attend_epilogue,
    )


def store_epilogue(result, wholes, blocks, outs):
    outs[0][...] = result.astype(outs[0].dtype)


def expanded(value, gain, pieces, first, columns, clock):
    return forward_product(
        clock,
        pieces,
        first,
        columns,
        [value, gain],
        [],
        [(value.shape, BF16)],
        [(F32, columns)],
        normed_prologue,
        store_epilogue,
    )


def backward_kernel(first, widths, counts, chunk, epilogue, spots, *refs):
    left_count, whole_count, block_count, full_out_count, block_out_count = counts
    refs = list(refs)

    def take(number):
        taken = refs[:number]
        del refs[:number]
        return taken

    lefts = take(left_count)
    wholes = take(whole_count)
    blocks = take(block_count)
    pieces = take(PIECES)
    full_outs = take(full_out_count)
    block_outs = take(block_out_count)
    left, weights, sems = refs
    step = pl.program_id(0)
    width = sum(widths)

    @pl.when(step == 0)
    def _():
        copies = loads(
            spots,
            pieces,
            first,
            width,
            lambda place, start, extent: weights.at[
                pl.ds(start, extent), pl.ds(place * width, width)
            ],
            sems,
        )
        for copy in copies:
            copy.start()
        for place in range(SLICES):
            offset = place * width
            for item, columns in zip(lefts, widths):
                start = pl.multiple_of(spots[place] * columns, 128)
                left[:, pl.ds(offset, columns)] = item[:, pl.ds(start, columns)]
                offset += columns
        for copy in copies:
            copy.wait()

    rows = weights[pl.ds(pl.multiple_of(step * chunk, 16), chunk), :]
    result = lax.dot_general(
        left[...], rows, (((1,), (1,)), ((), ())), preferred_element_type=F32
    )
    epilogue(spots, result, wholes, blocks, full_outs, block_outs)


def backward_product(clock, pieces, first, lefts, wholes, blocks, chunk, full_outs, block_outs, epilogue):
    rows = pieces[0].shape[0]
    frames = lefts[0].shape[0]
    widths = tuple(item.shape[1] // SLICES for item in lefts)
    width = sum(widths)
    fixed = lambda step, spots: (0, 0)
    along = lambda step, spots: (0, step)
    in_specs = [
        pl.BlockSpec(item.shape, fixed, pipeline_mode=pl.Buffered(1)) for item in lefts + wholes
    ]
    in_specs += [pl.BlockSpec((frames, chunk), along) for _ in blocks]
    in_specs += [pl.BlockSpec(memory_space=pl.ANY)] * PIECES
    out_shape = [jax.ShapeDtypeStruct(shape, kind) for shape, kind in full_outs]
    out_shape += [jax.ShapeDtypeStruct((frames, rows), kind) for kind in block_outs]
    out_specs = [pl.BlockSpec(shape, fixed) for shape, _ in full_outs]
    out_specs += [pl.BlockSpec((frames, chunk), along) for _ in block_outs]
    moved = sum(size_of(item) for item in lefts + wholes + blocks)
    moved += sum(size_of(item) for item in out_shape) + rows * width * SLICES * 2
    outs = pl.pallas_call(
        functools.partial(
            backward_kernel,
            first,
            widths,
            (len(lefts), len(wholes), len(blocks), len(full_outs), len(block_outs)),
            chunk,
            epilogue,
        ),
        out_shape=out_shape,
        grid_spec=pltpu.PrefetchScalarGridSpec(
            num_scalar_prefetch=1,
            grid=(rows // chunk,),
            in_specs=in_specs,
            out_specs=out_specs,
            scratch_shapes=[
                pltpu.VMEM((frames, SLICES * width), BF16),
                pltpu.VMEM((rows, SLICES * width), BF16),
                pltpu.SemaphoreType.DMA((PIECES,)),
            ],
        ),
        compiler_params=pltpu.CompilerParams(
            dimension_semantics=("arbitrary",), vmem_limit_bytes=VMEM_LIMIT
        ),
        cost_estimate=cost_of(2 * frames * rows * width * SLICES, moved),
    )(clock.spots, *lefts, *wholes, *blocks, *pieces)
    return clock(*outs)


def slope_epilogue(spots, result, wholes, blocks, full_outs, block_outs):
    grad = (result * swish_slope(blocks[0][...].astype(F32))).astype(BF16)
    block_outs[0][...] = grad
    parts = len(full_outs) // 2
    for index, out in enumerate(full_outs):
        columns = out.shape[1]
        start = (index % parts) * columns

        @pl.when(pl.program_id(0) == spots[(1, 3)[index // parts]])
        def _():
            out[...] = grad[:, start : start + columns]


def down_back(outer, inner, pieces, parts, clock):
    frames, depth = inner.shape
    columns = depth // SLICES
    part = ((frames, columns // parts), BF16)
    *sent, grad = backward_product(
        clock, pieces, 0, [outer], [], [inner], columns, [part] * (2 * parts), [BF16], slope_epilogue
    )
    return grad, sent


def send_slices(spots, source, sent):
    columns = source.shape[1] // SLICES
    for offset, place in ((0, 1), (columns, 3)):
        start = pl.multiple_of(spots[place] * columns, 128)
        sent[:, pl.ds(offset, columns)] = source[:, pl.ds(start, columns)]


def norm_back_store(scale, spots, result, value, gain, upstream, outs):
    _, scaled, inverse = normalize(value[...].astype(F32), 1.0)
    delta, gain_grad = normalize_back(result, scaled, inverse, gain[...])
    grad = upstream[...] + delta
    outs[0][...] = grad
    outs[1][...] = gain_grad
    outs[2][...] = (scale * grad).astype(BF16)
    send_slices(spots, outs[2], outs[3])


def norm_epilogue(scale, spots, result, wholes, blocks, full_outs, block_outs):
    norm_back_store(scale, spots, result, wholes[0], wholes[1], wholes[2], full_outs)


def norm_back_product(lefts, value, gain, upstream, pieces, first, scale, clock):
    frames, width = upstream.shape
    return backward_product(
        clock,
        pieces,
        first,
        lefts,
        [value, gain, upstream],
        [],
        width,
        [
            ((frames, width), F32),
            ((1, width), F32),
            ((frames, width), BF16),
            ((frames, width // 2), BF16),
        ],
        [],
        functools.partial(norm_epilogue, scale),
    )


def plain_epilogue(spots, result, wholes, blocks, full_outs, block_outs):
    block_outs[0][...] = result.astype(block_outs[0].dtype)


def plain_back(left, kind, pieces, first, clock):
    return backward_product(
        clock, pieces, first, [left], [], [], pieces[0].shape[0], [], [kind], plain_epilogue
    )[0]


def up_back_kernel(scale, spots, left, value, gain, upstream, *refs):
    pieces = refs[:PIECES]
    out, gain_out, low_out, sent, total, weights, sems = refs[PIECES:]
    step = pl.program_id(0)
    width = weights.shape[2]
    copies = loads(
        spots,
        pieces,
        0,
        width,
        lambda place, start, extent: weights.at[place, pl.ds(start, extent), :],
        sems,
    )

    @pl.when(step == 0)
    def _():
        for copy in copies:
            copy.start()

    for place, group in enumerate(WAITS):

        @pl.when(step == place)
        def _():
            for index in group:
                copies[index].wait()

    result = lax.dot_general(
        left[...], weights[step], (((1,), (1,)), ((), ())), preferred_element_type=F32
    )

    @pl.when(step == 0)
    def _():
        total[...] = result

    @pl.when(step > 0)
    def _():
        total[...] += result

    @pl.when(step == SLICES - 1)
    def _():
        norm_back_store(
            scale, spots, total[...], value, gain, upstream, (out, gain_out, low_out, sent)
        )


def up_back(left, value, gain, upstream, pieces, scale, clock):
    frames, width = upstream.shape
    columns = pieces[0].shape[1]
    fixed = lambda step, spots: (0, 0)
    single = functools.partial(pl.BlockSpec, index_map=fixed, pipeline_mode=pl.Buffered(1))
    moved = size_of(left) + size_of(value) + 2 * size_of(upstream) + width * columns * 8
    outs = pl.pallas_call(
        functools.partial(up_back_kernel, scale),
        out_shape=[
            jax.ShapeDtypeStruct((frames, width), F32),
            jax.ShapeDtypeStruct((1, width), F32),
            jax.ShapeDtypeStruct((frames, width), BF16),
            jax.ShapeDtypeStruct((frames, width // 2), BF16),
        ],
        grid_spec=pltpu.PrefetchScalarGridSpec(
            num_scalar_prefetch=1,
            grid=(SLICES,),
            in_specs=[
                pl.BlockSpec((frames, columns), lambda step, spots: (0, spots[step])),
                single(value.shape),
                single(gain.shape),
                single(upstream.shape),
            ]
            + [pl.BlockSpec(memory_space=pl.ANY)] * PIECES,
            out_specs=[
                pl.BlockSpec((frames, width), fixed),
                pl.BlockSpec((1, width), fixed),
                pl.BlockSpec((frames, width), fixed),
                pl.BlockSpec((frames, width // 2), fixed),
            ],
            scratch_shapes=[
                pltpu.VMEM((frames, width), F32),
                pltpu.VMEM((SLICES, width, columns), BF16),
                pltpu.SemaphoreType.DMA((PIECES,)),
            ],
        ),
        compiler_params=pltpu.CompilerParams(
            dimension_semantics=("arbitrary",), vmem_limit_bytes=VMEM_LIMIT
        ),
        cost_estimate=cost_of(2 * frames * width * columns * SLICES, moved),
    )(clock.spots, left, value, gain, upstream, *pieces)
    return clock(*outs)


def weight_kernel(count, spots, mine, paired, *refs):
    ups, (far, own) = refs[: 4 * count], refs[-2:]
    dims = (((0,), (0,)), ((), ()))
    offset = 0
    for index in range(count):
        near_own, pair_own, near_far, pair_far = ups[4 * index : 4 * index + 4]
        columns = near_own.shape[1]
        for out, first, second in ((far, near_far, pair_far), (own, near_own, pair_own)):
            result = lax.dot_general(mine[...], first[...], dims, preferred_element_type=F32)
            result += lax.dot_general(paired[...], second[...], dims, preferred_element_type=F32)
            out[:, offset : offset + columns] = result.astype(out.dtype)
        offset += columns


def in_parts(near, sent):
    parts = len(sent) // 2
    return [
        (near, parts * SLICES, part, (sent[part], 0), (sent[parts + part], 0))
        for part in range(parts)
    ]


def packed_pair(near, sent):
    return (near, SLICES, 0, (sent, 0), (sent, 1))


def weight_grads(left, ups, chunk, clock, first=0, depth=None, packed=None, place=0, base=None):
    rows = left[0] if isinstance(left, tuple) else left
    frames = ups[0][0].shape[0]
    depth = depth or rows.shape[1]
    skipped = first // chunk
    in_specs = []
    operands = []
    for core in range(2):
        if isinstance(left, tuple):
            operands.append(left[core])
            index = lambda step, spots: (0, step + skipped)
        else:
            operands.append(left)
            index = lambda step, spots, core=core: (spots[5 + core], step + skipped)
        in_specs.append(pl.BlockSpec((frames, chunk), index))
    widths = []
    for near, parts, part, *beside in ups:
        columns = near.shape[1] // parts
        for which, (item, block) in zip((0, 2), beside):
            operands += [near, item]
            stride = parts // SLICES
            mine = lambda step, spots, which=which, part=part, stride=stride: (
                0,
                spots[which] * stride + part,
            )
            theirs = lambda step, spots, block=block: (0, block)
            in_specs += [pl.BlockSpec((frames, columns), index) for index in (mine, theirs)]
        widths.append(columns)
    total = sum(widths)
    down = lambda step, spots: (step, place)
    count = len(operands)
    if base is not None:
        operands += base
        in_specs += [pl.BlockSpec(memory_space=pl.ANY)] * 2
    outs = pl.pallas_call(
        functools.partial(weight_kernel, len(ups)),
        input_output_aliases={} if base is None else {1 + count: 0, 2 + count: 1},
        out_shape=[jax.ShapeDtypeStruct((depth, packed or total), BF16)] * 2,
        grid_spec=pltpu.PrefetchScalarGridSpec(
            num_scalar_prefetch=1,
            grid=(depth // chunk,),
            in_specs=in_specs,
            out_specs=[pl.BlockSpec((chunk, total), down)] * 2,
        ),
        compiler_params=pltpu.CompilerParams(
            dimension_semantics=("arbitrary",), vmem_limit_bytes=VMEM_LIMIT
        ),
        cost_estimate=cost_of(
            8 * frames * depth * total, 4 * frames * depth + 8 * frames * total + 4 * depth * total
        ),
    )(clock.spots, *operands)
    return clock(*outs)


def attention_kernel(query, keys, values, across, along, mixed, summary):
    head = pl.program_id(0)
    scores = lax.dot_general(
        query[...], keys[...], (((1,), (1,)), ((), ())), preferred_element_type=F32
    )
    scores = jnp.where(across[...] == along[...], scores, MASKED)
    highest = jnp.max(scores, axis=-1, keepdims=True)
    raised = jnp.exp(scores - highest)
    totals = jnp.sum(raised, axis=-1, keepdims=True)
    probs = (raised * (1.0 / totals)).astype(BF16)
    mixed[...] = jnp.dot(probs, values[...], preferred_element_type=F32).astype(BF16)
    lane = lax.broadcasted_iota(jnp.int32, summary.shape, 1)
    kept = jnp.where(head == 0, jnp.zeros_like(summary), summary[...])
    summary[...] = jnp.where(lane == head, highest + jnp.log(totals), kept)


def attention(query, keys, values, across, along, clock):
    (query,) = clock(query)
    frames, width = query.shape
    head_block = pl.BlockSpec((frames, HEAD_DIM), lambda head: (0, head))
    fixed = lambda head: (0, 0)
    outs = pl.pallas_call(
        attention_kernel,
        out_shape=[
            jax.ShapeDtypeStruct((frames, width), BF16),
            jax.ShapeDtypeStruct((frames, HEAD_DIM), F32),
        ],
        grid=(width // HEAD_DIM,),
        in_specs=[head_block] * 3
        + [pl.BlockSpec((frames, 1), fixed), pl.BlockSpec((1, frames), fixed)],
        out_specs=[head_block, pl.BlockSpec((frames, HEAD_DIM), fixed)],
        compiler_params=pltpu.CompilerParams(
            dimension_semantics=("arbitrary",), vmem_limit_bytes=VMEM_LIMIT
        ),
        cost_estimate=cost_of(4 * frames * frames * width, 8 * frames * width),
    )(query, keys, values, across, along)
    return clock(*outs)


def attention_back_kernel(
    spots, query, keys, values, upstream, summary, across, along, cosine, sine, *outs
):
    head = pl.program_id(0)
    at = pl.ds(pl.multiple_of(head * HEAD_DIM, HEAD_DIM), HEAD_DIM)
    query_out, keys_out, values_out = outs[:3]
    contract_last = (((1,), (1,)), ((), ()))
    contract_first = (((0,), (0,)), ((), ()))
    scores = lax.dot_general(query[...], keys[...], contract_last, preferred_element_type=F32)
    scores = jnp.where(across[...] == along[...], scores, MASKED)
    lane = lax.broadcasted_iota(jnp.int32, summary.shape, 1)
    level = jnp.sum(jnp.where(lane == head, summary[...], 0.0), axis=-1, keepdims=True)
    probs = jnp.exp(scores - level)
    grads = lax.dot_general(upstream[...], values[...], contract_last, preferred_element_type=F32)
    balance = jnp.sum(probs * grads, axis=-1, keepdims=True)
    scores_grad = (probs * (grads - balance)).astype(BF16)
    values_out[:, at] = lax.dot_general(
        probs.astype(BF16), upstream[...], contract_first, preferred_element_type=F32
    ).astype(BF16)
    scale = HEAD_DIM ** (-0.5)
    query_back = jnp.dot(scores_grad, keys[...], preferred_element_type=F32)
    query_out[:, at] = (rotate(query_back, cosine[...], -sine[...]) * scale).astype(BF16)
    keys_back = lax.dot_general(scores_grad, query[...], contract_first, preferred_element_type=F32)
    keys_out[:, at] = rotate(keys_back, cosine[...], -sine[...]).astype(BF16)

    @pl.when(head == pl.num_programs(0) - 1)
    def _():
        for out, sent in zip(outs[:3], outs[3:]):
            send_slices(spots, out, sent)


def attention_back(query, keys, values, upstream, summary, across, along, cosine, sine, clock):
    frames, width = query.shape
    head_block = pl.BlockSpec((frames, HEAD_DIM), lambda head, spots: (0, head))
    fixed = lambda head, spots: (0, 0)
    whole = pl.BlockSpec((frames, HEAD_DIM), fixed)
    outs = pl.pallas_call(
        attention_back_kernel,
        out_shape=[jax.ShapeDtypeStruct((frames, width), BF16)] * 3
        + [jax.ShapeDtypeStruct((frames, width // 2), BF16)] * 3,
        grid_spec=pltpu.PrefetchScalarGridSpec(
            num_scalar_prefetch=1,
            grid=(width // HEAD_DIM,),
            in_specs=[head_block] * 4
            + [
                whole,
                pl.BlockSpec((frames, 1), fixed),
                pl.BlockSpec((1, frames), fixed),
                whole,
                whole,
            ],
            out_specs=[pl.BlockSpec((frames, width), fixed)] * 3
            + [pl.BlockSpec((frames, width // 2), fixed)] * 3,
        ),
        compiler_params=pltpu.CompilerParams(
            dimension_semantics=("arbitrary",), vmem_limit_bytes=VMEM_LIMIT
        ),
        cost_estimate=cost_of(10 * frames * frames * width, 14 * frames * width),
    )(clock.spots, query, keys, values, upstream, summary, across, along, cosine, sine)
    outs = clock(*outs)
    return outs[:3], outs[3:]


def bare_call(kernel, outs, operands, clock, flops=0):
    fixed = lambda spots: (0, 0)
    results = pl.pallas_call(
        kernel,
        out_shape=[jax.ShapeDtypeStruct(shape, kind) for shape, kind in outs],
        grid_spec=pltpu.PrefetchScalarGridSpec(
            num_scalar_prefetch=1,
            grid=(),
            in_specs=[
                pl.BlockSpec(item.shape, lambda spots, item=item: (0,) * item.ndim)
                for item in operands
            ],
            out_specs=[pl.BlockSpec(shape, fixed) for shape, _ in outs],
        ),
        compiler_params=pltpu.CompilerParams(vmem_limit_bytes=VMEM_LIMIT),
        cost_estimate=cost_of(flops, sum(size_of(item) for item in operands)),
    )(clock.spots, *operands)
    return clock(*results)


def final_kernel(spots, value, gain, valid, cotangent, out, grad_out, gain_out, low_out, sent):
    normed, scaled, inverse = normalize(value[...], gain[...])
    out[...] = (normed * valid[...]).astype(BF16)
    upstream = cotangent[...].astype(F32) * valid[...]
    grad, gain_grad = normalize_back(upstream, scaled, inverse, gain[...])
    grad_out[...] = grad
    gain_out[...] = gain_grad
    low_out[...] = (0.5 * grad).astype(BF16)
    send_slices(spots, low_out, sent)


def final(value, gain, valid, cotangent, clock):
    shape = value.shape
    return bare_call(
        final_kernel,
        [
            (shape, BF16),
            (shape, F32),
            (gain.shape, F32),
            (shape, BF16),
            ((shape[0], shape[1] // 2), BF16),
        ],
        [value, gain, valid, cotangent],
        clock,
    )


TAPS = 5
REACH = 2
CONV_BLOCK = 256


def convolve_kernel(spots, values, gates, taps, same, valid, mixed, shares):
    glued = values[...] * sigmoid(gates[...])
    frames = glued.shape[0]
    result = jnp.zeros_like(glued)
    for index in range(TAPS):
        moved = pltpu.roll(glued, (REACH - index) % frames, 0) if index != REACH else glued
        result += taps[index : index + 1, :] * moved * same[:, index : index + 1]
    mixed[...] = result
    counted = jnp.maximum(jnp.sum(valid[...]), 1.0)
    local_sum = jnp.sum(result * valid[...], axis=0, keepdims=True)
    spread = (result - local_sum / counted) * valid[...]
    shares[0:1, :] = local_sum
    shares[1:2, :] = jnp.sum(spread * spread, axis=0, keepdims=True)


def convolve(expand, taps, same, valid, clock):
    frames, width = expand.shape[0], expand.shape[1] // 2
    blocks = width // CONV_BLOCK
    along = lambda step, spots: (0, step)
    fixed = lambda step, spots: (0, 0)
    outs = pl.pallas_call(
        convolve_kernel,
        out_shape=[
            jax.ShapeDtypeStruct((frames, width), F32),
            jax.ShapeDtypeStruct((2, width), F32),
        ],
        grid_spec=pltpu.PrefetchScalarGridSpec(
            num_scalar_prefetch=1,
            grid=(blocks,),
            in_specs=[
                pl.BlockSpec((frames, CONV_BLOCK), along),
                pl.BlockSpec((frames, CONV_BLOCK), lambda step, spots: (0, step + blocks)),
                pl.BlockSpec((TAPS, CONV_BLOCK), along),
                pl.BlockSpec(same.shape, fixed),
                pl.BlockSpec(valid.shape, fixed),
            ],
            out_specs=[
                pl.BlockSpec((frames, CONV_BLOCK), along),
                pl.BlockSpec((2, CONV_BLOCK), along),
            ],
        ),
        compiler_params=pltpu.CompilerParams(
            dimension_semantics=("arbitrary",), vmem_limit_bytes=VMEM_LIMIT
        ),
        cost_estimate=cost_of(0, size_of(expand)),
    )(clock.spots, expand, expand, taps, same, valid)
    return clock(*outs)


def batch_prologue(wholes, full_outs):
    mixed, mean, inverse, gain, shift = (item[...] for item in wholes)
    normal = (mixed - mean) * inverse * gain + shift
    acted = (normal * sigmoid(normal)).astype(BF16)
    full_outs[0][...] = acted
    return acted


def projected(mixed, mean, inverse, gain, shift, value, pieces, first, columns, clock):
    return forward_product(
        clock,
        pieces,
        first,
        columns,
        [mixed, mean, inverse, gain, shift],
        [(value, columns)],
        [(mixed.shape, BF16)],
        [(F32, columns)],
        batch_prologue,
        functools.partial(add_epilogue, 1.0),
    )


def project_epilogue(spots, result, wholes, blocks, full_outs, block_outs):
    mixed, mean, inverse, gain, shift, valid = (item[...] for item in wholes)
    standard = (mixed - mean) * inverse
    grad = result * swish_slope(standard * gain + shift)
    full_outs[0][...] = grad
    counted = grad * valid
    full_outs[1][0:1, :] = jnp.sum(counted, axis=0, keepdims=True)
    full_outs[1][1:2, :] = jnp.sum(counted * standard, axis=0, keepdims=True)


def project_back(outer, mixed, mean, inverse, gain, shift, valid, pieces, first, clock):
    frames, width = mixed.shape
    return backward_product(
        clock,
        pieces,
        first,
        [outer],
        [mixed, mean, inverse, gain, shift, valid],
        [],
        width,
        [((frames, width), F32), ((2, width), F32)],
        [],
        project_epilogue,
    )


def convolve_back_kernel(
    spots, grad, mixed, values, gates, taps, same, valid, sums, mean, inverse, gain, count, out, taps_out, *sent
):
    step = pl.program_id(0)
    frames, columns = grad.shape
    width = out.shape[1] // 2
    standard = (mixed[...] - mean[...]) * inverse[...]
    share = (sums[0:1, :] + standard * sums[1:2, :]) / count[...]
    upstream = gain[...] * inverse[...] * (grad[...] - valid[...] * share)
    gate = sigmoid(gates[...])
    glued = values[...] * gate
    back = jnp.zeros_like(upstream)
    for index in range(TAPS):
        term = upstream * same[:, index : index + 1]
        if index == REACH:
            moved, returned = glued, term
        else:
            moved = pltpu.roll(glued, (REACH - index) % frames, 0)
            returned = pltpu.roll(term, (index - REACH) % frames, 0)
        taps_out[index : index + 1, :] = jnp.sum(term * moved, axis=0, keepdims=True)
        back += taps[index : index + 1, :] * returned
    low = pl.multiple_of(step * columns, 128)
    high = pl.multiple_of(width + step * columns, 128)
    out[:, pl.ds(low, columns)] = (back * gate).astype(BF16)
    out[:, pl.ds(high, columns)] = (back * glued * (1.0 - gate)).astype(BF16)

    @pl.when(step == pl.num_programs(0) - 1)
    def _():
        for part, place in zip(sent, (1, 3)):
            start = pl.multiple_of(spots[place] * part.shape[1], 128)
            part[...] = out[:, pl.ds(start, part.shape[1])]


def convolve_back(grad, mixed, expand, taps, same, valid, sums, mean, inverse, gain, count, clock):
    frames, width = mixed.shape
    blocks = width // CONV_BLOCK
    along = lambda step, spots: (0, step)
    fixed = lambda step, spots: (0, 0)
    wide = pl.BlockSpec((frames, CONV_BLOCK), along)
    row = pl.BlockSpec((1, CONV_BLOCK), along)
    outs = pl.pallas_call(
        convolve_back_kernel,
        out_shape=[
            jax.ShapeDtypeStruct((frames, 2 * width), BF16),
            jax.ShapeDtypeStruct((TAPS, width), F32),
        ]
        + [jax.ShapeDtypeStruct((frames, width // 2), BF16)] * 2,
        grid_spec=pltpu.PrefetchScalarGridSpec(
            num_scalar_prefetch=1,
            grid=(blocks,),
            in_specs=[
                wide,
                wide,
                wide,
                pl.BlockSpec((frames, CONV_BLOCK), lambda step, spots: (0, step + blocks)),
                pl.BlockSpec((TAPS, CONV_BLOCK), along),
                pl.BlockSpec(same.shape, fixed),
                pl.BlockSpec(valid.shape, fixed),
                pl.BlockSpec((2, CONV_BLOCK), along),
                row,
                row,
                row,
                pl.BlockSpec((1, 1), fixed),
            ],
            out_specs=[
                pl.BlockSpec((frames, 2 * width), fixed),
                pl.BlockSpec((TAPS, CONV_BLOCK), along),
            ]
            + [pl.BlockSpec((frames, width // 2), fixed)] * 2,
        ),
        compiler_params=pltpu.CompilerParams(
            dimension_semantics=("arbitrary",), vmem_limit_bytes=VMEM_LIMIT
        ),
        cost_estimate=cost_of(0, size_of(expand) * 2),
    )(clock.spots, grad, mixed, expand, expand, taps, same, valid, sums, mean, inverse, gain, count)
    return clock(*outs)


def split_kernel(spots, kept_value, kept_moving, sent_value, sent_moving, kept, sent):
    kept[...] = kept_value[...].astype(F32) + kept_moving[...].astype(F32)
    sent[...] = (sent_value[...].astype(F32) + sent_moving[...].astype(F32)).astype(BF16)


def split_sum(value, moving, which, clock):
    rows, columns = value.shape
    half = rows // 2
    steps = 2 if half * columns >= 2**18 else 1
    block = (half // steps, columns)
    kept = pl.BlockSpec(block, lambda step, spots: (spots[BITS + which] * steps + step, 0))
    sent = pl.BlockSpec(block, lambda step, spots: ((1 - spots[BITS + which]) * steps + step, 0))
    along = pl.BlockSpec(block, lambda step, spots: (step, 0))
    outs = pl.pallas_call(
        split_kernel,
        out_shape=[
            jax.ShapeDtypeStruct((half, columns), F32),
            jax.ShapeDtypeStruct((half, columns), BF16),
        ],
        grid_spec=pltpu.PrefetchScalarGridSpec(
            num_scalar_prefetch=1,
            grid=(steps,),
            in_specs=[kept, kept, sent, sent],
            out_specs=[along, along],
        ),
        compiler_params=pltpu.CompilerParams(
            dimension_semantics=("arbitrary",), vmem_limit_bytes=VMEM_LIMIT
        ),
        cost_estimate=cost_of(0, size_of(value)),
    )(clock.spots, value, moving, value, moving)
    return clock(*outs)


def sum_kernel(spots, value, moving, out):
    out[...] = (value[...].astype(F32) + moving[...].astype(F32)).astype(BF16)


def unfold_kernel(widths, size, spots, value, *outs):
    step = pl.program_id(0)
    bits = size.bit_length() - 1
    block = value.shape[0] // size
    for item in range(size // 2):
        place = step
        for bit in range(bits - 1):
            place += ((item >> bit) & 1) << (bits - 1 - bit)
        rows = value[pl.ds(pl.multiple_of(place * block, 16), block), :].astype(F32)
        offset = 0
        for out, width in zip(outs, widths):
            out[item * block : (item + 1) * block, :] = rows[:, offset : offset + width]
            offset += width


def unfold(value, size, widths, clock):
    rows, columns = value.shape
    outs = pl.pallas_call(
        functools.partial(unfold_kernel, widths, size),
        out_shape=[jax.ShapeDtypeStruct((rows, width), F32) for width in widths],
        grid_spec=pltpu.PrefetchScalarGridSpec(
            num_scalar_prefetch=1,
            grid=(2,),
            in_specs=[pl.BlockSpec((rows, columns), lambda step, spots: (0, 0))],
            out_specs=[
                pl.BlockSpec((rows // 2, width), lambda step, spots: (step, 0))
                for width in widths
            ],
        ),
        compiler_params=pltpu.CompilerParams(
            dimension_semantics=("arbitrary",), vmem_limit_bytes=VMEM_LIMIT
        ),
        cost_estimate=cost_of(0, size_of(value)),
    )(clock.spots, value)
    return clock(*outs)


class Clock:
    def __init__(self, spots):
        self.spots = spots

    def __call__(self, *values):
        self.spots, *values = lax.optimization_barrier((self.spots,) + values)
        return values

    def send(self, value, axis, mask):
        (value,) = self(value)
        return swapped(value, axis, mask)


class Gather:
    def __init__(self, slices, clock):
        self.own = slices[0] if len(slices) == 1 else jnp.concatenate(slices, axis=1)
        self.half = self.own.shape[0] // 2
        self.clock = clock
        self.beside()

    def cross(self):
        crossing = lax.dynamic_slice_in_dim(
            self.own, half_sent() * self.half, self.half, axis=0
        )
        self.across = self.clock.send(crossing, "fsdp", 2)

    def beside(self):
        self.own_beside = joined(self.own)

    def forward(self):
        quarter = self.half // 2
        self.across, self.own_beside = self.clock(self.across, self.own_beside)
        self.first = swapped(self.across[:quarter], "dp", 1)
        self.second = swapped(self.across[quarter:], "dp", 2)
        self.across_beside = swapped(self.across, "fsdp", 1)

    def turn(self):
        self.first, self.second, self.across_beside = self.clock(
            self.first, self.second, self.across_beside
        )
        self.first_beside = swapped(self.first, "fsdp", 1)
        self.second_beside = swapped(self.second, "fsdp", 1)

    def finish(self):
        self.first_beside, self.second_beside = self.clock(
            self.first_beside, self.second_beside
        )
        self.pieces = (
            self.own,
            self.own_beside,
            self.across,
            self.first,
            self.second,
            self.across_beside,
            self.first_beside,
            self.second_beside,
        )


def half_sent():
    place = lax.axis_index("dp")
    return (place ^ (place >> 1)) & 1


class Reduction:
    def __init__(self, far, own, clock):
        self.place = lax.axis_index("dp")
        self.size = lax.axis_size("dp")
        self.clock = clock
        self.value = own
        self.moving = clock.send(far, "fsdp", 2)
        self.mask = 1
        self.whole = None
        self.widening = False

    def advance(self):
        (moving,) = self.clock(self.moving)
        which = self.mask.bit_length() - 1
        self.value, sent = split_sum(self.value, moving, which, self.clock)
        self.moving = swapped(sent, "dp", self.mask)
        self.mask *= 2

    def piece(self):
        while self.mask < self.size:
            self.advance()
        (moving,) = self.clock(self.moving)
        return bare_call(sum_kernel, [(moving.shape, BF16)], [self.value, moving], self.clock)[0]

    def gather(self):
        self.whole = lax.all_gather(self.piece(), "dp", axis=0, tiled=True)

    def widen(self):
        if not self.widening:
            self.value = self.piece()
            self.widening = True
        else:
            self.value = self.joined()
            (self.value,) = self.clock(self.value)
        self.mask //= 2
        self.moving = swapped(self.value, "dp", self.mask)

    def joined(self):
        (moving,) = self.clock(self.moving)
        bit = (self.place // self.mask) & 1
        return jnp.where(
            bit == 0,
            jnp.concatenate([self.value, moving], axis=0),
            jnp.concatenate([moving, self.value], axis=0),
        )

    def result(self, widths=None):
        if self.whole is None:
            while self.mask > 1:
                self.widen()
            return [self.joined().astype(F32)]
        (whole,) = self.clock(self.whole)
        return unfold(whole, self.size, widths or (whole.shape[1],), self.clock)


def joined(value):
    groups = [[i, i + 1] for i in range(0, lax.axis_size("fsdp"), 2)]
    return lax.all_gather(value, "fsdp", axis=0, tiled=True, axis_index_groups=groups)


class Doubling:
    def __init__(self, value, clock):
        self.value = value
        self.clock = clock
        self.left = [
            (axis, 1 << bit)
            for axis in ("fsdp", "dp")
            for bit in range(lax.axis_size(axis).bit_length() - 1)
        ]
        self.send()

    def send(self):
        axis, mask = self.left.pop(0)
        self.moving = self.clock.send(self.value, axis, mask)

    def step(self):
        (moving,) = self.clock(self.moving)
        self.value = self.value + moving
        if self.left:
            self.send()

    def finish(self):
        while self.left:
            self.step()
        self.step()
        return self.value


def swapped(value, axis, mask):
    size = lax.axis_size(axis)
    return lax.ppermute(value, axis, [(i, i ^ mask) for i in range(size)])


def spread_sum(rows):
    axes = ("dp", "fsdp")
    count = lax.axis_size(axes)
    copies = jnp.broadcast_to(rows[None], (count,) + rows.shape)
    return lax.all_to_all(copies, axes, 0, 0, tiled=True)


def neighbours(segment, taps):
    frames = segment.shape[0]
    reach = (taps - 1) // 2
    side = jnp.pad(segment, (reach, reach), constant_values=-1)
    columns = [side[index : index + frames] == segment for index in range(taps)]
    return jnp.pad(jnp.stack(columns, axis=1).astype(F32), ((0, 0), (0, 8 - taps)))


def body(
    frames_in,
    cotangent,
    lengths,
    first_gain,
    first_up,
    first_down,
    attend_gain,
    query_proj,
    key_proj,
    value_proj,
    output_proj,
    conv_gain,
    conv_expand,
    conv_kernel,
    batch_gain,
    batch_shift,
    conv_project,
    second_gain,
    second_up,
    second_down,
    final_gain,
):
    frames, width = frames_in.shape
    slot = lax.axis_index("fsdp")
    part = half_sent()
    row, rows = lax.axis_index("dp"), lax.axis_size("dp")
    bits = [(row >> which) & 1 for which in range(rows.bit_length() - 1)]
    spots = jnp.stack(
        [slot, slot ^ 1, slot ^ 2, slot ^ 3, part, slot & 1, 1 - (slot & 1)] + bits
    ).astype(jnp.int32)
    clock = Clock(spots)
    segment, position, valid = layout(lengths[0], frames)
    cosine, sine = rotation(position, HEAD_DIM // 2)
    column = valid[:, None]
    seg_across, seg_along = segment[:, None], segment[None, :]
    first_gain, attend_gain, conv_gain, second_gain, final_gain, batch_gain, batch_shift = (
        item[None]
        for item in (
            first_gain,
            attend_gain,
            conv_gain,
            second_gain,
            final_gain,
            batch_gain,
            batch_shift,
        )
    )
    same = neighbours(segment, conv_kernel.shape[0])
    narrow = query_proj.shape[1]
    wide = conv_expand.shape[1]

    def pair(value):
        return clock.send(value, "fsdp", 1)

    groups = [
        Gather(slices, clock)
        for slices in (
            (first_up,),
            (first_down,),
            (query_proj, key_proj, value_proj),
            (output_proj, conv_expand, conv_project),
            (second_up,),
            (second_down,),
        )
    ]
    first_ups, first_downs, attends, convs, second_ups, second_downs = groups
    first_ups.cross()
    first_downs.cross()
    first_ups.forward()
    attends.cross()
    first_ups.turn()
    first_ups.finish()
    first_downs.forward()
    convs.cross()
    first_normed, first_inner, first_acted = up(frames_in, first_gain, first_ups.pieces, clock)
    first_downs.turn()
    first_downs.finish()
    attends.forward()
    second_ups.cross()
    after_first = added(
        first_acted, frames_in, 0.5, first_downs.pieces, 0, first_down.shape[1], clock
    )
    attends.turn()
    attends.finish()
    attend_normed, query, keys, values = attend_front(
        after_first, attend_gain, cosine, sine, attends.pieces, narrow, clock
    )
    convs.forward()
    second_downs.cross()
    attended, summary = attention(query, keys, values, seg_across, seg_along, clock)
    convs.turn()
    convs.finish()
    after_attend = added(attended, after_first, 1.0, convs.pieces, 0, narrow, clock)
    second_ups.forward()
    conv_normed, expand = expanded(after_attend, conv_gain, convs.pieces, narrow, wide, clock)
    second_ups.turn()

    mixed, local = convolve(expand, conv_kernel, same, column, clock)
    local = jnp.concatenate([local, jnp.broadcast_to(jnp.sum(valid), (2, 128))], axis=1)
    shares = spread_sum(local)
    second_ups.finish()
    second_downs.forward()
    (shares,) = clock(shares)
    counts = shares[:, 0, width : width + 1]
    count = jnp.sum(counts)
    sums = shares[:, 0, :width]
    mean = jnp.sum(sums, axis=0) / count
    offsets = sums / jnp.maximum(counts, 1.0) - mean
    variance = jnp.sum(shares[:, 1, :width] + counts * offsets * offsets, axis=0) / count
    deviation_inverse = lax.rsqrt(variance + EPSILON)
    mean_row, inverse_row = mean[None], deviation_inverse[None]
    conv_acted, after_conv = projected(
        mixed,
        mean_row,
        inverse_row,
        batch_gain,
        batch_shift,
        after_attend,
        convs.pieces,
        narrow + wide,
        narrow,
        clock,
    )
    second_downs.turn()
    second_downs.finish()
    second_normed, second_inner, second_acted = up(
        after_conv, second_gain, second_ups.pieces, clock
    )
    pair_acted, pair_normed = pair(second_acted), pair(second_normed)
    after_second = added(
        second_acted, after_conv, 0.5, second_downs.pieces, 0, second_down.shape[1], clock
    )
    pair_acted, pair_normed = clock(pair_acted, pair_normed)
    layer_out, upstream, final_gain_grad, outer, sent = final(
        after_second, final_gain, column, cotangent, clock
    )
    (pair_outer,) = clock(pair(sent))
    both_conv_acted, both_conv, both_attended, both_attend, both_first_acted, both_first = (
        joined(item)
        for item in clock(
            conv_acted, conv_normed, attended, attend_normed, first_acted, first_normed
        )
    )

    second_down_sum = Reduction(
        *weight_grads((second_acted, pair_acted), [packed_pair(outer, pair_outer)], 1024, clock), clock
    )
    inner_grad, sent = down_back(outer, second_inner, second_downs.pieces, 2, clock)
    pair_inner = [pair(item) for item in sent]
    upstream, second_gain_grad, outer, sent = up_back(
        inner_grad, after_conv, second_gain, upstream, second_ups.pieces, 1.0, clock
    )
    pair_inner = clock(*pair_inner)
    pair_outer = pair(sent)
    normal_grad, local = project_back(
        outer,
        mixed,
        mean_row,
        inverse_row,
        batch_gain,
        batch_shift,
        column,
        convs.pieces,
        narrow + wide,
        clock,
    )
    (local,) = clock(local)
    pieces = spread_sum(local)
    second_up_part = weight_grads(
        (second_normed, pair_normed), in_parts(inner_grad, pair_inner), 512, clock
    )
    pair_outer, both_conv_acted = clock(pair_outer, both_conv_acted)
    conv_part = weight_grads(
        both_conv_acted,
        [packed_pair(outer, pair_outer)],
        512,
        clock,
        packed=wide + narrow,
        place=wide // narrow,
    )
    (pieces,) = clock(pieces)
    second_up_sum = Reduction(*second_up_part, clock)
    second_down_sum.advance()
    sums = jnp.sum(pieces, axis=0)
    expand_back, kernel_local, *sent = convolve_back(
        normal_grad,
        mixed,
        expand,
        conv_kernel,
        same,
        column,
        sums,
        mean_row,
        inverse_row,
        batch_gain,
        count.reshape(1, 1),
        clock,
    )
    pair_back = [pair(item) for item in sent]
    upstream, conv_gain_grad, outer, sent = norm_back_product(
        [expand_back], after_attend, conv_gain, upstream, convs.pieces, narrow, 1.0, clock
    )
    pair_outer = pair(sent)
    second_down_sum.advance()
    *pair_back, both_conv = clock(*pair_back, both_conv)
    conv_part = weight_grads(
        both_conv,
        [(expand_back, SLICES, 0, *((item, 0) for item in pair_back))],
        512,
        clock,
        packed=wide + narrow,
        base=conv_part,
    )
    conv_sum = Reduction(*conv_part, clock)
    mixed_back = plain_back(outer, BF16, convs.pieces, 0, clock)
    second_up_sum.advance()
    second_down_sum.advance()
    backs, sent = attention_back(
        query, keys, values, mixed_back, summary, seg_across, seg_along, cosine, sine, clock
    )
    pair_outer, both_attended = clock(pair_outer, both_attended)
    pair_backs = [pair(item) for item in sent]
    conv_sum.advance()
    second_down_sum.gather()
    attend_part = weight_grads(
        both_attended, [packed_pair(outer, pair_outer)], 512, clock, packed=4 * narrow, place=3
    )
    *pair_backs, both_attend = clock(*pair_backs, both_attend)
    attend_part = weight_grads(
        both_attend,
        [packed_pair(item, other) for item, other in zip(backs, pair_backs)],
        512,
        clock,
        packed=4 * narrow,
        base=attend_part,
    )
    attend_sum = Reduction(*attend_part, clock)
    second_up_sum.advance()
    upstream, attend_gain_grad, outer, sent = norm_back_product(
        backs, after_first, attend_gain, upstream, attends.pieces, 0, 0.5, clock
    )
    pair_outer = pair(sent)
    conv_sum.advance()
    pair_outer, both_first_acted = clock(pair_outer, both_first_acted)
    first_down_sum = Reduction(
        *weight_grads(both_first_acted, [packed_pair(outer, pair_outer)], 1024, clock), clock
    )
    second_up_sum.advance()
    inner_grad, sent = down_back(outer, first_inner, first_downs.pieces, 1, clock)
    pair_inner = [pair(item) for item in sent]
    second_up_sum.gather()
    pair_inner = clock(*pair_inner)
    attend_sum.advance()
    conv_sum.advance()
    upstream, first_gain_grad, _, _ = up_back(
        inner_grad, frames_in, first_gain, upstream, first_ups.pieces, 1.0, clock
    )
    (both_first,) = clock(both_first)
    half = width // 2
    first_up_low, first_up_high = (
        Reduction(
            *weight_grads(both_first, in_parts(inner_grad, pair_inner), half, clock, start, half),
            clock,
        )
        for start in (0, half)
    )
    minor = jnp.concatenate(
        [
            first_gain_grad,
            attend_gain_grad,
            conv_gain_grad,
            second_gain_grad,
            final_gain_grad,
            kernel_local,
        ]
    )
    minors = Doubling(minor, clock)
    first_down_sum.advance()
    attend_sum.advance()
    conv_sum.gather()
    minors.step()
    first_up_low.advance()
    attend_sum.advance()
    first_down_sum.advance()
    minors.step()
    first_up_high.advance()
    attend_sum.gather()
    first_up_low.advance()
    first_down_sum.advance()
    minors.step()
    (second_down_grad,) = second_down_sum.result()
    first_up_high.advance()
    first_up_low.advance()
    first_down_sum.gather()
    first_up_high.advance()
    first_up_low.widen()
    minors.step()
    (second_up_grad,) = second_up_sum.result()
    first_up_high.widen()
    first_up_low.widen()
    first_up_high.widen()
    first_up_low.widen()
    first_up_high.widen()
    minor_sums = minors.finish()
    expand_grad, project_grad = conv_sum.result((wide, narrow))
    query_grad, key_grad, value_grad, output_grad = attend_sum.result((narrow,) * 4)
    first_up_grad = jnp.concatenate(first_up_low.result() + first_up_high.result(), axis=0)
    (first_up_grad,) = clock(first_up_grad)
    (first_down_grad,) = first_down_sum.result()
    shift_grad, scale_grad = sums
    taps = conv_kernel.shape[0]
    return (
        layer_out,
        upstream,
        first_up_grad,
        first_down_grad,
        query_grad,
        key_grad,
        value_grad,
        output_grad,
        expand_grad,
        project_grad,
        second_up_grad,
        second_down_grad,
        minor_sums[0],
        minor_sums[1],
        minor_sums[2],
        minor_sums[3],
        minor_sums[4],
        minor_sums[5 : 5 + taps],
        scale_grad,
        shift_grad,
        mean,
        variance,
    )


def solution(mesh):
    placed = (
        P(("dp", "fsdp"), None),
        P(("dp", "fsdp"), None),
        P(("dp", "fsdp"), None),
        P(),
        P(None, "fsdp"),
        P(None, "fsdp"),
        P(),
        P(None, "fsdp"),
        P(None, "fsdp"),
        P(None, "fsdp"),
        P(None, "fsdp"),
        P(),
        P(None, "fsdp"),
        P(),
        P(),
        P(),
        P(None, "fsdp"),
        P(),
        P(None, "fsdp"),
        P(None, "fsdp"),
        P(),
    )
    return jax.shard_map(
        body,
        mesh=mesh,
        in_specs=placed,
        out_specs=(
            P(("dp", "fsdp"), None),
            P(("dp", "fsdp"), None),
            P(None, "fsdp"),
            P(None, "fsdp"),
            P(None, "fsdp"),
            P(None, "fsdp"),
            P(None, "fsdp"),
            P(None, "fsdp"),
            P(None, "fsdp"),
            P(None, "fsdp"),
            P(None, "fsdp"),
            P(None, "fsdp"),
            P(),
            P(),
            P(),
            P(),
            P(),
            P(),
            P(),
            P(),
            P(),
            P(),
        ),
        check_vma=False,
    )
```

```python
import functools

import jax
import jax.numpy as jnp
from jax import lax
from jax.experimental import pallas as pl
from jax.experimental.pallas import tpu as pltpu
from jax.sharding import PartitionSpec as P

HEADS = 8
HEAD_DIM = 128


EPSILON = 1e-05
MASKED = -1e30
SLICES = 4
VMEM_LIMIT = 60 * 1024 * 1024
COST_SCALE = 0.01
BITS = 7

F32 = jnp.float32
BF16 = jnp.bfloat16


def cost_of(flops, moved):
    return pl.CostEstimate(
        flops=int(flops * COST_SCALE),
        transcendentals=0,
        bytes_accessed=int(moved * COST_SCALE),
    )


def size_of(item):
    return item.size * item.dtype.itemsize


def normalize(value, gain):
    centre = jnp.mean(value, axis=-1, keepdims=True)
    centred = value - centre
    inverse = lax.rsqrt(jnp.mean(centred * centred, axis=-1, keepdims=True) + EPSILON)
    scaled = centred * inverse
    return (scaled * gain, scaled, inverse)


def normalize_back(upstream, scaled, inverse, gain):
    inner = upstream * gain
    first_mean = jnp.mean(inner, axis=-1, keepdims=True)
    second_mean = jnp.mean(inner * scaled, axis=-1, keepdims=True)
    return (
        inverse * (inner - first_mean - scaled * second_mean),
        jnp.sum(upstream * scaled, axis=0, keepdims=True),
    )


def sigmoid(value):
    return 0.5 * jnp.tanh(0.5 * value) + 0.5


def swish_slope(value):
    gate = sigmoid(value)
    return gate * (1.0 + value * (1.0 - gate))


def layout(row, frames):
    ends = jnp.cumsum(row, dtype=jnp.int32)
    times = jnp.arange(frames, dtype=jnp.int32)
    reached = times[:, None] >= ends[None, :]
    segment = jnp.sum(reached.astype(jnp.int32), axis=1, dtype=jnp.int32)
    start = jnp.max(jnp.where(reached, ends[None, :], 0), axis=1)
    position = (times - start).astype(jnp.float32)
    valid = (times < ends[-1]).astype(jnp.float32)
    return (segment, position, valid)


def rotation(position, half):
    rates = 10000.0 ** (-jnp.arange(half, dtype=jnp.float32) / half)
    angle = position[:, None] * rates[None, :]
    cosine, sine = jnp.cos(angle), jnp.sin(angle)
    return (
        jnp.concatenate([cosine, cosine], axis=1),
        jnp.concatenate([-sine, sine], axis=1),
    )


def rotate(value, cosine, sine):
    heads = []
    for start in range(0, value.shape[1], HEAD_DIM):
        head = value[:, start : start + HEAD_DIM]
        heads.append(head * cosine + pltpu.roll(head, HEAD_DIM // 2, 1) * sine)
    return heads[0] if len(heads) == 1 else jnp.concatenate(heads, axis=1)


def loads(spots, pieces, first, width, target, sems):
    half = pieces[2].shape[0]
    quarter = half // 2
    low = pl.multiple_of(spots[4] * half, 16)
    high = pl.multiple_of((1 - spots[4]) * half, 16)
    rows = pieces[0].shape[0]
    beside = pl.multiple_of(spots[6] * rows, 16)
    places = (
        (0, 0, rows),
        (1, 0, rows),
        (2, low, half),
        (2, high, quarter),
        (2, high + quarter, quarter),
        (3, low, half),
        (3, high, quarter),
        (3, high + quarter, quarter),
    )
    return [
        pltpu.make_async_copy(
            piece.at[pl.ds(beside if index == 1 else 0, extent), pl.ds(first, width)],
            target(place, start, extent),
            sems.at[index],
        )
        for index, (piece, (place, start, extent)) in enumerate(zip(pieces, places))
    ]


PIECES = 8
WAITS = ((0,), (1,), (2, 3, 4), (5, 6, 7))


def forward_kernel(first, width, counts, prologue, epilogue, spots, *refs):
    whole_count, block_count, full_out_count, block_out_count = counts
    refs = list(refs)

    def take(number):
        taken = refs[:number]
        del refs[:number]
        return taken

    wholes = take(whole_count)
    blocks = take(block_count)
    pieces = take(PIECES)
    full_outs = take(full_out_count)
    block_outs = take(block_out_count)
    left, weights, sems = refs
    step = pl.program_id(0)
    copies = loads(
        spots,
        pieces,
        first,
        width,
        lambda place, start, extent: weights.at[place, pl.ds(start, extent), :],
        sems,
    )

    @pl.when(step == 0)
    def _():
        for copy in copies:
            copy.start()
        left[...] = prologue(wholes, full_outs)

    for place, group in enumerate(WAITS):

        @pl.when(step == place)
        def _():
            for index in group:
                copies[index].wait()

    result = jnp.dot(left[...], weights[step], preferred_element_type=F32)
    epilogue(result, wholes, blocks, block_outs)


def forward_product(clock, pieces, first, width, wholes, blocks, full_outs, block_outs, prologue, epilogue):
    depth = pieces[0].shape[0]
    frames = wholes[0].shape[0]
    turned = lambda step, spots: (0, spots[step])
    fixed = lambda step, spots: (0, 0)
    in_specs = [pl.BlockSpec(item.shape, fixed, pipeline_mode=pl.Buffered(1)) for item in wholes]
    in_specs += [pl.BlockSpec((frames, columns), turned) for _, columns in blocks]
    in_specs += [pl.BlockSpec(memory_space=pl.ANY)] * PIECES
    out_shape = [jax.ShapeDtypeStruct(shape, kind) for shape, kind in full_outs]
    out_shape += [
        jax.ShapeDtypeStruct((frames, SLICES * columns), kind) for kind, columns in block_outs
    ]
    out_specs = [pl.BlockSpec(shape, fixed) for shape, _ in full_outs]
    out_specs += [pl.BlockSpec((frames, columns), turned) for _, columns in block_outs]
    moved = sum(size_of(item) for item in wholes) + sum(size_of(item) for item, _ in blocks)
    moved += sum(size_of(item) for item in out_shape) + depth * width * SLICES * 2
    outs = pl.pallas_call(
        functools.partial(
            forward_kernel,
            first,
            width,
            (len(wholes), len(blocks), len(full_outs), len(block_outs)),
            prologue,
            epilogue,
        ),
        out_shape=out_shape,
        grid_spec=pltpu.PrefetchScalarGridSpec(
            num_scalar_prefetch=1,
            grid=(SLICES,),
            in_specs=in_specs,
            out_specs=out_specs,
            scratch_shapes=[
                pltpu.VMEM((frames, depth), BF16),
                pltpu.VMEM((SLICES, depth, width), BF16),
                pltpu.SemaphoreType.DMA((PIECES,)),
            ],
        ),
        compiler_params=pltpu.CompilerParams(
            dimension_semantics=("arbitrary",), vmem_limit_bytes=VMEM_LIMIT
        ),
        cost_estimate=cost_of(2 * frames * depth * width * SLICES, moved),
    )(clock.spots, *wholes, *[item for item, _ in blocks], *pieces)
    return clock(*outs)


def normed_prologue(wholes, full_outs):
    value, gain = wholes[:2]
    normed = normalize(value[...].astype(F32), gain[...])[0].astype(BF16)
    full_outs[0][...] = normed
    return normed


def plain_prologue(wholes, full_outs):
    return wholes[0][...]


def up_epilogue(result, wholes, blocks, outs):
    inner, acted = outs
    inner[...] = result.astype(BF16)
    acted[...] = (result * sigmoid(result)).astype(BF16)


def up(value, gain, pieces, clock):
    frames, width = value.shape
    columns = pieces[0].shape[1]
    return forward_product(
        clock,
        pieces,
        0,
        columns,
        [value, gain],
        [],
        [((frames, width), BF16)],
        [(BF16, columns), (BF16, columns)],
        normed_prologue,
        up_epilogue,
    )


def add_epilogue(scale, result, wholes, blocks, outs):
    outs[0][...] = blocks[0][...].astype(F32) + scale * result


def added(left, value, scale, pieces, first, columns, clock):
    return forward_product(
        clock,
        pieces,
        first,
        columns,
        [left],
        [(value, columns)],
        [],
        [(F32, columns)],
        plain_prologue,
        functools.partial(add_epilogue, scale),
    )[0]


def attend_epilogue(result, wholes, blocks, outs):
    cosine, sine = wholes[2][...], wholes[3][...]
    columns = result.shape[1] // 3
    scale = HEAD_DIM ** (-0.5)
    outs[0][...] = (rotate(result[:, :columns], cosine, sine) * scale).astype(BF16)
    outs[1][...] = rotate(result[:, columns : 2 * columns], cosine, sine).astype(BF16)
    outs[2][...] = result[:, 2 * columns :].astype(BF16)


def attend_front(value, gain, cosine, sine, pieces, columns, clock):
    return forward_product(
        clock,
        pieces,
        0,
        3 * columns,
        [value, gain, cosine, sine],
        [],
        [(value.shape, BF16)],
        [(BF16, columns)] * 3,
        normed_prologue,
        attend_epilogue,
    )


def store_epilogue(result, wholes, blocks, outs):
    outs[0][...] = result.astype(outs[0].dtype)


def expanded(value, gain, pieces, first, columns, clock):
    return forward_product(
        clock,
        pieces,
        first,
        columns,
        [value, gain],
        [],
        [(value.shape, BF16)],
        [(F32, columns)],
        normed_prologue,
        store_epilogue,
    )


def backward_kernel(first, widths, counts, chunk, epilogue, spots, *refs):
    left_count, whole_count, block_count, full_out_count, block_out_count = counts
    refs = list(refs)

    def take(number):
        taken = refs[:number]
        del refs[:number]
        return taken

    lefts = take(left_count)
    wholes = take(whole_count)
    blocks = take(block_count)
    pieces = take(PIECES)
    full_outs = take(full_out_count)
    block_outs = take(block_out_count)
    left, weights, sems = refs
    step = pl.program_id(0)
    width = sum(widths)

    @pl.when(step == 0)
    def _():
        copies = loads(
            spots,
            pieces,
            first,
            width,
            lambda place, start, extent: weights.at[
                pl.ds(start, extent), pl.ds(place * width, width)
            ],
            sems,
        )
        for copy in copies:
            copy.start()
        for place in range(SLICES):
            offset = place * width
            for item, columns in zip(lefts, widths):
                start = pl.multiple_of(spots[place] * columns, 128)
                left[:, pl.ds(offset, columns)] = item[:, pl.ds(start, columns)]
                offset += columns
        for copy in copies:
            copy.wait()

    rows = weights[pl.ds(pl.multiple_of(step * chunk, 16), chunk), :]
    result = lax.dot_general(
        left[...], rows, (((1,), (1,)), ((), ())), preferred_element_type=F32
    )
    epilogue(spots, result, wholes, blocks, full_outs, block_outs)


def backward_product(clock, pieces, first, lefts, wholes, blocks, chunk, full_outs, block_outs, epilogue):
    rows = pieces[0].shape[0]
    frames = lefts[0].shape[0]
    widths = tuple(item.shape[1] // SLICES for item in lefts)
    width = sum(widths)
    fixed = lambda step, spots: (0, 0)
    along = lambda step, spots: (0, step)
    in_specs = [
        pl.BlockSpec(item.shape, fixed, pipeline_mode=pl.Buffered(1)) for item in lefts + wholes
    ]
    in_specs += [pl.BlockSpec((frames, chunk), along) for _ in blocks]
    in_specs += [pl.BlockSpec(memory_space=pl.ANY)] * PIECES
    out_shape = [jax.ShapeDtypeStruct(shape, kind) for shape, kind in full_outs]
    out_shape += [jax.ShapeDtypeStruct((frames, rows), kind) for kind in block_outs]
    out_specs = [pl.BlockSpec(shape, fixed) for shape, _ in full_outs]
    out_specs += [pl.BlockSpec((frames, chunk), along) for _ in block_outs]
    moved = sum(size_of(item) for item in lefts + wholes + blocks)
    moved += sum(size_of(item) for item in out_shape) + rows * width * SLICES * 2
    outs = pl.pallas_call(
        functools.partial(
            backward_kernel,
            first,
            widths,
            (len(lefts), len(wholes), len(blocks), len(full_outs), len(block_outs)),
            chunk,
            epilogue,
        ),
        out_shape=out_shape,
        grid_spec=pltpu.PrefetchScalarGridSpec(
            num_scalar_prefetch=1,
            grid=(rows // chunk,),
            in_specs=in_specs,
            out_specs=out_specs,
            scratch_shapes=[
                pltpu.VMEM((frames, SLICES * width), BF16),
                pltpu.VMEM((rows, SLICES * width), BF16),
                pltpu.SemaphoreType.DMA((PIECES,)),
            ],
        ),
        compiler_params=pltpu.CompilerParams(
            dimension_semantics=("arbitrary",), vmem_limit_bytes=VMEM_LIMIT
        ),
        cost_estimate=cost_of(2 * frames * rows * width * SLICES, moved),
    )(clock.spots, *lefts, *wholes, *blocks, *pieces)
    return clock(*outs)


def slope_epilogue(spots, result, wholes, blocks, full_outs, block_outs):
    grad = (result * swish_slope(blocks[0][...].astype(F32))).astype(BF16)
    block_outs[0][...] = grad
    parts = len(full_outs) // 2
    for index, out in enumerate(full_outs):
        columns = out.shape[1]
        start = (index % parts) * columns

        @pl.when(pl.program_id(0) == spots[(1, 3)[index // parts]])
        def _():
            out[...] = grad[:, start : start + columns]


def down_back(outer, inner, pieces, parts, clock):
    frames, depth = inner.shape
    columns = depth // SLICES
    part = ((frames, columns // parts), BF16)
    *sent, grad = backward_product(
        clock, pieces, 0, [outer], [], [inner], columns, [part] * (2 * parts), [BF16], slope_epilogue
    )
    return grad, sent


def send_slices(spots, source, sent):
    columns = source.shape[1] // SLICES
    for offset, place in ((0, 1), (columns, 3)):
        start = pl.multiple_of(spots[place] * columns, 128)
        sent[:, pl.ds(offset, columns)] = source[:, pl.ds(start, columns)]


def norm_back_store(scale, spots, result, value, gain, upstream, outs):
    _, scaled, inverse = normalize(value[...].astype(F32), 1.0)
    delta, gain_grad = normalize_back(result, scaled, inverse, gain[...])
    grad = upstream[...] + delta
    outs[0][...] = grad
    outs[1][...] = gain_grad
    outs[2][...] = (scale * grad).astype(BF16)
    send_slices(spots, outs[2], outs[3])


def norm_epilogue(scale, spots, result, wholes, blocks, full_outs, block_outs):
    norm_back_store(scale, spots, result, wholes[0], wholes[1], wholes[2], full_outs)


def norm_back_product(lefts, value, gain, upstream, pieces, first, scale, clock):
    frames, width = upstream.shape
    return backward_product(
        clock,
        pieces,
        first,
        lefts,
        [value, gain, upstream],
        [],
        width,
        [
            ((frames, width), F32),
            ((1, width), F32),
            ((frames, width), BF16),
            ((frames, width // 2), BF16),
        ],
        [],
        functools.partial(norm_epilogue, scale),
    )


def plain_epilogue(spots, result, wholes, blocks, full_outs, block_outs):
    block_outs[0][...] = result.astype(block_outs[0].dtype)


def plain_back(left, kind, pieces, first, clock):
    return backward_product(
        clock, pieces, first, [left], [], [], pieces[0].shape[0], [], [kind], plain_epilogue
    )[0]


def up_back_kernel(scale, spots, left, value, gain, upstream, *refs):
    pieces = refs[:PIECES]
    out, gain_out, low_out, sent, total, weights, sems = refs[PIECES:]
    step = pl.program_id(0)
    width = weights.shape[2]
    copies = loads(
        spots,
        pieces,
        0,
        width,
        lambda place, start, extent: weights.at[place, pl.ds(start, extent), :],
        sems,
    )

    @pl.when(step == 0)
    def _():
        for copy in copies:
            copy.start()

    for place, group in enumerate(WAITS):

        @pl.when(step == place)
        def _():
            for index in group:
                copies[index].wait()

    result = lax.dot_general(
        left[...], weights[step], (((1,), (1,)), ((), ())), preferred_element_type=F32
    )

    @pl.when(step == 0)
    def _():
        total[...] = result

    @pl.when(step > 0)
    def _():
        total[...] += result

    @pl.when(step == SLICES - 1)
    def _():
        norm_back_store(
            scale, spots, total[...], value, gain, upstream, (out, gain_out, low_out, sent)
        )


def up_back(left, value, gain, upstream, pieces, scale, clock):
    frames, width = upstream.shape
    columns = pieces[0].shape[1]
    fixed = lambda step, spots: (0, 0)
    single = functools.partial(pl.BlockSpec, index_map=fixed, pipeline_mode=pl.Buffered(1))
    moved = size_of(left) + size_of(value) + 2 * size_of(upstream) + width * columns * 8
    outs = pl.pallas_call(
        functools.partial(up_back_kernel, scale),
        out_shape=[
            jax.ShapeDtypeStruct((frames, width), F32),
            jax.ShapeDtypeStruct((1, width), F32),
            jax.ShapeDtypeStruct((frames, width), BF16),
            jax.ShapeDtypeStruct((frames, width // 2), BF16),
        ],
        grid_spec=pltpu.PrefetchScalarGridSpec(
            num_scalar_prefetch=1,
            grid=(SLICES,),
            in_specs=[
                pl.BlockSpec((frames, columns), lambda step, spots: (0, spots[step])),
                single(value.shape),
                single(gain.shape),
                single(upstream.shape),
            ]
            + [pl.BlockSpec(memory_space=pl.ANY)] * PIECES,
            out_specs=[
                pl.BlockSpec((frames, width), fixed),
                pl.BlockSpec((1, width), fixed),
                pl.BlockSpec((frames, width), fixed),
                pl.BlockSpec((frames, width // 2), fixed),
            ],
            scratch_shapes=[
                pltpu.VMEM((frames, width), F32),
                pltpu.VMEM((SLICES, width, columns), BF16),
                pltpu.SemaphoreType.DMA((PIECES,)),
            ],
        ),
        compiler_params=pltpu.CompilerParams(
            dimension_semantics=("arbitrary",), vmem_limit_bytes=VMEM_LIMIT
        ),
        cost_estimate=cost_of(2 * frames * width * columns * SLICES, moved),
    )(clock.spots, left, value, gain, upstream, *pieces)
    return clock(*outs)


def weight_kernel(count, spots, mine, paired, *refs):
    ups, (far, own) = refs[: 4 * count], refs[-2:]
    dims = (((0,), (0,)), ((), ()))
    offset = 0
    for index in range(count):
        near_own, pair_own, near_far, pair_far = ups[4 * index : 4 * index + 4]
        columns = near_own.shape[1]
        for out, first, second in ((far, near_far, pair_far), (own, near_own, pair_own)):
            result = lax.dot_general(mine[...], first[...], dims, preferred_element_type=F32)
            result += lax.dot_general(paired[...], second[...], dims, preferred_element_type=F32)
            out[:, offset : offset + columns] = result.astype(out.dtype)
        offset += columns


def in_parts(near, sent):
    parts = len(sent) // 2
    return [
        (near, parts * SLICES, part, (sent[part], 0), (sent[parts + part], 0))
        for part in range(parts)
    ]


def packed_pair(near, sent):
    return (near, SLICES, 0, (sent, 0), (sent, 1))


def weight_grads(left, ups, chunk, clock, first=0, depth=None, packed=None, place=0, base=None):
    rows = left[0] if isinstance(left, tuple) else left
    frames = ups[0][0].shape[0]
    depth = depth or rows.shape[1]
    skipped = first // chunk
    in_specs = []
    operands = []
    for core in range(2):
        if isinstance(left, tuple):
            operands.append(left[core])
            index = lambda step, spots: (0, step + skipped)
        else:
            operands.append(left)
            index = lambda step, spots, core=core: (spots[5 + core], step + skipped)
        in_specs.append(pl.BlockSpec((frames, chunk), index))
    widths = []
    for near, parts, part, *beside in ups:
        columns = near.shape[1] // parts
        for which, (item, block) in zip((0, 2), beside):
            operands += [near, item]
            stride = parts // SLICES
            mine = lambda step, spots, which=which, part=part, stride=stride: (
                0,
                spots[which] * stride + part,
            )
            theirs = lambda step, spots, block=block: (0, block)
            in_specs += [pl.BlockSpec((frames, columns), index) for index in (mine, theirs)]
        widths.append(columns)
    total = sum(widths)
    down = lambda step, spots: (step, place)
    count = len(operands)
    if base is not None:
        operands += base
        in_specs += [pl.BlockSpec(memory_space=pl.ANY)] * 2
    outs = pl.pallas_call(
        functools.partial(weight_kernel, len(ups)),
        input_output_aliases={} if base is None else {1 + count: 0, 2 + count: 1},
        out_shape=[jax.ShapeDtypeStruct((depth, packed or total), BF16)] * 2,
        grid_spec=pltpu.PrefetchScalarGridSpec(
            num_scalar_prefetch=1,
            grid=(depth // chunk,),
            in_specs=in_specs,
            out_specs=[pl.BlockSpec((chunk, total), down)] * 2,
        ),
        compiler_params=pltpu.CompilerParams(
            dimension_semantics=("arbitrary",), vmem_limit_bytes=VMEM_LIMIT
        ),
        cost_estimate=cost_of(
            8 * frames * depth * total, 4 * frames * depth + 8 * frames * total + 4 * depth * total
        ),
    )(clock.spots, *operands)
    return clock(*outs)


def attention_kernel(query, keys, values, across, along, mixed, summary):
    head = pl.program_id(0)
    scores = lax.dot_general(
        query[...], keys[...], (((1,), (1,)), ((), ())), preferred_element_type=F32
    )
    scores = jnp.where(across[...] == along[...], scores, MASKED)
    highest = jnp.max(scores, axis=-1, keepdims=True)
    raised = jnp.exp(scores - highest)
    totals = jnp.sum(raised, axis=-1, keepdims=True)
    probs = (raised * (1.0 / totals)).astype(BF16)
    mixed[...] = jnp.dot(probs, values[...], preferred_element_type=F32).astype(BF16)
    lane = lax.broadcasted_iota(jnp.int32, summary.shape, 1)
    kept = jnp.where(head == 0, jnp.zeros_like(summary), summary[...])
    summary[...] = jnp.where(lane == head, highest + jnp.log(totals), kept)


def attention(query, keys, values, across, along, clock):
    (query,) = clock(query)
    frames, width = query.shape
    head_block = pl.BlockSpec((frames, HEAD_DIM), lambda head: (0, head))
    fixed = lambda head: (0, 0)
    outs = pl.pallas_call(
        attention_kernel,
        out_shape=[
            jax.ShapeDtypeStruct((frames, width), BF16),
            jax.ShapeDtypeStruct((frames, HEAD_DIM), F32),
        ],
        grid=(width // HEAD_DIM,),
        in_specs=[head_block] * 3
        + [pl.BlockSpec((frames, 1), fixed), pl.BlockSpec((1, frames), fixed)],
        out_specs=[head_block, pl.BlockSpec((frames, HEAD_DIM), fixed)],
        compiler_params=pltpu.CompilerParams(
            dimension_semantics=("arbitrary",), vmem_limit_bytes=VMEM_LIMIT
        ),
        cost_estimate=cost_of(4 * frames * frames * width, 8 * frames * width),
    )(query, keys, values, across, along)
    return clock(*outs)


def attention_back_kernel(
    spots, query, keys, values, upstream, summary, across, along, cosine, sine, *outs
):
    head = pl.program_id(0)
    at = pl.ds(pl.multiple_of(head * HEAD_DIM, HEAD_DIM), HEAD_DIM)
    query_out, keys_out, values_out = outs[:3]
    contract_last = (((1,), (1,)), ((), ()))
    contract_first = (((0,), (0,)), ((), ()))
    scores = lax.dot_general(query[...], keys[...], contract_last, preferred_element_type=F32)
    scores = jnp.where(across[...] == along[...], scores, MASKED)
    lane = lax.broadcasted_iota(jnp.int32, summary.shape, 1)
    level = jnp.sum(jnp.where(lane == head, summary[...], 0.0), axis=-1, keepdims=True)
    probs = jnp.exp(scores - level)
    grads = lax.dot_general(upstream[...], values[...], contract_last, preferred_element_type=F32)
    balance = jnp.sum(probs * grads, axis=-1, keepdims=True)
    scores_grad = (probs * (grads - balance)).astype(BF16)
    values_out[:, at] = lax.dot_general(
        probs.astype(BF16), upstream[...], contract_first, preferred_element_type=F32
    ).astype(BF16)
    scale = HEAD_DIM ** (-0.5)
    query_back = jnp.dot(scores_grad, keys[...], preferred_element_type=F32)
    query_out[:, at] = (rotate(query_back, cosine[...], -sine[...]) * scale).astype(BF16)
    keys_back = lax.dot_general(scores_grad, query[...], contract_first, preferred_element_type=F32)
    keys_out[:, at] = rotate(keys_back, cosine[...], -sine[...]).astype(BF16)

    @pl.when(head == pl.num_programs(0) - 1)
    def _():
        for out, sent in zip(outs[:3], outs[3:]):
            send_slices(spots, out, sent)


def attention_back(query, keys, values, upstream, summary, across, along, cosine, sine, clock):
    frames, width = query.shape
    head_block = pl.BlockSpec((frames, HEAD_DIM), lambda head, spots: (0, head))
    fixed = lambda head, spots: (0, 0)
    whole = pl.BlockSpec((frames, HEAD_DIM), fixed)
    outs = pl.pallas_call(
        attention_back_kernel,
        out_shape=[jax.ShapeDtypeStruct((frames, width), BF16)] * 3
        + [jax.ShapeDtypeStruct((frames, width // 2), BF16)] * 3,
        grid_spec=pltpu.PrefetchScalarGridSpec(
            num_scalar_prefetch=1,
            grid=(width // HEAD_DIM,),
            in_specs=[head_block] * 4
            + [
                whole,
                pl.BlockSpec((frames, 1), fixed),
                pl.BlockSpec((1, frames), fixed),
                whole,
                whole,
            ],
            out_specs=[pl.BlockSpec((frames, width), fixed)] * 3
            + [pl.BlockSpec((frames, width // 2), fixed)] * 3,
        ),
        compiler_params=pltpu.CompilerParams(
            dimension_semantics=("arbitrary",), vmem_limit_bytes=VMEM_LIMIT
        ),
        cost_estimate=cost_of(10 * frames * frames * width, 14 * frames * width),
    )(clock.spots, query, keys, values, upstream, summary, across, along, cosine, sine)
    outs = clock(*outs)
    return outs[:3], outs[3:]


def bare_call(kernel, outs, operands, clock, flops=0):
    fixed = lambda spots: (0, 0)
    results = pl.pallas_call(
        kernel,
        out_shape=[jax.ShapeDtypeStruct(shape, kind) for shape, kind in outs],
        grid_spec=pltpu.PrefetchScalarGridSpec(
            num_scalar_prefetch=1,
            grid=(),
            in_specs=[
                pl.BlockSpec(item.shape, lambda spots, item=item: (0,) * item.ndim)
                for item in operands
            ],
            out_specs=[pl.BlockSpec(shape, fixed) for shape, _ in outs],
        ),
        compiler_params=pltpu.CompilerParams(vmem_limit_bytes=VMEM_LIMIT),
        cost_estimate=cost_of(flops, sum(size_of(item) for item in operands)),
    )(clock.spots, *operands)
    return clock(*results)


def final_kernel(spots, value, gain, valid, cotangent, out, grad_out, gain_out, low_out, sent):
    normed, scaled, inverse = normalize(value[...], gain[...])
    out[...] = (normed * valid[...]).astype(BF16)
    upstream = cotangent[...].astype(F32) * valid[...]
    grad, gain_grad = normalize_back(upstream, scaled, inverse, gain[...])
    grad_out[...] = grad
    gain_out[...] = gain_grad
    low_out[...] = (0.5 * grad).astype(BF16)
    send_slices(spots, low_out, sent)


def final(value, gain, valid, cotangent, clock):
    shape = value.shape
    return bare_call(
        final_kernel,
        [
            (shape, BF16),
            (shape, F32),
            (gain.shape, F32),
            (shape, BF16),
            ((shape[0], shape[1] // 2), BF16),
        ],
        [value, gain, valid, cotangent],
        clock,
    )


TAPS = 5
REACH = 2
CONV_BLOCK = 256


def convolve_kernel(spots, values, gates, taps, same, valid, mixed, shares):
    glued = values[...] * sigmoid(gates[...])
    frames = glued.shape[0]
    result = jnp.zeros_like(glued)
    for index in range(TAPS):
        moved = pltpu.roll(glued, (REACH - index) % frames, 0) if index != REACH else glued
        result += taps[index : index + 1, :] * moved * same[:, index : index + 1]
    mixed[...] = result
    counted = jnp.maximum(jnp.sum(valid[...]), 1.0)
    local_sum = jnp.sum(result * valid[...], axis=0, keepdims=True)
    spread = (result - local_sum / counted) * valid[...]
    shares[0:1, :] = local_sum
    shares[1:2, :] = jnp.sum(spread * spread, axis=0, keepdims=True)


def convolve(expand, taps, same, valid, clock):
    frames, width = expand.shape[0], expand.shape[1] // 2
    blocks = width // CONV_BLOCK
    along = lambda step, spots: (0, step)
    fixed = lambda step, spots: (0, 0)
    outs = pl.pallas_call(
        convolve_kernel,
        out_shape=[
            jax.ShapeDtypeStruct((frames, width), F32),
            jax.ShapeDtypeStruct((2, width), F32),
        ],
        grid_spec=pltpu.PrefetchScalarGridSpec(
            num_scalar_prefetch=1,
            grid=(blocks,),
            in_specs=[
                pl.BlockSpec((frames, CONV_BLOCK), along),
                pl.BlockSpec((frames, CONV_BLOCK), lambda step, spots: (0, step + blocks)),
                pl.BlockSpec((TAPS, CONV_BLOCK), along),
                pl.BlockSpec(same.shape, fixed),
                pl.BlockSpec(valid.shape, fixed),
            ],
            out_specs=[
                pl.BlockSpec((frames, CONV_BLOCK), along),
                pl.BlockSpec((2, CONV_BLOCK), along),
            ],
        ),
        compiler_params=pltpu.CompilerParams(
            dimension_semantics=("arbitrary",), vmem_limit_bytes=VMEM_LIMIT
        ),
        cost_estimate=cost_of(0, size_of(expand)),
    )(clock.spots, expand, expand, taps, same, valid)
    return clock(*outs)


def batch_prologue(wholes, full_outs):
    mixed, mean, inverse, gain, shift = (item[...] for item in wholes)
    normal = (mixed - mean) * inverse * gain + shift
    acted = (normal * sigmoid(normal)).astype(BF16)
    full_outs[0][...] = acted
    return acted


def projected(mixed, mean, inverse, gain, shift, value, pieces, first, columns, clock):
    return forward_product(
        clock,
        pieces,
        first,
        columns,
        [mixed, mean, inverse, gain, shift],
        [(value, columns)],
        [(mixed.shape, BF16)],
        [(F32, columns)],
        batch_prologue,
        functools.partial(add_epilogue, 1.0),
    )


def project_epilogue(spots, result, wholes, blocks, full_outs, block_outs):
    mixed, mean, inverse, gain, shift, valid = (item[...] for item in wholes)
    standard = (mixed - mean) * inverse
    grad = result * swish_slope(standard * gain + shift)
    full_outs[0][...] = grad
    counted = grad * valid
    full_outs[1][0:1, :] = jnp.sum(counted, axis=0, keepdims=True)
    full_outs[1][1:2, :] = jnp.sum(counted * standard, axis=0, keepdims=True)


def project_back(outer, mixed, mean, inverse, gain, shift, valid, pieces, first, clock):
    frames, width = mixed.shape
    return backward_product(
        clock,
        pieces,
        first,
        [outer],
        [mixed, mean, inverse, gain, shift, valid],
        [],
        width,
        [((frames, width), F32), ((2, width), F32)],
        [],
        project_epilogue,
    )


def convolve_back_kernel(
    spots, grad, mixed, values, gates, taps, same, valid, sums, mean, inverse, gain, count, out, taps_out, *sent
):
    step = pl.program_id(0)
    frames, columns = grad.shape
    width = out.shape[1] // 2
    standard = (mixed[...] - mean[...]) * inverse[...]
    share = (sums[0:1, :] + standard * sums[1:2, :]) / count[...]
    upstream = gain[...] * inverse[...] * (grad[...] - valid[...] * share)
    gate = sigmoid(gates[...])
    glued = values[...] * gate
    back = jnp.zeros_like(upstream)
    for index in range(TAPS):
        term = upstream * same[:, index : index + 1]
        if index == REACH:
            moved, returned = glued, term
        else:
            moved = pltpu.roll(glued, (REACH - index) % frames, 0)
            returned = pltpu.roll(term, (index - REACH) % frames, 0)
        taps_out[index : index + 1, :] = jnp.sum(term * moved, axis=0, keepdims=True)
        back += taps[index : index + 1, :] * returned
    low = pl.multiple_of(step * columns, 128)
    high = pl.multiple_of(width + step * columns, 128)
    out[:, pl.ds(low, columns)] = (back * gate).astype(BF16)
    out[:, pl.ds(high, columns)] = (back * glued * (1.0 - gate)).astype(BF16)

    @pl.when(step == pl.num_programs(0) - 1)
    def _():
        for part, place in zip(sent, (1, 3)):
            start = pl.multiple_of(spots[place] * part.shape[1], 128)
            part[...] = out[:, pl.ds(start, part.shape[1])]


def convolve_back(grad, mixed, expand, taps, same, valid, sums, mean, inverse, gain, count, clock):
    frames, width = mixed.shape
    blocks = width // CONV_BLOCK
    along = lambda step, spots: (0, step)
    fixed = lambda step, spots: (0, 0)
    wide = pl.BlockSpec((frames, CONV_BLOCK), along)
    row = pl.BlockSpec((1, CONV_BLOCK), along)
    outs = pl.pallas_call(
        convolve_back_kernel,
        out_shape=[
            jax.ShapeDtypeStruct((frames, 2 * width), BF16),
            jax.ShapeDtypeStruct((TAPS, width), F32),
        ]
        + [jax.ShapeDtypeStruct((frames, width // 2), BF16)] * 2,
        grid_spec=pltpu.PrefetchScalarGridSpec(
            num_scalar_prefetch=1,
            grid=(blocks,),
            in_specs=[
                wide,
                wide,
                wide,
                pl.BlockSpec((frames, CONV_BLOCK), lambda step, spots: (0, step + blocks)),
                pl.BlockSpec((TAPS, CONV_BLOCK), along),
                pl.BlockSpec(same.shape, fixed),
                pl.BlockSpec(valid.shape, fixed),
                pl.BlockSpec((2, CONV_BLOCK), along),
                row,
                row,
                row,
                pl.BlockSpec((1, 1), fixed),
            ],
            out_specs=[
                pl.BlockSpec((frames, 2 * width), fixed),
                pl.BlockSpec((TAPS, CONV_BLOCK), along),
            ]
            + [pl.BlockSpec((frames, width // 2), fixed)] * 2,
        ),
        compiler_params=pltpu.CompilerParams(
            dimension_semantics=("arbitrary",), vmem_limit_bytes=VMEM_LIMIT
        ),
        cost_estimate=cost_of(0, size_of(expand) * 2),
    )(clock.spots, grad, mixed, expand, expand, taps, same, valid, sums, mean, inverse, gain, count)
    return clock(*outs)


def split_kernel(spots, kept_value, kept_moving, sent_value, sent_moving, kept, sent):
    kept[...] = kept_value[...].astype(F32) + kept_moving[...].astype(F32)
    sent[...] = (sent_value[...].astype(F32) + sent_moving[...].astype(F32)).astype(BF16)


def split_sum(value, moving, which, clock):
    rows, columns = value.shape
    half = rows // 2
    steps = 2 if half * columns >= 2**18 else 1
    block = (half // steps, columns)
    kept = pl.BlockSpec(block, lambda step, spots: (spots[BITS + which] * steps + step, 0))
    sent = pl.BlockSpec(block, lambda step, spots: ((1 - spots[BITS + which]) * steps + step, 0))
    along = pl.BlockSpec(block, lambda step, spots: (step, 0))
    outs = pl.pallas_call(
        split_kernel,
        out_shape=[
            jax.ShapeDtypeStruct((half, columns), F32),
            jax.ShapeDtypeStruct((half, columns), BF16),
        ],
        grid_spec=pltpu.PrefetchScalarGridSpec(
            num_scalar_prefetch=1,
            grid=(steps,),
            in_specs=[kept, kept, sent, sent],
            out_specs=[along, along],
        ),
        compiler_params=pltpu.CompilerParams(
            dimension_semantics=("arbitrary",), vmem_limit_bytes=VMEM_LIMIT
        ),
        cost_estimate=cost_of(0, size_of(value)),
    )(clock.spots, value, moving, value, moving)
    return clock(*outs)


def sum_kernel(spots, value, moving, out):
    out[...] = (value[...].astype(F32) + moving[...].astype(F32)).astype(BF16)


def blocks_kernel(spots, blocks, out):
    total = blocks[0].astype(F32)
    for index in range(1, blocks.shape[0]):
        total += blocks[index].astype(F32)
    out[...] = total.astype(BF16)


def unfold_kernel(widths, size, spots, value, *outs):
    step = pl.program_id(0)
    block = value.shape[0] // size
    for item in range(size // 2):
        place = 2 * item + step
        rows = value[pl.ds(pl.multiple_of(place * block, 16), block), :].astype(F32)
        offset = 0
        for out, width in zip(outs, widths):
            out[item * block : (item + 1) * block, :] = rows[:, offset : offset + width]
            offset += width


def unfold(value, size, widths, clock):
    rows, columns = value.shape
    outs = pl.pallas_call(
        functools.partial(unfold_kernel, widths, size),
        out_shape=[jax.ShapeDtypeStruct((rows, width), F32) for width in widths],
        grid_spec=pltpu.PrefetchScalarGridSpec(
            num_scalar_prefetch=1,
            grid=(2,),
            in_specs=[pl.BlockSpec((rows, columns), lambda step, spots: (0, 0))],
            out_specs=[
                pl.BlockSpec((rows // 2, width), lambda step, spots: (step, 0))
                for width in widths
            ],
        ),
        compiler_params=pltpu.CompilerParams(
            dimension_semantics=("arbitrary",), vmem_limit_bytes=VMEM_LIMIT
        ),
        cost_estimate=cost_of(0, size_of(value)),
    )(clock.spots, value)
    return clock(*outs)


class Clock:
    def __init__(self, spots):
        self.spots = spots

    def __call__(self, *values):
        self.spots, *values = lax.optimization_barrier((self.spots,) + values)
        return values

    def send(self, value, axis, mask):
        (value,) = self(value)
        return swapped(value, axis, mask)


class Gather:
    def __init__(self, slices, clock):
        self.own = slices[0] if len(slices) == 1 else jnp.concatenate(slices, axis=1)
        self.half = self.own.shape[0] // 2
        self.clock = clock
        self.crossing = lax.dynamic_slice_in_dim(
            self.own, half_sent() * self.half, self.half, axis=0
        )

    def cross(self):
        self.across = self.clock.send(self.crossing, "fsdp", 2)

    def beside(self):
        self.own_beside = joined(self.own)

    def forward(self):
        quarter = self.half // 2
        self.across, self.own_beside = self.clock(self.across, self.own_beside)
        self.first = swapped(self.across[:quarter], "dp", 1)
        self.second = swapped(self.across[quarter:], "dp", 2)
        self.across_beside = swapped(self.across, "fsdp", 1)

    def turn(self):
        self.first, self.second, self.across_beside = self.clock(
            self.first, self.second, self.across_beside
        )
        self.first_beside = swapped(self.first, "fsdp", 1)
        self.second_beside = swapped(self.second, "fsdp", 1)

    def finish(self):
        self.first_beside, self.second_beside = self.clock(
            self.first_beside, self.second_beside
        )
        self.pieces = (
            self.own,
            self.own_beside,
            self.across,
            self.first,
            self.second,
            self.across_beside,
            self.first_beside,
            self.second_beside,
        )


def half_sent():
    place = lax.axis_index("dp")
    return (place ^ (place >> 1)) & 1


class Reduction:
    def __init__(self, far, own, clock, wide=False):
        self.size = lax.axis_size("dp")
        self.clock = clock
        self.value = own
        self.sent = far
        self.stage = 0
        self.wide = wide
        self.moving = None
        self.whole = None

    def exchange(self, blocks):
        groups = [[i for i in range(self.size) if i % 2 == low] for low in range(2)]
        return lax.all_to_all(blocks, "dp", 0, 0, axis_index_groups=groups, tiled=True)

    def fold(self, moving):
        members = self.size // 2
        self.stage += 1
        if self.stage == 1:
            self.value, self.sent = split_sum(self.value, moving, 0, self.clock)
        elif self.stage == 2:
            rows, columns = moving.shape
            (total,) = bare_call(
                sum_kernel, [(moving.shape, BF16)], [self.value, moving], self.clock
            )
            self.sent = total.reshape(members, rows // members, columns)
        elif self.stage == 3:
            (self.sent,) = bare_call(
                blocks_kernel, [(moving.shape[1:], BF16)], [moving], self.clock
            )
        else:
            self.sent = moving.reshape(-1, moving.shape[2])

    def send(self, sent):
        if self.stage == 0:
            self.moving = swapped(sent, "fsdp", 2)
        elif self.stage == 1:
            self.moving = swapped(sent, "dp", 1)
        elif self.stage == 2:
            self.moving = self.exchange(sent)
        elif self.stage == 3 and self.wide:
            copies = (self.size // 2,) + sent.shape
            self.moving = self.exchange(jnp.broadcast_to(sent[None], copies))
        elif self.stage == 3:
            self.whole = lax.all_gather(sent, "dp", axis=0, tiled=True)
            self.moving = None
        else:
            self.value = sent
            self.moving = swapped(sent, "dp", 1)

    def ended(self):
        return self.whole is not None or self.stage == 4

    def result(self, widths=None):
        while not self.ended():
            turn(self.clock, self)
        if self.wide:
            (moving,) = self.clock(self.moving)
            return [
                jnp.where(
                    lax.axis_index("dp") & 1 == 0,
                    jnp.concatenate([self.value, moving], axis=0),
                    jnp.concatenate([moving, self.value], axis=0),
                ).astype(F32)
            ]
        (whole,) = self.clock(self.whole)
        return unfold(whole, self.size, widths or (whole.shape[1],), self.clock)


def turn(clock, *groups):
    groups = [group for group in groups if not group.ended()]
    waiting = [group for group in groups if group.moving is not None]
    fresh = [group for group in groups if group.moving is None]
    arrived = clock(*[group.moving for group in waiting], *[group.sent for group in fresh])
    for group, item in zip(fresh, arrived[len(waiting) :]):
        group.send(item)
    for group, moving in zip(waiting, arrived):
        group.fold(moving)
    sent = clock(*[group.sent for group in waiting])
    for group, item in zip(waiting, sent):
        group.send(item)


def joined(value):
    groups = [[i, i + 1] for i in range(0, lax.axis_size("fsdp"), 2)]
    return lax.all_gather(value, "fsdp", axis=0, tiled=True, axis_index_groups=groups)


class Doubling:
    def __init__(self, value):
        self.sent = value
        self.moving = None
        self.left = [
            (axis, 1 << bit)
            for axis in ("fsdp", "dp")
            for bit in range(lax.axis_size(axis).bit_length() - 1)
        ]

    def fold(self, moving):
        self.sent = self.sent + moving

    def send(self, sent):
        self.sent = sent
        if self.left:
            axis, mask = self.left.pop(0)
            self.moving = swapped(sent, axis, mask)
        else:
            self.moving = None
            self.left = None

    def ended(self):
        return self.left is None

    def result(self, clock):
        while not self.ended():
            turn(clock, self)
        return self.sent


def swapped(value, axis, mask):
    size = lax.axis_size(axis)
    return lax.ppermute(value, axis, [(i, i ^ mask) for i in range(size)])


def spread_sum(rows):
    axes = ("dp", "fsdp")
    count = lax.axis_size(axes)
    copies = jnp.broadcast_to(rows[None], (count,) + rows.shape)
    return lax.all_to_all(copies, axes, 0, 0, tiled=True)


def neighbours(segment, taps):
    frames = segment.shape[0]
    reach = (taps - 1) // 2
    side = jnp.pad(segment, (reach, reach), constant_values=-1)
    columns = [side[index : index + frames] == segment for index in range(taps)]
    return jnp.pad(jnp.stack(columns, axis=1).astype(F32), ((0, 0), (0, 8 - taps)))


def body(
    frames_in,
    cotangent,
    lengths,
    first_gain,
    first_up,
    first_down,
    attend_gain,
    query_proj,
    key_proj,
    value_proj,
    output_proj,
    conv_gain,
    conv_expand,
    conv_kernel,
    batch_gain,
    batch_shift,
    conv_project,
    second_gain,
    second_up,
    second_down,
    final_gain,
):
    frames, width = frames_in.shape
    slot = lax.axis_index("fsdp")
    part = half_sent()
    row, rows = lax.axis_index("dp"), lax.axis_size("dp")
    bits = [(row >> which) & 1 for which in range(rows.bit_length() - 1)]
    spots = jnp.stack(
        [slot, slot ^ 1, slot ^ 2, slot ^ 3, part, slot & 1, 1 - (slot & 1)] + bits
    ).astype(jnp.int32)
    clock = Clock(spots)
    segment, position, valid = layout(lengths[0], frames)
    cosine, sine = rotation(position, HEAD_DIM // 2)
    column = valid[:, None]
    seg_across, seg_along = segment[:, None], segment[None, :]
    first_gain, attend_gain, conv_gain, second_gain, final_gain, batch_gain, batch_shift = (
        item[None]
        for item in (
            first_gain,
            attend_gain,
            conv_gain,
            second_gain,
            final_gain,
            batch_gain,
            batch_shift,
        )
    )
    same = neighbours(segment, conv_kernel.shape[0])
    narrow = query_proj.shape[1]
    wide = conv_expand.shape[1]

    def pair(value):
        return clock.send(value, "fsdp", 1)

    first_ups = Gather((first_up,), clock)
    first_ups.cross()
    first_ups.beside()
    first_downs = Gather((first_down,), clock)
    attends = Gather((query_proj, key_proj, value_proj), clock)
    convs = Gather((output_proj, conv_expand, conv_project), clock)
    second_ups = Gather((second_up,), clock)
    second_downs = Gather((second_down,), clock)
    later = (first_downs, attends, convs, second_ups, second_downs)
    for group, item in zip(later, clock(*[group.crossing for group in later])):
        group.crossing = item
        group.beside()
    first_ups.forward()
    first_downs.cross()
    attends.cross()
    first_ups.turn()
    first_ups.finish()
    first_normed, first_inner, first_acted = up(frames_in, first_gain, first_ups.pieces, clock)
    first_downs.forward()
    convs.cross()
    first_downs.turn()
    first_downs.finish()
    attends.forward()
    second_ups.cross()
    after_first = added(
        first_acted, frames_in, 0.5, first_downs.pieces, 0, first_down.shape[1], clock
    )
    attends.turn()
    attends.finish()
    attend_normed, query, keys, values = attend_front(
        after_first, attend_gain, cosine, sine, attends.pieces, narrow, clock
    )
    convs.forward()
    attended, summary = attention(query, keys, values, seg_across, seg_along, clock)
    convs.turn()
    convs.finish()
    after_attend = added(attended, after_first, 1.0, convs.pieces, 0, narrow, clock)
    conv_normed, expand = expanded(after_attend, conv_gain, convs.pieces, narrow, wide, clock)

    mixed, local = convolve(expand, conv_kernel, same, column, clock)
    local = jnp.concatenate([local, jnp.broadcast_to(jnp.sum(valid), (2, 128))], axis=1)
    shares = spread_sum(local)
    second_downs.cross()
    second_ups.forward()
    (shares,) = clock(shares)
    second_ups.turn()
    counts = shares[:, 0, width : width + 1]
    count = jnp.sum(counts)
    sums = shares[:, 0, :width]
    mean = jnp.sum(sums, axis=0) / count
    offsets = sums / jnp.maximum(counts, 1.0) - mean
    variance = jnp.sum(shares[:, 1, :width] + counts * offsets * offsets, axis=0) / count
    deviation_inverse = lax.rsqrt(variance + EPSILON)
    mean_row, inverse_row = mean[None], deviation_inverse[None]
    conv_acted, after_conv = projected(
        mixed,
        mean_row,
        inverse_row,
        batch_gain,
        batch_shift,
        after_attend,
        convs.pieces,
        narrow + wide,
        narrow,
        clock,
    )
    second_ups.finish()
    second_downs.forward()
    second_normed, second_inner, second_acted = up(
        after_conv, second_gain, second_ups.pieces, clock
    )
    second_downs.turn()
    second_downs.finish()
    pair_acted, pair_normed = pair(second_acted), pair(second_normed)
    after_second = added(
        second_acted, after_conv, 0.5, second_downs.pieces, 0, second_down.shape[1], clock
    )
    pair_acted, pair_normed = clock(pair_acted, pair_normed)
    layer_out, upstream, final_gain_grad, outer, sent = final(
        after_second, final_gain, column, cotangent, clock
    )
    (pair_outer,) = clock(pair(sent))
    both_conv_acted, both_conv, both_attended, both_attend, both_first_acted, both_first = (
        joined(item)
        for item in clock(
            conv_acted, conv_normed, attended, attend_normed, first_acted, first_normed
        )
    )

    second_down_sum = Reduction(
        *weight_grads((second_acted, pair_acted), [packed_pair(outer, pair_outer)], 1024, clock),
        clock,
    )
    turn(clock, second_down_sum)
    inner_grad, sent = down_back(outer, second_inner, second_downs.pieces, 2, clock)
    pair_inner = [pair(item) for item in sent]
    upstream, second_gain_grad, outer, sent = up_back(
        inner_grad, after_conv, second_gain, upstream, second_ups.pieces, 1.0, clock
    )
    pair_inner = clock(*pair_inner)
    pair_outer = pair(sent)
    normal_grad, local = project_back(
        outer,
        mixed,
        mean_row,
        inverse_row,
        batch_gain,
        batch_shift,
        column,
        convs.pieces,
        narrow + wide,
        clock,
    )
    (local,) = clock(local)
    pieces = spread_sum(local)
    second_up_sum = Reduction(
        *weight_grads((second_normed, pair_normed), in_parts(inner_grad, pair_inner), 512, clock),
        clock,
    )
    pair_outer, both_conv_acted = clock(pair_outer, both_conv_acted)
    conv_part = weight_grads(
        both_conv_acted,
        [packed_pair(outer, pair_outer)],
        512,
        clock,
        packed=wide + narrow,
        place=wide // narrow,
    )
    (pieces,) = clock(pieces)
    turn(clock, second_up_sum, second_down_sum)
    sums = jnp.sum(pieces, axis=0)
    expand_back, kernel_local, *sent = convolve_back(
        normal_grad,
        mixed,
        expand,
        conv_kernel,
        same,
        column,
        sums,
        mean_row,
        inverse_row,
        batch_gain,
        count.reshape(1, 1),
        clock,
    )
    pair_back = [pair(item) for item in sent]
    upstream, conv_gain_grad, outer, sent = norm_back_product(
        [expand_back], after_attend, conv_gain, upstream, convs.pieces, narrow, 1.0, clock
    )
    *pair_back, both_conv = clock(*pair_back, both_conv)
    pair_outer = pair(sent)
    conv_part = weight_grads(
        both_conv,
        [(expand_back, SLICES, 0, *((item, 0) for item in pair_back))],
        512,
        clock,
        packed=wide + narrow,
        base=conv_part,
    )
    conv_sum = Reduction(*conv_part, clock)
    mixed_back = plain_back(outer, BF16, convs.pieces, 0, clock)
    pair_outer, both_attended = clock(pair_outer, both_attended)
    turn(clock, conv_sum, second_up_sum, second_down_sum)
    backs, sent = attention_back(
        query, keys, values, mixed_back, summary, seg_across, seg_along, cosine, sine, clock
    )
    pair_backs = [pair(item) for item in sent]
    attend_part = weight_grads(
        both_attended, [packed_pair(outer, pair_outer)], 512, clock, packed=4 * narrow, place=3
    )
    *pair_backs, both_attend = clock(*pair_backs, both_attend)
    attend_part = weight_grads(
        both_attend,
        [packed_pair(item, other) for item, other in zip(backs, pair_backs)],
        512,
        clock,
        packed=4 * narrow,
        base=attend_part,
    )
    attend_sum = Reduction(*attend_part, clock)
    turn(clock, attend_sum, conv_sum, second_up_sum, second_down_sum)
    upstream, attend_gain_grad, outer, sent = norm_back_product(
        backs, after_first, attend_gain, upstream, attends.pieces, 0, 0.5, clock
    )
    (pair_outer,) = clock(pair(sent))
    (both_first_acted,) = clock(both_first_acted)
    first_down_sum = Reduction(
        *weight_grads(both_first_acted, [packed_pair(outer, pair_outer)], 1024, clock), clock
    )
    inner_grad, sent = down_back(outer, first_inner, first_downs.pieces, 1, clock)
    turn(clock, first_down_sum, attend_sum, conv_sum, second_up_sum)
    *pair_inner, both_first = clock(*[pair(item) for item in sent], both_first)
    first_up_sum = Reduction(
        *weight_grads(both_first, in_parts(inner_grad, pair_inner), 512, clock), clock, wide=True
    )
    turn(clock, first_up_sum)
    upstream, first_gain_grad, _, _ = up_back(
        inner_grad, frames_in, first_gain, upstream, first_ups.pieces, 1.0, clock
    )
    minor = jnp.concatenate(
        [
            first_gain_grad,
            attend_gain_grad,
            conv_gain_grad,
            second_gain_grad,
            final_gain_grad,
            kernel_local,
        ]
    )
    minors = Doubling(minor)
    turn(clock, minors, first_down_sum, attend_sum, conv_sum)
    (second_down_grad,) = second_down_sum.result()
    turn(clock, minors, first_down_sum, attend_sum)
    turn(clock, first_up_sum)
    (second_up_grad,) = second_up_sum.result()
    turn(clock, minors, first_down_sum)
    turn(clock, minors, first_up_sum)
    expand_grad, project_grad = conv_sum.result((wide, narrow))
    turn(clock, minors, first_up_sum)
    query_grad, key_grad, value_grad, output_grad = attend_sum.result((narrow,) * 4)
    turn(clock, first_up_sum)
    minor_sums = minors.result(clock)
    (first_down_grad,) = first_down_sum.result()
    (first_up_grad,) = first_up_sum.result()
    shift_grad, scale_grad = sums
    taps = conv_kernel.shape[0]
    return (
        layer_out,
        upstream,
        first_up_grad,
        first_down_grad,
        query_grad,
        key_grad,
        value_grad,
        output_grad,
        expand_grad,
        project_grad,
        second_up_grad,
        second_down_grad,
        minor_sums[0],
        minor_sums[1],
        minor_sums[2],
        minor_sums[3],
        minor_sums[4],
        minor_sums[5 : 5 + taps],
        scale_grad,
        shift_grad,
        mean,
        variance,
    )


def solution(mesh):
    placed = (
        P(("dp", "fsdp"), None),
        P(("dp", "fsdp"), None),
        P(("dp", "fsdp"), None),
        P(),
        P(None, "fsdp"),
        P(None, "fsdp"),
        P(),
        P(None, "fsdp"),
        P(None, "fsdp"),
        P(None, "fsdp"),
        P(None, "fsdp"),
        P(),
        P(None, "fsdp"),
        P(),
        P(),
        P(),
        P(None, "fsdp"),
        P(),
        P(None, "fsdp"),
        P(None, "fsdp"),
        P(),
    )
    return jax.shard_map(
        body,
        mesh=mesh,
        in_specs=placed,
        out_specs=(
            P(("dp", "fsdp"), None),
            P(("dp", "fsdp"), None),
            P(None, "fsdp"),
            P(None, "fsdp"),
            P(None, "fsdp"),
            P(None, "fsdp"),
            P(None, "fsdp"),
            P(None, "fsdp"),
            P(None, "fsdp"),
            P(None, "fsdp"),
            P(None, "fsdp"),
            P(None, "fsdp"),
            P(),
            P(),
            P(),
            P(),
            P(),
            P(),
            P(),
            P(),
            P(),
            P(),
        ),
        check_vma=False,
    )
```

```python
import functools

import jax
import jax.numpy as jnp
from jax import lax
from jax.experimental import pallas as pl
from jax.experimental.pallas import tpu as pltpu
from jax.sharding import PartitionSpec as P

HEADS = 8
HEAD_DIM = 128


EPSILON = 1e-05
MASKED = -1e30
SLICES = 4
VMEM_LIMIT = 60 * 1024 * 1024
VMEM_MOST = 63 * 1024 * 1024 + 512 * 1024
COST_SCALE = 0.01
BITS = 7

F32 = jnp.float32
BF16 = jnp.bfloat16


def cost_of(flops, moved):
    return pl.CostEstimate(
        flops=int(flops * COST_SCALE),
        transcendentals=0,
        bytes_accessed=int(moved * COST_SCALE),
    )


def size_of(item):
    return item.size * item.dtype.itemsize


def normalize(value, gain):
    centre = jnp.mean(value, axis=-1, keepdims=True)
    centred = value - centre
    inverse = lax.rsqrt(jnp.mean(centred * centred, axis=-1, keepdims=True) + EPSILON)
    scaled = centred * inverse
    return (scaled * gain, scaled, inverse)


def normalize_back(upstream, scaled, inverse, gain):
    inner = upstream * gain
    first_mean = jnp.mean(inner, axis=-1, keepdims=True)
    second_mean = jnp.mean(inner * scaled, axis=-1, keepdims=True)
    return (
        inverse * (inner - first_mean - scaled * second_mean),
        jnp.sum(upstream * scaled, axis=0, keepdims=True),
    )


def sigmoid(value):
    return 0.5 * jnp.tanh(0.5 * value) + 0.5


def swish_slope(value):
    gate = sigmoid(value)
    return gate * (1.0 + value * (1.0 - gate))


def layout(row, frames):
    ends = jnp.cumsum(row, dtype=jnp.int32)
    times = jnp.arange(frames, dtype=jnp.int32)
    reached = times[:, None] >= ends[None, :]
    segment = jnp.sum(reached.astype(jnp.int32), axis=1, dtype=jnp.int32)
    start = jnp.max(jnp.where(reached, ends[None, :], 0), axis=1)
    position = (times - start).astype(jnp.float32)
    valid = (times < ends[-1]).astype(jnp.float32)
    return (segment, position, valid)


def rotation(position, half):
    rates = 10000.0 ** (-jnp.arange(half, dtype=jnp.float32) / half)
    angle = position[:, None] * rates[None, :]
    cosine, sine = jnp.cos(angle), jnp.sin(angle)
    return (
        jnp.concatenate([cosine, cosine], axis=1),
        jnp.concatenate([-sine, sine], axis=1),
    )


def rotate(value, cosine, sine):
    heads = []
    for start in range(0, value.shape[1], HEAD_DIM):
        head = value[:, start : start + HEAD_DIM]
        heads.append(head * cosine + pltpu.roll(head, HEAD_DIM // 2, 1) * sine)
    return heads[0] if len(heads) == 1 else jnp.concatenate(heads, axis=1)


def loads(spots, pieces, first, width, target, sems):
    half = pieces[2].shape[0]
    quarter = half // 2
    low = pl.multiple_of(spots[4] * half, 16)
    high = pl.multiple_of((1 - spots[4]) * half, 16)
    rows = pieces[0].shape[0]
    beside = pl.multiple_of(spots[6] * rows, 16)
    places = (
        (0, 0, rows),
        (1, 0, rows),
        (2, low, half),
        (2, high, quarter),
        (2, high + quarter, quarter),
        (3, low, half),
        (3, high, quarter),
        (3, high + quarter, quarter),
    )
    return [
        pltpu.make_async_copy(
            piece.at[pl.ds(beside if index == 1 else 0, extent), pl.ds(first, width)],
            target(place, start, extent),
            sems.at[index],
        )
        for index, (piece, (place, start, extent)) in enumerate(zip(pieces, places))
    ]


PIECES = 8
WAITS = ((0,), (1,), (2, 3, 4), (5, 6, 7))


def forward_kernel(first, width, counts, prologue, epilogue, spots, *refs):
    whole_count, block_count, full_out_count, block_out_count = counts
    refs = list(refs)

    def take(number):
        taken = refs[:number]
        del refs[:number]
        return taken

    wholes = take(whole_count)
    blocks = take(block_count)
    pieces = take(PIECES)
    full_outs = take(full_out_count)
    block_outs = take(block_out_count)
    left, weights, sems = refs
    step = pl.program_id(0)
    copies = loads(
        spots,
        pieces,
        first,
        width,
        lambda place, start, extent: weights.at[place, pl.ds(start, extent), :],
        sems,
    )

    @pl.when(step == 0)
    def _():
        for copy in copies:
            copy.start()
        left[...] = prologue(wholes, full_outs)

    for place, group in enumerate(WAITS):

        @pl.when(step == place)
        def _():
            for index in group:
                copies[index].wait()

    result = jnp.dot(left[...], weights[step], preferred_element_type=F32)
    epilogue(result, wholes, blocks, block_outs)


def forward_product(clock, pieces, first, width, wholes, blocks, full_outs, block_outs, prologue, epilogue):
    depth = pieces[0].shape[0]
    frames = wholes[0].shape[0]
    turned = lambda step, spots: (0, spots[step])
    fixed = lambda step, spots: (0, 0)
    in_specs = [pl.BlockSpec(item.shape, fixed, pipeline_mode=pl.Buffered(1)) for item in wholes]
    in_specs += [pl.BlockSpec((frames, columns), turned) for _, columns in blocks]
    in_specs += [pl.BlockSpec(memory_space=pl.ANY)] * PIECES
    out_shape = [jax.ShapeDtypeStruct(shape, kind) for shape, kind in full_outs]
    out_shape += [
        jax.ShapeDtypeStruct((frames, SLICES * columns), kind) for kind, columns in block_outs
    ]
    out_specs = [pl.BlockSpec(shape, fixed) for shape, _ in full_outs]
    out_specs += [pl.BlockSpec((frames, columns), turned) for _, columns in block_outs]
    moved = sum(size_of(item) for item in wholes) + sum(size_of(item) for item, _ in blocks)
    moved += sum(size_of(item) for item in out_shape) + depth * width * SLICES * 2
    outs = pl.pallas_call(
        functools.partial(
            forward_kernel,
            first,
            width,
            (len(wholes), len(blocks), len(full_outs), len(block_outs)),
            prologue,
            epilogue,
        ),
        out_shape=out_shape,
        grid_spec=pltpu.PrefetchScalarGridSpec(
            num_scalar_prefetch=1,
            grid=(SLICES,),
            in_specs=in_specs,
            out_specs=out_specs,
            scratch_shapes=[
                pltpu.VMEM((frames, depth), BF16),
                pltpu.VMEM((SLICES, depth, width), BF16),
                pltpu.SemaphoreType.DMA((PIECES,)),
            ],
        ),
        compiler_params=pltpu.CompilerParams(
            dimension_semantics=("arbitrary",), vmem_limit_bytes=VMEM_LIMIT
        ),
        cost_estimate=cost_of(2 * frames * depth * width * SLICES, moved),
    )(clock.spots, *wholes, *[item for item, _ in blocks], *pieces)
    return clock(*outs)


def normed_prologue(wholes, full_outs):
    value, gain = wholes[:2]
    normed = normalize(value[...].astype(F32), gain[...])[0].astype(BF16)
    full_outs[0][...] = normed
    return normed


def plain_prologue(wholes, full_outs):
    return wholes[0][...]


def up_epilogue(result, wholes, blocks, outs):
    inner, acted = outs
    inner[...] = result.astype(BF16)
    acted[...] = (result * sigmoid(result)).astype(BF16)


def up(value, gain, pieces, clock):
    frames, width = value.shape
    columns = pieces[0].shape[1]
    return forward_product(
        clock,
        pieces,
        0,
        columns,
        [value, gain],
        [],
        [((frames, width), BF16)],
        [(BF16, columns), (BF16, columns)],
        normed_prologue,
        up_epilogue,
    )


def add_epilogue(scale, result, wholes, blocks, outs):
    outs[0][...] = blocks[0][...].astype(F32) + scale * result


def added(left, value, scale, pieces, first, columns, clock):
    return forward_product(
        clock,
        pieces,
        first,
        columns,
        [left],
        [(value, columns)],
        [],
        [(F32, columns)],
        plain_prologue,
        functools.partial(add_epilogue, scale),
    )[0]


def attend_epilogue(result, wholes, blocks, outs):
    cosine, sine = wholes[2][...], wholes[3][...]
    columns = result.shape[1] // 3
    scale = HEAD_DIM ** (-0.5)
    outs[0][...] = (rotate(result[:, :columns], cosine, sine) * scale).astype(BF16)
    outs[1][...] = rotate(result[:, columns : 2 * columns], cosine, sine).astype(BF16)
    outs[2][...] = result[:, 2 * columns :].astype(BF16)


def attend_front(value, gain, cosine, sine, pieces, columns, clock):
    return forward_product(
        clock,
        pieces,
        0,
        3 * columns,
        [value, gain, cosine, sine],
        [],
        [(value.shape, BF16)],
        [(BF16, columns)] * 3,
        normed_prologue,
        attend_epilogue,
    )


def store_epilogue(result, wholes, blocks, outs):
    outs[0][...] = result.astype(outs[0].dtype)


def expanded(value, gain, pieces, first, columns, clock):
    return forward_product(
        clock,
        pieces,
        first,
        columns,
        [value, gain],
        [],
        [(value.shape, BF16)],
        [(F32, columns)],
        normed_prologue,
        store_epilogue,
    )


def backward_kernel(first, widths, counts, chunk, epilogue, spots, *refs):
    left_count, whole_count, block_count, full_out_count, block_out_count = counts
    refs = list(refs)

    def take(number):
        taken = refs[:number]
        del refs[:number]
        return taken

    lefts = take(left_count)
    wholes = take(whole_count)
    blocks = take(block_count)
    pieces = take(PIECES)
    full_outs = take(full_out_count)
    block_outs = take(block_out_count)
    left, weights, sems = refs
    step = pl.program_id(0)
    width = sum(widths)

    @pl.when(step == 0)
    def _():
        copies = loads(
            spots,
            pieces,
            first,
            width,
            lambda place, start, extent: weights.at[
                pl.ds(start, extent), pl.ds(place * width, width)
            ],
            sems,
        )
        for copy in copies:
            copy.start()
        for place in range(SLICES):
            offset = place * width
            for item, columns in zip(lefts, widths):
                start = pl.multiple_of(spots[place] * columns, 128)
                left[:, pl.ds(offset, columns)] = item[:, pl.ds(start, columns)]
                offset += columns
        for copy in copies:
            copy.wait()

    rows = weights[pl.ds(pl.multiple_of(step * chunk, 16), chunk), :]
    result = lax.dot_general(
        left[...], rows, (((1,), (1,)), ((), ())), preferred_element_type=F32
    )
    epilogue(spots, result, wholes, blocks, full_outs, block_outs)


def backward_product(clock, pieces, first, lefts, wholes, blocks, chunk, full_outs, block_outs, epilogue):
    rows = pieces[0].shape[0]
    frames = lefts[0].shape[0]
    widths = tuple(item.shape[1] // SLICES for item in lefts)
    width = sum(widths)
    fixed = lambda step, spots: (0, 0)
    along = lambda step, spots: (0, step)
    in_specs = [
        pl.BlockSpec(item.shape, fixed, pipeline_mode=pl.Buffered(1)) for item in lefts + wholes
    ]
    in_specs += [pl.BlockSpec((frames, chunk), along) for _ in blocks]
    in_specs += [pl.BlockSpec(memory_space=pl.ANY)] * PIECES
    out_shape = [jax.ShapeDtypeStruct(shape, kind) for shape, kind in full_outs]
    out_shape += [jax.ShapeDtypeStruct((frames, rows), kind) for kind in block_outs]
    out_specs = [pl.BlockSpec(shape, fixed) for shape, _ in full_outs]
    out_specs += [pl.BlockSpec((frames, chunk), along) for _ in block_outs]
    moved = sum(size_of(item) for item in lefts + wholes + blocks)
    moved += sum(size_of(item) for item in out_shape) + rows * width * SLICES * 2
    outs = pl.pallas_call(
        functools.partial(
            backward_kernel,
            first,
            widths,
            (len(lefts), len(wholes), len(blocks), len(full_outs), len(block_outs)),
            chunk,
            epilogue,
        ),
        out_shape=out_shape,
        grid_spec=pltpu.PrefetchScalarGridSpec(
            num_scalar_prefetch=1,
            grid=(rows // chunk,),
            in_specs=in_specs,
            out_specs=out_specs,
            scratch_shapes=[
                pltpu.VMEM((frames, SLICES * width), BF16),
                pltpu.VMEM((rows, SLICES * width), BF16),
                pltpu.SemaphoreType.DMA((PIECES,)),
            ],
        ),
        compiler_params=pltpu.CompilerParams(
            dimension_semantics=("arbitrary",), vmem_limit_bytes=VMEM_MOST
        ),
        cost_estimate=cost_of(2 * frames * rows * width * SLICES, moved),
    )(clock.spots, *lefts, *wholes, *blocks, *pieces)
    return clock(*outs)


def slope_epilogue(spots, result, wholes, blocks, full_outs, block_outs):
    grad = (result * swish_slope(blocks[0][...].astype(F32))).astype(BF16)
    block_outs[0][...] = grad
    parts = len(full_outs) // 2
    for index, out in enumerate(full_outs):
        columns = out.shape[1]
        start = (index % parts) * columns

        @pl.when(pl.program_id(0) == spots[(1, 3)[index // parts]])
        def _():
            out[...] = grad[:, start : start + columns]


def down_back(outer, inner, pieces, parts, clock):
    frames, depth = inner.shape
    columns = depth // SLICES
    part = ((frames, columns // parts), BF16)
    *sent, grad = backward_product(
        clock, pieces, 0, [outer], [], [inner], columns, [part] * (2 * parts), [BF16], slope_epilogue
    )
    return grad, sent


def send_slices(spots, source, sent):
    columns = source.shape[1] // SLICES
    for offset, place in ((0, 1), (columns, 3)):
        start = pl.multiple_of(spots[place] * columns, 128)
        sent[:, pl.ds(offset, columns)] = source[:, pl.ds(start, columns)]


def norm_back_store(scale, spots, result, value, gain, upstream, outs):
    _, scaled, inverse = normalize(value[...].astype(F32), 1.0)
    delta, gain_grad = normalize_back(result, scaled, inverse, gain[...])
    grad = upstream[...] + delta
    outs[0][...] = grad
    outs[1][...] = gain_grad
    outs[2][...] = (scale * grad).astype(BF16)
    send_slices(spots, outs[2], outs[3])


def norm_epilogue(scale, spots, result, wholes, blocks, full_outs, block_outs):
    norm_back_store(scale, spots, result, wholes[0], wholes[1], wholes[2], full_outs)


def norm_back_product(lefts, value, gain, upstream, pieces, first, scale, clock):
    frames, width = upstream.shape
    return backward_product(
        clock,
        pieces,
        first,
        lefts,
        [value, gain, upstream],
        [],
        width,
        [
            ((frames, width), F32),
            ((1, width), F32),
            ((frames, width), BF16),
            ((frames, width // 2), BF16),
        ],
        [],
        functools.partial(norm_epilogue, scale),
    )


def plain_epilogue(spots, result, wholes, blocks, full_outs, block_outs):
    block_outs[0][...] = result.astype(block_outs[0].dtype)


def plain_back(left, kind, pieces, first, clock):
    return backward_product(
        clock, pieces, first, [left], [], [], pieces[0].shape[0], [], [kind], plain_epilogue
    )[0]


def up_back_kernel(scale, spots, left, value, gain, upstream, *refs):
    pieces = refs[:PIECES]
    out, gain_out, low_out, sent, total, weights, sems = refs[PIECES:]
    step = pl.program_id(0)
    width = weights.shape[2]
    copies = loads(
        spots,
        pieces,
        0,
        width,
        lambda place, start, extent: weights.at[place, pl.ds(start, extent), :],
        sems,
    )

    @pl.when(step == 0)
    def _():
        for copy in copies:
            copy.start()

    for place, group in enumerate(WAITS):

        @pl.when(step == place)
        def _():
            for index in group:
                copies[index].wait()

    result = lax.dot_general(
        left[...], weights[step], (((1,), (1,)), ((), ())), preferred_element_type=F32
    )

    @pl.when(step == 0)
    def _():
        total[...] = result

    @pl.when(step > 0)
    def _():
        total[...] += result

    @pl.when(step == SLICES - 1)
    def _():
        norm_back_store(
            scale, spots, total[...], value, gain, upstream, (out, gain_out, low_out, sent)
        )


def up_back(left, value, gain, upstream, pieces, scale, clock):
    frames, width = upstream.shape
    columns = pieces[0].shape[1]
    fixed = lambda step, spots: (0, 0)
    single = functools.partial(pl.BlockSpec, index_map=fixed, pipeline_mode=pl.Buffered(1))
    moved = size_of(left) + size_of(value) + 2 * size_of(upstream) + width * columns * 8
    outs = pl.pallas_call(
        functools.partial(up_back_kernel, scale),
        out_shape=[
            jax.ShapeDtypeStruct((frames, width), F32),
            jax.ShapeDtypeStruct((1, width), F32),
            jax.ShapeDtypeStruct((frames, width), BF16),
            jax.ShapeDtypeStruct((frames, width // 2), BF16),
        ],
        grid_spec=pltpu.PrefetchScalarGridSpec(
            num_scalar_prefetch=1,
            grid=(SLICES,),
            in_specs=[
                pl.BlockSpec((frames, columns), lambda step, spots: (0, spots[step])),
                single(value.shape),
                single(gain.shape),
                single(upstream.shape),
            ]
            + [pl.BlockSpec(memory_space=pl.ANY)] * PIECES,
            out_specs=[
                pl.BlockSpec((frames, width), fixed),
                pl.BlockSpec((1, width), fixed),
                pl.BlockSpec((frames, width), fixed),
                pl.BlockSpec((frames, width // 2), fixed),
            ],
            scratch_shapes=[
                pltpu.VMEM((frames, width), F32),
                pltpu.VMEM((SLICES, width, columns), BF16),
                pltpu.SemaphoreType.DMA((PIECES,)),
            ],
        ),
        compiler_params=pltpu.CompilerParams(
            dimension_semantics=("arbitrary",), vmem_limit_bytes=VMEM_MOST
        ),
        cost_estimate=cost_of(2 * frames * width * columns * SLICES, moved),
    )(clock.spots, left, value, gain, upstream, *pieces)
    return clock(*outs)


def weight_kernel(count, spots, mine, paired, *refs):
    ups, (far, own) = refs[: 4 * count], refs[-2:]
    dims = (((0,), (0,)), ((), ()))
    offset = 0
    for index in range(count):
        near_own, pair_own, near_far, pair_far = ups[4 * index : 4 * index + 4]
        columns = near_own.shape[1]
        for out, first, second in ((far, near_far, pair_far), (own, near_own, pair_own)):
            result = lax.dot_general(mine[...], first[...], dims, preferred_element_type=F32)
            result += lax.dot_general(paired[...], second[...], dims, preferred_element_type=F32)
            out[:, offset : offset + columns] = result.astype(out.dtype)
        offset += columns


def in_parts(near, sent):
    parts = len(sent) // 2
    return [
        (near, parts * SLICES, part, (sent[part], 0), (sent[parts + part], 0))
        for part in range(parts)
    ]


def packed_pair(near, sent):
    return (near, SLICES, 0, (sent, 0), (sent, 1))


def weight_grads(left, ups, chunk, clock, first=0, depth=None, packed=None, place=0, base=None):
    rows = left[0] if isinstance(left, tuple) else left
    frames = ups[0][0].shape[0]
    depth = depth or rows.shape[1]
    skipped = first // chunk
    in_specs = []
    operands = []
    for core in range(2):
        if isinstance(left, tuple):
            operands.append(left[core])
            index = lambda step, spots: (0, step + skipped)
        else:
            operands.append(left)
            index = lambda step, spots, core=core: (spots[5 + core], step + skipped)
        in_specs.append(pl.BlockSpec((frames, chunk), index))
    widths = []
    for near, parts, part, *beside in ups:
        columns = near.shape[1] // parts
        for which, (item, block) in zip((0, 2), beside):
            operands += [near, item]
            stride = parts // SLICES
            mine = lambda step, spots, which=which, part=part, stride=stride: (
                0,
                spots[which] * stride + part,
            )
            theirs = lambda step, spots, block=block: (0, block)
            in_specs += [pl.BlockSpec((frames, columns), index) for index in (mine, theirs)]
        widths.append(columns)
    total = sum(widths)
    down = lambda step, spots: (step, place)
    count = len(operands)
    if base is not None:
        operands += base
        in_specs += [pl.BlockSpec(memory_space=pl.ANY)] * 2
    outs = pl.pallas_call(
        functools.partial(weight_kernel, len(ups)),
        input_output_aliases={} if base is None else {1 + count: 0, 2 + count: 1},
        out_shape=[jax.ShapeDtypeStruct((depth, packed or total), BF16)] * 2,
        grid_spec=pltpu.PrefetchScalarGridSpec(
            num_scalar_prefetch=1,
            grid=(depth // chunk,),
            in_specs=in_specs,
            out_specs=[pl.BlockSpec((chunk, total), down)] * 2,
        ),
        compiler_params=pltpu.CompilerParams(
            dimension_semantics=("arbitrary",), vmem_limit_bytes=VMEM_MOST
        ),
        cost_estimate=cost_of(
            8 * frames * depth * total, 4 * frames * depth + 8 * frames * total + 4 * depth * total
        ),
    )(clock.spots, *operands)
    return clock(*outs)


def attention_kernel(query, keys, values, across, along, mixed, summary):
    head = pl.program_id(0)
    scores = lax.dot_general(
        query[...], keys[...], (((1,), (1,)), ((), ())), preferred_element_type=F32
    )
    scores = jnp.where(across[...] == along[...], scores, MASKED)
    highest = jnp.max(scores, axis=-1, keepdims=True)
    raised = jnp.exp(scores - highest)
    totals = jnp.sum(raised, axis=-1, keepdims=True)
    probs = (raised * (1.0 / totals)).astype(BF16)
    mixed[...] = jnp.dot(probs, values[...], preferred_element_type=F32).astype(BF16)
    lane = lax.broadcasted_iota(jnp.int32, summary.shape, 1)
    kept = jnp.where(head == 0, jnp.zeros_like(summary), summary[...])
    summary[...] = jnp.where(lane == head, highest + jnp.log(totals), kept)


def attention(query, keys, values, across, along, clock):
    (query,) = clock(query)
    frames, width = query.shape
    head_block = pl.BlockSpec((frames, HEAD_DIM), lambda head: (0, head))
    fixed = lambda head: (0, 0)
    outs = pl.pallas_call(
        attention_kernel,
        out_shape=[
            jax.ShapeDtypeStruct((frames, width), BF16),
            jax.ShapeDtypeStruct((frames, HEAD_DIM), F32),
        ],
        grid=(width // HEAD_DIM,),
        in_specs=[head_block] * 3
        + [pl.BlockSpec((frames, 1), fixed), pl.BlockSpec((1, frames), fixed)],
        out_specs=[head_block, pl.BlockSpec((frames, HEAD_DIM), fixed)],
        compiler_params=pltpu.CompilerParams(
            dimension_semantics=("arbitrary",), vmem_limit_bytes=VMEM_LIMIT
        ),
        cost_estimate=cost_of(4 * frames * frames * width, 8 * frames * width),
    )(query, keys, values, across, along)
    return clock(*outs)


def attention_back_kernel(
    spots, query, keys, values, upstream, summary, across, along, cosine, sine, *outs
):
    head = pl.program_id(0)
    at = pl.ds(pl.multiple_of(head * HEAD_DIM, HEAD_DIM), HEAD_DIM)
    query_out, keys_out, values_out = outs[:3]
    contract_last = (((1,), (1,)), ((), ()))
    contract_first = (((0,), (0,)), ((), ()))
    scores = lax.dot_general(query[...], keys[...], contract_last, preferred_element_type=F32)
    scores = jnp.where(across[...] == along[...], scores, MASKED)
    lane = lax.broadcasted_iota(jnp.int32, summary.shape, 1)
    level = jnp.sum(jnp.where(lane == head, summary[...], 0.0), axis=-1, keepdims=True)
    probs = jnp.exp(scores - level)
    grads = lax.dot_general(upstream[...], values[...], contract_last, preferred_element_type=F32)
    balance = jnp.sum(probs * grads, axis=-1, keepdims=True)
    scores_grad = (probs * (grads - balance)).astype(BF16)
    values_out[:, at] = lax.dot_general(
        probs.astype(BF16), upstream[...], contract_first, preferred_element_type=F32
    ).astype(BF16)
    scale = HEAD_DIM ** (-0.5)
    query_back = jnp.dot(scores_grad, keys[...], preferred_element_type=F32)
    query_out[:, at] = (rotate(query_back, cosine[...], -sine[...]) * scale).astype(BF16)
    keys_back = lax.dot_general(scores_grad, query[...], contract_first, preferred_element_type=F32)
    keys_out[:, at] = rotate(keys_back, cosine[...], -sine[...]).astype(BF16)

    @pl.when(head == pl.num_programs(0) - 1)
    def _():
        for out, sent in zip(outs[:3], outs[3:]):
            send_slices(spots, out, sent)


def attention_back(query, keys, values, upstream, summary, across, along, cosine, sine, clock):
    frames, width = query.shape
    head_block = pl.BlockSpec((frames, HEAD_DIM), lambda head, spots: (0, head))
    fixed = lambda head, spots: (0, 0)
    whole = pl.BlockSpec((frames, HEAD_DIM), fixed)
    outs = pl.pallas_call(
        attention_back_kernel,
        out_shape=[jax.ShapeDtypeStruct((frames, width), BF16)] * 3
        + [jax.ShapeDtypeStruct((frames, width // 2), BF16)] * 3,
        grid_spec=pltpu.PrefetchScalarGridSpec(
            num_scalar_prefetch=1,
            grid=(width // HEAD_DIM,),
            in_specs=[head_block] * 4
            + [
                whole,
                pl.BlockSpec((frames, 1), fixed),
                pl.BlockSpec((1, frames), fixed),
                whole,
                whole,
            ],
            out_specs=[pl.BlockSpec((frames, width), fixed)] * 3
            + [pl.BlockSpec((frames, width // 2), fixed)] * 3,
        ),
        compiler_params=pltpu.CompilerParams(
            dimension_semantics=("arbitrary",), vmem_limit_bytes=VMEM_MOST
        ),
        cost_estimate=cost_of(10 * frames * frames * width, 14 * frames * width),
    )(clock.spots, query, keys, values, upstream, summary, across, along, cosine, sine)
    outs = clock(*outs)
    return outs[:3], outs[3:]


def bare_call(kernel, outs, operands, clock, flops=0):
    fixed = lambda spots: (0, 0)
    results = pl.pallas_call(
        kernel,
        out_shape=[jax.ShapeDtypeStruct(shape, kind) for shape, kind in outs],
        grid_spec=pltpu.PrefetchScalarGridSpec(
            num_scalar_prefetch=1,
            grid=(),
            in_specs=[
                pl.BlockSpec(item.shape, lambda spots, item=item: (0,) * item.ndim)
                for item in operands
            ],
            out_specs=[pl.BlockSpec(shape, fixed) for shape, _ in outs],
        ),
        compiler_params=pltpu.CompilerParams(vmem_limit_bytes=VMEM_MOST),
        cost_estimate=cost_of(flops, sum(size_of(item) for item in operands)),
    )(clock.spots, *operands)
    return clock(*results)


def final_kernel(spots, value, gain, valid, cotangent, out, grad_out, gain_out, low_out, sent):
    normed, scaled, inverse = normalize(value[...], gain[...])
    out[...] = (normed * valid[...]).astype(BF16)
    upstream = cotangent[...].astype(F32) * valid[...]
    grad, gain_grad = normalize_back(upstream, scaled, inverse, gain[...])
    grad_out[...] = grad
    gain_out[...] = gain_grad
    low_out[...] = (0.5 * grad).astype(BF16)
    send_slices(spots, low_out, sent)


def final(value, gain, valid, cotangent, clock):
    shape = value.shape
    return bare_call(
        final_kernel,
        [
            (shape, BF16),
            (shape, F32),
            (gain.shape, F32),
            (shape, BF16),
            ((shape[0], shape[1] // 2), BF16),
        ],
        [value, gain, valid, cotangent],
        clock,
    )


TAPS = 5
REACH = 2
CONV_BLOCK = 256


def convolve_kernel(spots, values, gates, taps, same, valid, mixed, shares):
    glued = values[...] * sigmoid(gates[...])
    frames = glued.shape[0]
    result = jnp.zeros_like(glued)
    for index in range(TAPS):
        moved = pltpu.roll(glued, (REACH - index) % frames, 0) if index != REACH else glued
        result += taps[index : index + 1, :] * moved * same[:, index : index + 1]
    mixed[...] = result
    counted = jnp.maximum(jnp.sum(valid[...]), 1.0)
    local_sum = jnp.sum(result * valid[...], axis=0, keepdims=True)
    spread = (result - local_sum / counted) * valid[...]
    shares[0:1, :] = local_sum
    shares[1:2, :] = jnp.sum(spread * spread, axis=0, keepdims=True)


def convolve(expand, taps, same, valid, clock):
    frames, width = expand.shape[0], expand.shape[1] // 2
    blocks = width // CONV_BLOCK
    along = lambda step, spots: (0, step)
    fixed = lambda step, spots: (0, 0)
    outs = pl.pallas_call(
        convolve_kernel,
        out_shape=[
            jax.ShapeDtypeStruct((frames, width), F32),
            jax.ShapeDtypeStruct((2, width), F32),
        ],
        grid_spec=pltpu.PrefetchScalarGridSpec(
            num_scalar_prefetch=1,
            grid=(blocks,),
            in_specs=[
                pl.BlockSpec((frames, CONV_BLOCK), along),
                pl.BlockSpec((frames, CONV_BLOCK), lambda step, spots: (0, step + blocks)),
                pl.BlockSpec((TAPS, CONV_BLOCK), along),
                pl.BlockSpec(same.shape, fixed),
                pl.BlockSpec(valid.shape, fixed),
            ],
            out_specs=[
                pl.BlockSpec((frames, CONV_BLOCK), along),
                pl.BlockSpec((2, CONV_BLOCK), along),
            ],
        ),
        compiler_params=pltpu.CompilerParams(
            dimension_semantics=("arbitrary",), vmem_limit_bytes=VMEM_LIMIT
        ),
        cost_estimate=cost_of(0, size_of(expand)),
    )(clock.spots, expand, expand, taps, same, valid)
    return clock(*outs)


def batch_prologue(wholes, full_outs):
    mixed, mean, inverse, gain, shift = (item[...] for item in wholes)
    normal = (mixed - mean) * inverse * gain + shift
    acted = (normal * sigmoid(normal)).astype(BF16)
    full_outs[0][...] = acted
    return acted


def projected(mixed, mean, inverse, gain, shift, value, pieces, first, columns, clock):
    return forward_product(
        clock,
        pieces,
        first,
        columns,
        [mixed, mean, inverse, gain, shift],
        [(value, columns)],
        [(mixed.shape, BF16)],
        [(F32, columns)],
        batch_prologue,
        functools.partial(add_epilogue, 1.0),
    )


def project_epilogue(spots, result, wholes, blocks, full_outs, block_outs):
    mixed, mean, inverse, gain, shift, valid = (item[...] for item in wholes)
    standard = (mixed - mean) * inverse
    grad = result * swish_slope(standard * gain + shift)
    full_outs[0][...] = grad
    counted = grad * valid
    full_outs[1][0:1, :] = jnp.sum(counted, axis=0, keepdims=True)
    full_outs[1][1:2, :] = jnp.sum(counted * standard, axis=0, keepdims=True)


def project_back(outer, mixed, mean, inverse, gain, shift, valid, pieces, first, clock):
    frames, width = mixed.shape
    return backward_product(
        clock,
        pieces,
        first,
        [outer],
        [mixed, mean, inverse, gain, shift, valid],
        [],
        width,
        [((frames, width), F32), ((2, width), F32)],
        [],
        project_epilogue,
    )


def convolve_back_kernel(
    spots, grad, mixed, values, gates, taps, same, valid, sums, mean, inverse, gain, count, out, taps_out, *sent
):
    step = pl.program_id(0)
    frames, columns = grad.shape
    width = out.shape[1] // 2
    standard = (mixed[...] - mean[...]) * inverse[...]
    share = (sums[0:1, :] + standard * sums[1:2, :]) / count[...]
    upstream = gain[...] * inverse[...] * (grad[...] - valid[...] * share)
    gate = sigmoid(gates[...])
    glued = values[...] * gate
    back = jnp.zeros_like(upstream)
    for index in range(TAPS):
        term = upstream * same[:, index : index + 1]
        if index == REACH:
            moved, returned = glued, term
        else:
            moved = pltpu.roll(glued, (REACH - index) % frames, 0)
            returned = pltpu.roll(term, (index - REACH) % frames, 0)
        taps_out[index : index + 1, :] = jnp.sum(term * moved, axis=0, keepdims=True)
        back += taps[index : index + 1, :] * returned
    low = pl.multiple_of(step * columns, 128)
    high = pl.multiple_of(width + step * columns, 128)
    out[:, pl.ds(low, columns)] = (back * gate).astype(BF16)
    out[:, pl.ds(high, columns)] = (back * glued * (1.0 - gate)).astype(BF16)

    @pl.when(step == pl.num_programs(0) - 1)
    def _():
        for part, place in zip(sent, (1, 3)):
            start = pl.multiple_of(spots[place] * part.shape[1], 128)
            part[...] = out[:, pl.ds(start, part.shape[1])]


def convolve_back(grad, mixed, expand, taps, same, valid, sums, mean, inverse, gain, count, clock):
    frames, width = mixed.shape
    blocks = width // CONV_BLOCK
    along = lambda step, spots: (0, step)
    fixed = lambda step, spots: (0, 0)
    wide = pl.BlockSpec((frames, CONV_BLOCK), along)
    row = pl.BlockSpec((1, CONV_BLOCK), along)
    outs = pl.pallas_call(
        convolve_back_kernel,
        out_shape=[
            jax.ShapeDtypeStruct((frames, 2 * width), BF16),
            jax.ShapeDtypeStruct((TAPS, width), F32),
        ]
        + [jax.ShapeDtypeStruct((frames, width // 2), BF16)] * 2,
        grid_spec=pltpu.PrefetchScalarGridSpec(
            num_scalar_prefetch=1,
            grid=(blocks,),
            in_specs=[
                wide,
                wide,
                wide,
                pl.BlockSpec((frames, CONV_BLOCK), lambda step, spots: (0, step + blocks)),
                pl.BlockSpec((TAPS, CONV_BLOCK), along),
                pl.BlockSpec(same.shape, fixed),
                pl.BlockSpec(valid.shape, fixed),
                pl.BlockSpec((2, CONV_BLOCK), along),
                row,
                row,
                row,
                pl.BlockSpec((1, 1), fixed),
            ],
            out_specs=[
                pl.BlockSpec((frames, 2 * width), fixed),
                pl.BlockSpec((TAPS, CONV_BLOCK), along),
            ]
            + [pl.BlockSpec((frames, width // 2), fixed)] * 2,
        ),
        compiler_params=pltpu.CompilerParams(
            dimension_semantics=("arbitrary",), vmem_limit_bytes=VMEM_MOST
        ),
        cost_estimate=cost_of(0, size_of(expand) * 2),
    )(clock.spots, grad, mixed, expand, expand, taps, same, valid, sums, mean, inverse, gain, count)
    return clock(*outs)


def folds_kernel(kinds, spots, *refs):
    refs = list(refs)

    def take(number):
        taken = refs[:number]
        del refs[:number]
        return taken

    inputs = [take(FOLD_INPUTS[kind]) for kind in kinds]
    for kind, items in zip(kinds, inputs):
        if kind == "blocks":
            (blocks,) = items
            (out,) = take(1)
            total = blocks[0].astype(F32)
            for index in range(1, blocks.shape[0]):
                total += blocks[index].astype(F32)
            out[...] = total.astype(BF16)
        else:
            for first in range(0, len(items), 2):
                (out,) = take(1)
                total = items[first][...].astype(F32) + items[first + 1][...].astype(F32)
                out[...] = total.astype(out.dtype)


FOLD_INPUTS = {"split": 4, "sum": 2, "blocks": 1}


def folds(items, clock):
    steps = 2
    for kind, operands in items:
        rows = operands[-1].shape[-2] // (2 if kind == "split" else 1)
        if rows % 32:
            steps = 1
    operands, in_specs, out_specs, out_shape = [], [], [], []

    def put(item, block, index):
        operands.append(item)
        in_specs.append(pl.BlockSpec(block, index))

    def give(shape, kind):
        out_shape.append(jax.ShapeDtypeStruct(shape, kind))
        block = (shape[0] // steps, shape[1])
        out_specs.append(pl.BlockSpec(block, lambda step, spots: (step, 0)))

    for kind, (*value, moving) in items:
        rows, columns = moving.shape[-2:]
        if kind == "split":
            block = (rows // 2 // steps, columns)
            kept = lambda step, spots: (spots[BITS] * steps + step, 0)
            sent = lambda step, spots: ((1 - spots[BITS]) * steps + step, 0)
            for index in (kept, sent):
                put(value[0], block, index)
                put(moving, block, index)
            give((rows // 2, columns), F32)
            give((rows // 2, columns), BF16)
        elif kind == "sum":
            for item in (value[0], moving):
                put(item, (rows // steps, columns), lambda step, spots: (step, 0))
            give((rows, columns), BF16)
        else:
            block = (moving.shape[0], rows // steps, columns)
            put(moving, block, lambda step, spots: (0, step, 0))
            give((rows, columns), BF16)
    outs = pl.pallas_call(
        functools.partial(folds_kernel, tuple(kind for kind, _ in items)),
        out_shape=out_shape,
        grid_spec=pltpu.PrefetchScalarGridSpec(
            num_scalar_prefetch=1,
            grid=(steps,),
            in_specs=in_specs,
            out_specs=out_specs,
        ),
        compiler_params=pltpu.CompilerParams(
            dimension_semantics=("arbitrary",), vmem_limit_bytes=VMEM_MOST
        ),
        cost_estimate=cost_of(0, sum(size_of(item) for item in operands)),
    )(clock.spots, *operands)
    return list(clock(*outs))


def unfold_kernel(widths, size, spots, value, *outs):
    step = pl.program_id(0)
    block = value.shape[0] // size
    for item in range(size // 2):
        place = 2 * item + step
        rows = value[pl.ds(pl.multiple_of(place * block, 16), block), :].astype(F32)
        offset = 0
        for out, width in zip(outs, widths):
            out[item * block : (item + 1) * block, :] = rows[:, offset : offset + width]
            offset += width


def unfold(value, size, widths, clock):
    rows, columns = value.shape
    outs = pl.pallas_call(
        functools.partial(unfold_kernel, widths, size),
        out_shape=[jax.ShapeDtypeStruct((rows, width), F32) for width in widths],
        grid_spec=pltpu.PrefetchScalarGridSpec(
            num_scalar_prefetch=1,
            grid=(2,),
            in_specs=[pl.BlockSpec((rows, columns), lambda step, spots: (0, 0))],
            out_specs=[
                pl.BlockSpec((rows // 2, width), lambda step, spots: (step, 0))
                for width in widths
            ],
        ),
        compiler_params=pltpu.CompilerParams(
            dimension_semantics=("arbitrary",), vmem_limit_bytes=VMEM_MOST
        ),
        cost_estimate=cost_of(0, size_of(value)),
    )(clock.spots, value)
    return clock(*outs)


class Clock:
    def __init__(self, spots):
        self.spots = spots

    def __call__(self, *values):
        self.spots, *values = lax.optimization_barrier((self.spots,) + values)
        return values

    def send(self, value, axis, mask):
        (value,) = self(value)
        return swapped(value, axis, mask)


class Gather:
    def __init__(self, slices, clock):
        self.own = slices[0] if len(slices) == 1 else jnp.concatenate(slices, axis=1)
        self.half = self.own.shape[0] // 2
        self.clock = clock
        self.crossing = lax.dynamic_slice_in_dim(
            self.own, half_sent() * self.half, self.half, axis=0
        )

    def cross(self):
        self.across = self.clock.send(self.crossing, "fsdp", 2)

    def beside(self):
        self.own_beside = joined(self.own)

    def forward(self):
        quarter = self.half // 2
        self.across, self.own_beside = self.clock(self.across, self.own_beside)
        self.first = swapped(self.across[:quarter], "dp", 1)
        self.second = swapped(self.across[quarter:], "dp", 2)
        self.across_beside = swapped(self.across, "fsdp", 1)

    def turn(self):
        self.first, self.second, self.across_beside = self.clock(
            self.first, self.second, self.across_beside
        )
        self.first_beside = swapped(self.first, "fsdp", 1)
        self.second_beside = swapped(self.second, "fsdp", 1)

    def finish(self):
        self.first_beside, self.second_beside = self.clock(
            self.first_beside, self.second_beside
        )
        self.pieces = (
            self.own,
            self.own_beside,
            self.across,
            self.first,
            self.second,
            self.across_beside,
            self.first_beside,
            self.second_beside,
        )


def half_sent():
    place = lax.axis_index("dp")
    return (place ^ (place >> 1)) & 1


class Reduction:
    def __init__(self, far, own, clock, wide=False):
        self.size = lax.axis_size("dp")
        self.clock = clock
        self.value = own
        self.sent = far
        self.stage = 0
        self.wide = wide
        self.moving = None
        self.whole = None

    def exchange(self, blocks):
        groups = [[i for i in range(self.size) if i % 2 == low] for low in range(2)]
        return lax.all_to_all(blocks, "dp", 0, 0, axis_index_groups=groups, tiled=True)

    def fold(self, moving):
        self.stage += 1
        if self.stage == 1:
            return "split", (self.value, moving)
        if self.stage == 2:
            return "sum", (self.value, moving)
        if self.stage == 3:
            return "blocks", (moving,)
        self.sent = moving.reshape(-1, moving.shape[2])
        return None

    def take(self, outs):
        if self.stage == 1:
            self.value = outs.pop(0)
        self.sent = outs.pop(0)
        if self.stage == 2:
            rows, columns = self.sent.shape
            members = self.size // 2
            self.sent = self.sent.reshape(members, rows // members, columns)

    def send(self, sent):
        if self.stage == 0:
            self.moving = swapped(sent, "fsdp", 2)
        elif self.stage == 1:
            self.moving = swapped(sent, "dp", 1)
        elif self.stage == 2:
            self.moving = self.exchange(sent)
        elif self.stage == 3 and self.wide:
            copies = (self.size // 2,) + sent.shape
            self.moving = self.exchange(jnp.broadcast_to(sent[None], copies))
        elif self.stage == 3:
            self.whole = lax.all_gather(sent, "dp", axis=0, tiled=True)
            self.moving = None
        else:
            self.value = sent
            self.moving = swapped(sent, "dp", 1)

    def ended(self):
        return self.whole is not None or self.stage == 4

    def result(self, widths=None):
        while not self.ended():
            turn(self.clock, self)
        if self.wide:
            (moving,) = self.clock(self.moving)
            return [
                jnp.where(
                    lax.axis_index("dp") & 1 == 0,
                    jnp.concatenate([self.value, moving], axis=0),
                    jnp.concatenate([moving, self.value], axis=0),
                ).astype(F32)
            ]
        (whole,) = self.clock(self.whole)
        return unfold(whole, self.size, widths or (whole.shape[1],), self.clock)


def turn(clock, *groups):
    groups = [group for group in groups if not group.ended()]
    waiting = [group for group in groups if group.moving is not None]
    fresh = [group for group in groups if group.moving is None]
    arrived = clock(*[group.moving for group in waiting], *[group.sent for group in fresh])
    for group, item in zip(fresh, arrived[len(waiting) :]):
        group.send(item)
    sums = [(group, group.fold(moving)) for group, moving in zip(waiting, arrived)]
    sums = [(group, item) for group, item in sums if item is not None]
    if sums:
        outs = folds([item for _, item in sums], clock)
        for group, _ in sums:
            group.take(outs)
    sent = clock(*[group.sent for group in waiting])
    for group, item in zip(waiting, sent):
        group.send(item)


def joined(value):
    groups = [[i, i + 1] for i in range(0, lax.axis_size("fsdp"), 2)]
    return lax.all_gather(value, "fsdp", axis=0, tiled=True, axis_index_groups=groups)


class Doubling:
    def __init__(self, value):
        self.sent = value
        self.moving = None
        self.left = [
            (axis, 1 << bit)
            for axis in ("fsdp", "dp")
            for bit in range(lax.axis_size(axis).bit_length() - 1)
        ]

    def fold(self, moving):
        self.sent = self.sent + moving

    def send(self, sent):
        self.sent = sent
        if self.left:
            axis, mask = self.left.pop(0)
            self.moving = swapped(sent, axis, mask)
        else:
            self.moving = None
            self.left = None

    def ended(self):
        return self.left is None

    def result(self, clock):
        while not self.ended():
            turn(clock, self)
        return self.sent


def swapped(value, axis, mask):
    size = lax.axis_size(axis)
    return lax.ppermute(value, axis, [(i, i ^ mask) for i in range(size)])


def spread_sum(rows):
    axes = ("dp", "fsdp")
    count = lax.axis_size(axes)
    copies = jnp.broadcast_to(rows[None], (count,) + rows.shape)
    return lax.all_to_all(copies, axes, 0, 0, tiled=True)


def neighbours(segment, taps):
    frames = segment.shape[0]
    reach = (taps - 1) // 2
    side = jnp.pad(segment, (reach, reach), constant_values=-1)
    columns = [side[index : index + frames] == segment for index in range(taps)]
    return jnp.pad(jnp.stack(columns, axis=1).astype(F32), ((0, 0), (0, 8 - taps)))


def body(
    frames_in,
    cotangent,
    lengths,
    first_gain,
    first_up,
    first_down,
    attend_gain,
    query_proj,
    key_proj,
    value_proj,
    output_proj,
    conv_gain,
    conv_expand,
    conv_kernel,
    batch_gain,
    batch_shift,
    conv_project,
    second_gain,
    second_up,
    second_down,
    final_gain,
):
    frames, width = frames_in.shape
    slot = lax.axis_index("fsdp")
    part = half_sent()
    row, rows = lax.axis_index("dp"), lax.axis_size("dp")
    bits = [(row >> which) & 1 for which in range(rows.bit_length() - 1)]
    spots = jnp.stack(
        [slot, slot ^ 1, slot ^ 2, slot ^ 3, part, slot & 1, 1 - (slot & 1)] + bits
    ).astype(jnp.int32)
    clock = Clock(spots)
    segment, position, valid = layout(lengths[0], frames)
    cosine, sine = rotation(position, HEAD_DIM // 2)
    column = valid[:, None]
    seg_across, seg_along = segment[:, None], segment[None, :]
    first_gain, attend_gain, conv_gain, second_gain, final_gain, batch_gain, batch_shift = (
        item[None]
        for item in (
            first_gain,
            attend_gain,
            conv_gain,
            second_gain,
            final_gain,
            batch_gain,
            batch_shift,
        )
    )
    same = neighbours(segment, conv_kernel.shape[0])
    narrow = query_proj.shape[1]
    wide = conv_expand.shape[1]

    def pair(value):
        return clock.send(value, "fsdp", 1)

    first_ups = Gather((first_up,), clock)
    first_ups.cross()
    first_ups.beside()
    first_downs = Gather((first_down,), clock)
    attends = Gather((query_proj, key_proj, value_proj), clock)
    convs = Gather((output_proj, conv_expand, conv_project), clock)
    second_ups = Gather((second_up,), clock)
    second_downs = Gather((second_down,), clock)
    later = (first_downs, attends, convs, second_ups, second_downs)
    for group, item in zip(later, clock(*[group.crossing for group in later])):
        group.crossing = item
        group.beside()
    first_ups.forward()
    first_downs.cross()
    attends.cross()
    first_ups.turn()
    first_ups.finish()
    first_normed, first_inner, first_acted = up(frames_in, first_gain, first_ups.pieces, clock)
    first_downs.forward()
    convs.cross()
    first_downs.turn()
    first_downs.finish()
    attends.forward()
    second_ups.cross()
    after_first = added(
        first_acted, frames_in, 0.5, first_downs.pieces, 0, first_down.shape[1], clock
    )
    attends.turn()
    attends.finish()
    attend_normed, query, keys, values = attend_front(
        after_first, attend_gain, cosine, sine, attends.pieces, narrow, clock
    )
    convs.forward()
    attended, summary = attention(query, keys, values, seg_across, seg_along, clock)
    convs.turn()
    convs.finish()
    after_attend = added(attended, after_first, 1.0, convs.pieces, 0, narrow, clock)
    conv_normed, expand = expanded(after_attend, conv_gain, convs.pieces, narrow, wide, clock)

    mixed, local = convolve(expand, conv_kernel, same, column, clock)
    local = jnp.concatenate([local, jnp.broadcast_to(jnp.sum(valid), (2, 128))], axis=1)
    shares = spread_sum(local)
    second_downs.cross()
    second_ups.forward()
    (shares,) = clock(shares)
    second_ups.turn()
    counts = shares[:, 0, width : width + 1]
    count = jnp.sum(counts)
    sums = shares[:, 0, :width]
    mean = jnp.sum(sums, axis=0) / count
    offsets = sums / jnp.maximum(counts, 1.0) - mean
    variance = jnp.sum(shares[:, 1, :width] + counts * offsets * offsets, axis=0) / count
    deviation_inverse = lax.rsqrt(variance + EPSILON)
    mean_row, inverse_row = mean[None], deviation_inverse[None]
    conv_acted, after_conv = projected(
        mixed,
        mean_row,
        inverse_row,
        batch_gain,
        batch_shift,
        after_attend,
        convs.pieces,
        narrow + wide,
        narrow,
        clock,
    )
    second_ups.finish()
    second_downs.forward()
    second_normed, second_inner, second_acted = up(
        after_conv, second_gain, second_ups.pieces, clock
    )
    second_downs.turn()
    second_downs.finish()
    pair_acted, pair_normed = pair(second_acted), pair(second_normed)
    after_second = added(
        second_acted, after_conv, 0.5, second_downs.pieces, 0, second_down.shape[1], clock
    )
    pair_acted, pair_normed = clock(pair_acted, pair_normed)
    layer_out, upstream, final_gain_grad, outer, sent = final(
        after_second, final_gain, column, cotangent, clock
    )
    (pair_outer,) = clock(pair(sent))
    both_conv_acted, both_conv, both_attended, both_attend, both_first_acted, both_first = (
        joined(item)
        for item in clock(
            conv_acted, conv_normed, attended, attend_normed, first_acted, first_normed
        )
    )

    second_down_sum = Reduction(
        *weight_grads((second_acted, pair_acted), [packed_pair(outer, pair_outer)], 1024, clock),
        clock,
    )
    turn(clock, second_down_sum)
    inner_grad, sent = down_back(outer, second_inner, second_downs.pieces, 2, clock)
    pair_inner = [pair(item) for item in sent]
    upstream, second_gain_grad, outer, sent = up_back(
        inner_grad, after_conv, second_gain, upstream, second_ups.pieces, 1.0, clock
    )
    pair_inner = clock(*pair_inner)
    pair_outer = pair(sent)
    normal_grad, local = project_back(
        outer,
        mixed,
        mean_row,
        inverse_row,
        batch_gain,
        batch_shift,
        column,
        convs.pieces,
        narrow + wide,
        clock,
    )
    (local,) = clock(local)
    pieces = spread_sum(local)
    second_up_sum = Reduction(
        *weight_grads((second_normed, pair_normed), in_parts(inner_grad, pair_inner), 512, clock),
        clock,
    )
    pair_outer, both_conv_acted = clock(pair_outer, both_conv_acted)
    conv_part = weight_grads(
        both_conv_acted,
        [packed_pair(outer, pair_outer)],
        512,
        clock,
        packed=wide + narrow,
        place=wide // narrow,
    )
    (pieces,) = clock(pieces)
    turn(clock, second_up_sum, second_down_sum)
    sums = jnp.sum(pieces, axis=0)
    expand_back, kernel_local, *sent = convolve_back(
        normal_grad,
        mixed,
        expand,
        conv_kernel,
        same,
        column,
        sums,
        mean_row,
        inverse_row,
        batch_gain,
        count.reshape(1, 1),
        clock,
    )
    pair_back = [pair(item) for item in sent]
    upstream, conv_gain_grad, outer, sent = norm_back_product(
        [expand_back], after_attend, conv_gain, upstream, convs.pieces, narrow, 1.0, clock
    )
    *pair_back, both_conv = clock(*pair_back, both_conv)
    pair_outer = pair(sent)
    conv_part = weight_grads(
        both_conv,
        [(expand_back, SLICES, 0, *((item, 0) for item in pair_back))],
        512,
        clock,
        packed=wide + narrow,
        base=conv_part,
    )
    conv_sum = Reduction(*conv_part, clock)
    mixed_back = plain_back(outer, BF16, convs.pieces, 0, clock)
    pair_outer, both_attended = clock(pair_outer, both_attended)
    turn(clock, conv_sum, second_up_sum, second_down_sum)
    backs, sent = attention_back(
        query, keys, values, mixed_back, summary, seg_across, seg_along, cosine, sine, clock
    )
    pair_backs = [pair(item) for item in sent]
    attend_part = weight_grads(
        both_attended, [packed_pair(outer, pair_outer)], 512, clock, packed=4 * narrow, place=3
    )
    *pair_backs, both_attend = clock(*pair_backs, both_attend)
    attend_part = weight_grads(
        both_attend,
        [packed_pair(item, other) for item, other in zip(backs, pair_backs)],
        512,
        clock,
        packed=4 * narrow,
        base=attend_part,
    )
    attend_sum = Reduction(*attend_part, clock)
    turn(clock, attend_sum, conv_sum, second_up_sum, second_down_sum)
    upstream, attend_gain_grad, outer, sent = norm_back_product(
        backs, after_first, attend_gain, upstream, attends.pieces, 0, 0.5, clock
    )
    (pair_outer,) = clock(pair(sent))
    (both_first_acted,) = clock(both_first_acted)
    first_down_sum = Reduction(
        *weight_grads(both_first_acted, [packed_pair(outer, pair_outer)], 1024, clock), clock
    )
    inner_grad, sent = down_back(outer, first_inner, first_downs.pieces, 1, clock)
    turn(clock, first_down_sum, attend_sum, conv_sum, second_up_sum)
    *pair_inner, both_first = clock(*[pair(item) for item in sent], both_first)
    first_up_sum = Reduction(
        *weight_grads(both_first, in_parts(inner_grad, pair_inner), 512, clock), clock, wide=True
    )
    turn(clock, first_up_sum)
    upstream, first_gain_grad, _, _ = up_back(
        inner_grad, frames_in, first_gain, upstream, first_ups.pieces, 1.0, clock
    )
    minor = jnp.concatenate(
        [
            first_gain_grad,
            attend_gain_grad,
            conv_gain_grad,
            second_gain_grad,
            final_gain_grad,
            kernel_local,
        ]
    )
    minors = Doubling(minor)
    turn(clock, minors, first_down_sum, attend_sum, conv_sum)
    (second_down_grad,) = second_down_sum.result()
    turn(clock, minors, first_down_sum, attend_sum)
    turn(clock, first_up_sum)
    (second_up_grad,) = second_up_sum.result()
    turn(clock, minors, first_down_sum)
    turn(clock, minors, first_up_sum)
    expand_grad, project_grad = conv_sum.result((wide, narrow))
    turn(clock, minors, first_up_sum)
    query_grad, key_grad, value_grad, output_grad = attend_sum.result((narrow,) * 4)
    turn(clock, first_up_sum)
    minor_sums = minors.result(clock)
    (first_down_grad,) = first_down_sum.result()
    (first_up_grad,) = first_up_sum.result()
    shift_grad, scale_grad = sums
    taps = conv_kernel.shape[0]
    return (
        layer_out,
        upstream,
        first_up_grad,
        first_down_grad,
        query_grad,
        key_grad,
        value_grad,
        output_grad,
        expand_grad,
        project_grad,
        second_up_grad,
        second_down_grad,
        minor_sums[0],
        minor_sums[1],
        minor_sums[2],
        minor_sums[3],
        minor_sums[4],
        minor_sums[5 : 5 + taps],
        scale_grad,
        shift_grad,
        mean,
        variance,
    )


def solution(mesh):
    placed = (
        P(("dp", "fsdp"), None),
        P(("dp", "fsdp"), None),
        P(("dp", "fsdp"), None),
        P(),
        P(None, "fsdp"),
        P(None, "fsdp"),
        P(),
        P(None, "fsdp"),
        P(None, "fsdp"),
        P(None, "fsdp"),
        P(None, "fsdp"),
        P(),
        P(None, "fsdp"),
        P(),
        P(),
        P(),
        P(None, "fsdp"),
        P(),
        P(None, "fsdp"),
        P(None, "fsdp"),
        P(),
    )
    return jax.shard_map(
        body,
        mesh=mesh,
        in_specs=placed,
        out_specs=(
            P(("dp", "fsdp"), None),
            P(("dp", "fsdp"), None),
            P(None, "fsdp"),
            P(None, "fsdp"),
            P(None, "fsdp"),
            P(None, "fsdp"),
            P(None, "fsdp"),
            P(None, "fsdp"),
            P(None, "fsdp"),
            P(None, "fsdp"),
            P(None, "fsdp"),
            P(None, "fsdp"),
            P(),
            P(),
            P(),
            P(),
            P(),
            P(),
            P(),
            P(),
            P(),
            P(),
        ),
        check_vma=False,
    )
```

```python
import functools

import jax
import jax.numpy as jnp
from jax import lax
from jax.experimental import pallas as pl
from jax.experimental.pallas import tpu as pltpu
from jax.sharding import PartitionSpec as P

HEADS = 8
HEAD_DIM = 128


EPSILON = 1e-05
MASKED = -1e30
SLICES = 4
VMEM_LIMIT = 60 * 1024 * 1024
VMEM_MOST = 63 * 1024 * 1024 + 512 * 1024
COST_SCALE = 0.01
BITS = 7

F32 = jnp.float32
BF16 = jnp.bfloat16


def cost_of(flops, moved):
    return pl.CostEstimate(
        flops=int(flops * COST_SCALE),
        transcendentals=0,
        bytes_accessed=int(moved * COST_SCALE),
    )


def size_of(item):
    return item.size * item.dtype.itemsize


def normalize(value, gain):
    centre = jnp.mean(value, axis=-1, keepdims=True)
    centred = value - centre
    inverse = lax.rsqrt(jnp.mean(centred * centred, axis=-1, keepdims=True) + EPSILON)
    scaled = centred * inverse
    return (scaled * gain, scaled, inverse)


def normalize_back(upstream, scaled, inverse, gain):
    inner = upstream * gain
    first_mean = jnp.mean(inner, axis=-1, keepdims=True)
    second_mean = jnp.mean(inner * scaled, axis=-1, keepdims=True)
    return (
        inverse * (inner - first_mean - scaled * second_mean),
        jnp.sum(upstream * scaled, axis=0, keepdims=True),
    )


def sigmoid(value):
    return 0.5 * jnp.tanh(0.5 * value) + 0.5


def swish_slope(value):
    gate = sigmoid(value)
    return gate * (1.0 + value * (1.0 - gate))


def layout(row, frames):
    ends = jnp.cumsum(row, dtype=jnp.int32)
    times = jnp.arange(frames, dtype=jnp.int32)
    reached = times[:, None] >= ends[None, :]
    segment = jnp.sum(reached.astype(jnp.int32), axis=1, dtype=jnp.int32)
    start = jnp.max(jnp.where(reached, ends[None, :], 0), axis=1)
    position = (times - start).astype(jnp.float32)
    valid = (times < ends[-1]).astype(jnp.float32)
    return (segment, position, valid)


def rotation(position, half):
    rates = 10000.0 ** (-jnp.arange(half, dtype=jnp.float32) / half)
    angle = position[:, None] * rates[None, :]
    cosine, sine = jnp.cos(angle), jnp.sin(angle)
    return (
        jnp.concatenate([cosine, cosine], axis=1),
        jnp.concatenate([-sine, sine], axis=1),
    )


def rotate(value, cosine, sine):
    heads = []
    for start in range(0, value.shape[1], HEAD_DIM):
        head = value[:, start : start + HEAD_DIM]
        heads.append(head * cosine + pltpu.roll(head, HEAD_DIM // 2, 1) * sine)
    return heads[0] if len(heads) == 1 else jnp.concatenate(heads, axis=1)


def loads(spots, pieces, first, width, target, sems):
    half = pieces[2].shape[0]
    quarter = half // 2
    low = pl.multiple_of(spots[4] * half, 16)
    high = pl.multiple_of((1 - spots[4]) * half, 16)
    rows = pieces[0].shape[0]
    beside = pl.multiple_of(spots[6] * rows, 16)
    places = (
        (0, 0, rows),
        (1, 0, rows),
        (2, low, half),
        (2, high, quarter),
        (2, high + quarter, quarter),
        (3, low, half),
        (3, high, quarter),
        (3, high + quarter, quarter),
    )
    return [
        pltpu.make_async_copy(
            piece.at[pl.ds(beside if index == 1 else 0, extent), pl.ds(first, width)],
            target(place, start, extent),
            sems.at[index],
        )
        for index, (piece, (place, start, extent)) in enumerate(zip(pieces, places))
    ]


PIECES = 8
WAITS = ((0,), (1,), (2, 3, 4), (5, 6, 7))


def forward_kernel(first, width, counts, prologue, epilogue, spots, *refs):
    whole_count, block_count, full_out_count, block_out_count = counts
    refs = list(refs)

    def take(number):
        taken = refs[:number]
        del refs[:number]
        return taken

    wholes = take(whole_count)
    blocks = take(block_count)
    pieces = take(PIECES)
    full_outs = take(full_out_count)
    block_outs = take(block_out_count)
    left, weights, sems = refs
    step = pl.program_id(0)
    copies = loads(
        spots,
        pieces,
        first,
        width,
        lambda place, start, extent: weights.at[place, pl.ds(start, extent), :],
        sems,
    )

    @pl.when(step == 0)
    def _():
        for copy in copies:
            copy.start()
        left[...] = prologue(wholes, full_outs)

    for place, group in enumerate(WAITS):

        @pl.when(step == place)
        def _():
            for index in group:
                copies[index].wait()

    result = jnp.dot(left[...], weights[step], preferred_element_type=F32)
    epilogue(result, wholes, blocks, block_outs)


def forward_product(clock, pieces, first, width, wholes, blocks, full_outs, block_outs, prologue, epilogue):
    depth = pieces[0].shape[0]
    frames = wholes[0].shape[0]
    turned = lambda step, spots: (0, spots[step])
    fixed = lambda step, spots: (0, 0)
    in_specs = [pl.BlockSpec(item.shape, fixed, pipeline_mode=pl.Buffered(1)) for item in wholes]
    in_specs += [pl.BlockSpec((frames, columns), turned) for _, columns in blocks]
    in_specs += [pl.BlockSpec(memory_space=pl.ANY)] * PIECES
    out_shape = [jax.ShapeDtypeStruct(shape, kind) for shape, kind in full_outs]
    out_shape += [
        jax.ShapeDtypeStruct((frames, SLICES * columns), kind) for kind, columns in block_outs
    ]
    out_specs = [pl.BlockSpec(shape, fixed) for shape, _ in full_outs]
    out_specs += [pl.BlockSpec((frames, columns), turned) for _, columns in block_outs]
    moved = sum(size_of(item) for item in wholes) + sum(size_of(item) for item, _ in blocks)
    moved += sum(size_of(item) for item in out_shape) + depth * width * SLICES * 2
    outs = pl.pallas_call(
        functools.partial(
            forward_kernel,
            first,
            width,
            (len(wholes), len(blocks), len(full_outs), len(block_outs)),
            prologue,
            epilogue,
        ),
        out_shape=out_shape,
        grid_spec=pltpu.PrefetchScalarGridSpec(
            num_scalar_prefetch=1,
            grid=(SLICES,),
            in_specs=in_specs,
            out_specs=out_specs,
            scratch_shapes=[
                pltpu.VMEM((frames, depth), BF16),
                pltpu.VMEM((SLICES, depth, width), BF16),
                pltpu.SemaphoreType.DMA((PIECES,)),
            ],
        ),
        compiler_params=pltpu.CompilerParams(
            dimension_semantics=("arbitrary",), vmem_limit_bytes=VMEM_LIMIT
        ),
        cost_estimate=cost_of(2 * frames * depth * width * SLICES, moved),
    )(clock.spots, *wholes, *[item for item, _ in blocks], *pieces)
    return clock(*outs)


def normed_prologue(wholes, full_outs):
    value, gain = wholes[:2]
    normed = normalize(value[...].astype(F32), gain[...])[0].astype(BF16)
    full_outs[0][...] = normed
    return normed


def plain_prologue(wholes, full_outs):
    return wholes[0][...]


def up_epilogue(result, wholes, blocks, outs):
    inner, acted = outs
    inner[...] = result.astype(BF16)
    acted[...] = (result * sigmoid(result)).astype(BF16)


def up(value, gain, pieces, clock):
    frames, width = value.shape
    columns = pieces[0].shape[1]
    return forward_product(
        clock,
        pieces,
        0,
        columns,
        [value, gain],
        [],
        [((frames, width), BF16)],
        [(BF16, columns), (BF16, columns)],
        normed_prologue,
        up_epilogue,
    )


def add_epilogue(scale, result, wholes, blocks, outs):
    outs[0][...] = blocks[0][...].astype(F32) + scale * result


def added(left, value, scale, pieces, first, columns, clock):
    return forward_product(
        clock,
        pieces,
        first,
        columns,
        [left],
        [(value, columns)],
        [],
        [(F32, columns)],
        plain_prologue,
        functools.partial(add_epilogue, scale),
    )[0]


def attend_epilogue(result, wholes, blocks, outs):
    cosine, sine = wholes[2][...], wholes[3][...]
    columns = result.shape[1] // 3
    scale = HEAD_DIM ** (-0.5)
    outs[0][...] = (rotate(result[:, :columns], cosine, sine) * scale).astype(BF16)
    outs[1][...] = rotate(result[:, columns : 2 * columns], cosine, sine).astype(BF16)
    outs[2][...] = result[:, 2 * columns :].astype(BF16)


def attend_front(value, gain, cosine, sine, pieces, columns, clock):
    return forward_product(
        clock,
        pieces,
        0,
        3 * columns,
        [value, gain, cosine, sine],
        [],
        [(value.shape, BF16)],
        [(BF16, columns)] * 3,
        normed_prologue,
        attend_epilogue,
    )


def store_epilogue(result, wholes, blocks, outs):
    outs[0][...] = result.astype(outs[0].dtype)


def expanded(value, gain, pieces, first, columns, clock):
    return forward_product(
        clock,
        pieces,
        first,
        columns,
        [value, gain],
        [],
        [(value.shape, BF16)],
        [(F32, columns)],
        normed_prologue,
        store_epilogue,
    )


def backward_kernel(first, widths, counts, chunk, epilogue, spots, *refs):
    left_count, whole_count, block_count, full_out_count, block_out_count = counts
    refs = list(refs)

    def take(number):
        taken = refs[:number]
        del refs[:number]
        return taken

    lefts = take(left_count)
    wholes = take(whole_count)
    blocks = take(block_count)
    pieces = take(PIECES)
    full_outs = take(full_out_count)
    block_outs = take(block_out_count)
    left, weights, sems = refs
    step = pl.program_id(0)
    width = sum(widths)

    @pl.when(step == 0)
    def _():
        copies = loads(
            spots,
            pieces,
            first,
            width,
            lambda place, start, extent: weights.at[
                pl.ds(start, extent), pl.ds(place * width, width)
            ],
            sems,
        )
        for copy in copies:
            copy.start()
        for place in range(SLICES):
            offset = place * width
            for item, columns in zip(lefts, widths):
                start = pl.multiple_of(spots[place] * columns, 128)
                left[:, pl.ds(offset, columns)] = item[:, pl.ds(start, columns)]
                offset += columns
        for copy in copies:
            copy.wait()

    rows = weights[pl.ds(pl.multiple_of(step * chunk, 16), chunk), :]
    result = lax.dot_general(
        left[...], rows, (((1,), (1,)), ((), ())), preferred_element_type=F32
    )
    epilogue(spots, result, wholes, blocks, full_outs, block_outs)


def backward_product(clock, pieces, first, lefts, wholes, blocks, chunk, full_outs, block_outs, epilogue):
    rows = pieces[0].shape[0]
    frames = lefts[0].shape[0]
    widths = tuple(item.shape[1] // SLICES for item in lefts)
    width = sum(widths)
    fixed = lambda step, spots: (0, 0)
    along = lambda step, spots: (0, step)
    in_specs = [
        pl.BlockSpec(item.shape, fixed, pipeline_mode=pl.Buffered(1)) for item in lefts + wholes
    ]
    in_specs += [pl.BlockSpec((frames, chunk), along) for _ in blocks]
    in_specs += [pl.BlockSpec(memory_space=pl.ANY)] * PIECES
    out_shape = [jax.ShapeDtypeStruct(shape, kind) for shape, kind in full_outs]
    out_shape += [jax.ShapeDtypeStruct((frames, rows), kind) for kind in block_outs]
    out_specs = [pl.BlockSpec(shape, fixed) for shape, _ in full_outs]
    out_specs += [pl.BlockSpec((frames, chunk), along) for _ in block_outs]
    moved = sum(size_of(item) for item in lefts + wholes + blocks)
    moved += sum(size_of(item) for item in out_shape) + rows * width * SLICES * 2
    outs = pl.pallas_call(
        functools.partial(
            backward_kernel,
            first,
            widths,
            (len(lefts), len(wholes), len(blocks), len(full_outs), len(block_outs)),
            chunk,
            epilogue,
        ),
        out_shape=out_shape,
        grid_spec=pltpu.PrefetchScalarGridSpec(
            num_scalar_prefetch=1,
            grid=(rows // chunk,),
            in_specs=in_specs,
            out_specs=out_specs,
            scratch_shapes=[
                pltpu.VMEM((frames, SLICES * width), BF16),
                pltpu.VMEM((rows, SLICES * width), BF16),
                pltpu.SemaphoreType.DMA((PIECES,)),
            ],
        ),
        compiler_params=pltpu.CompilerParams(
            dimension_semantics=("arbitrary",), vmem_limit_bytes=VMEM_MOST
        ),
        cost_estimate=cost_of(2 * frames * rows * width * SLICES, moved),
    )(clock.spots, *lefts, *wholes, *blocks, *pieces)
    return clock(*outs)


def slope_epilogue(spots, result, wholes, blocks, full_outs, block_outs):
    grad = (result * swish_slope(blocks[0][...].astype(F32))).astype(BF16)
    block_outs[0][...] = grad
    parts = len(full_outs) // 2
    for index, out in enumerate(full_outs):
        columns = out.shape[1]
        start = (index % parts) * columns

        @pl.when(pl.program_id(0) == spots[(1, 3)[index // parts]])
        def _():
            out[...] = grad[:, start : start + columns]


def down_back(outer, inner, pieces, parts, clock):
    frames, depth = inner.shape
    columns = depth // SLICES
    part = ((frames, columns // parts), BF16)
    *sent, grad = backward_product(
        clock, pieces, 0, [outer], [], [inner], columns, [part] * (2 * parts), [BF16], slope_epilogue
    )
    return grad, sent


def send_slices(spots, source, sent):
    columns = source.shape[1] // SLICES
    for offset, place in ((0, 1), (columns, 3)):
        start = pl.multiple_of(spots[place] * columns, 128)
        sent[:, pl.ds(offset, columns)] = source[:, pl.ds(start, columns)]


def norm_back_store(scale, spots, result, value, gain, upstream, outs):
    _, scaled, inverse = normalize(value[...].astype(F32), 1.0)
    delta, gain_grad = normalize_back(result, scaled, inverse, gain[...])
    grad = upstream[...] + delta
    outs[0][...] = grad
    outs[1][...] = gain_grad
    outs[2][...] = (scale * grad).astype(BF16)
    send_slices(spots, outs[2], outs[3])


def norm_epilogue(scale, spots, result, wholes, blocks, full_outs, block_outs):
    norm_back_store(scale, spots, result, wholes[0], wholes[1], wholes[2], full_outs)


def norm_back_product(lefts, value, gain, upstream, pieces, first, scale, clock):
    frames, width = upstream.shape
    return backward_product(
        clock,
        pieces,
        first,
        lefts,
        [value, gain, upstream],
        [],
        width,
        [
            ((frames, width), F32),
            ((1, width), F32),
            ((frames, width), BF16),
            ((frames, width // 2), BF16),
        ],
        [],
        functools.partial(norm_epilogue, scale),
    )


def plain_epilogue(spots, result, wholes, blocks, full_outs, block_outs):
    block_outs[0][...] = result.astype(block_outs[0].dtype)


def plain_back(left, kind, pieces, first, clock):
    return backward_product(
        clock, pieces, first, [left], [], [], pieces[0].shape[0], [], [kind], plain_epilogue
    )[0]


def up_back_kernel(scale, spots, left, value, gain, upstream, *refs):
    pieces = refs[:PIECES]
    out, gain_out, low_out, sent, total, weights, sems = refs[PIECES:]
    step = pl.program_id(0)
    width = weights.shape[2]
    copies = loads(
        spots,
        pieces,
        0,
        width,
        lambda place, start, extent: weights.at[place, pl.ds(start, extent), :],
        sems,
    )

    @pl.when(step == 0)
    def _():
        for copy in copies:
            copy.start()

    for place, group in enumerate(WAITS):

        @pl.when(step == place)
        def _():
            for index in group:
                copies[index].wait()

    result = lax.dot_general(
        left[...], weights[step], (((1,), (1,)), ((), ())), preferred_element_type=F32
    )

    @pl.when(step == 0)
    def _():
        total[...] = result

    @pl.when(step > 0)
    def _():
        total[...] += result

    @pl.when(step == SLICES - 1)
    def _():
        norm_back_store(
            scale, spots, total[...], value, gain, upstream, (out, gain_out, low_out, sent)
        )


def up_back(left, value, gain, upstream, pieces, scale, clock):
    frames, width = upstream.shape
    columns = pieces[0].shape[1]
    fixed = lambda step, spots: (0, 0)
    single = functools.partial(pl.BlockSpec, index_map=fixed, pipeline_mode=pl.Buffered(1))
    moved = size_of(left) + size_of(value) + 2 * size_of(upstream) + width * columns * 8
    outs = pl.pallas_call(
        functools.partial(up_back_kernel, scale),
        out_shape=[
            jax.ShapeDtypeStruct((frames, width), F32),
            jax.ShapeDtypeStruct((1, width), F32),
            jax.ShapeDtypeStruct((frames, width), BF16),
            jax.ShapeDtypeStruct((frames, width // 2), BF16),
        ],
        grid_spec=pltpu.PrefetchScalarGridSpec(
            num_scalar_prefetch=1,
            grid=(SLICES,),
            in_specs=[
                pl.BlockSpec((frames, columns), lambda step, spots: (0, spots[step])),
                single(value.shape),
                single(gain.shape),
                single(upstream.shape),
            ]
            + [pl.BlockSpec(memory_space=pl.ANY)] * PIECES,
            out_specs=[
                pl.BlockSpec((frames, width), fixed),
                pl.BlockSpec((1, width), fixed),
                pl.BlockSpec((frames, width), fixed),
                pl.BlockSpec((frames, width // 2), fixed),
            ],
            scratch_shapes=[
                pltpu.VMEM((frames, width), F32),
                pltpu.VMEM((SLICES, width, columns), BF16),
                pltpu.SemaphoreType.DMA((PIECES,)),
            ],
        ),
        compiler_params=pltpu.CompilerParams(
            dimension_semantics=("arbitrary",), vmem_limit_bytes=VMEM_MOST
        ),
        cost_estimate=cost_of(2 * frames * width * columns * SLICES, moved),
    )(clock.spots, left, value, gain, upstream, *pieces)
    return clock(*outs)


def weight_kernel(count, spots, mine, paired, *refs):
    ups, (far, own) = refs[: 4 * count], refs[-2:]
    dims = (((0,), (0,)), ((), ()))
    offset = 0
    for index in range(count):
        near_own, pair_own, near_far, pair_far = ups[4 * index : 4 * index + 4]
        columns = near_own.shape[1]
        for out, first, second in ((far, near_far, pair_far), (own, near_own, pair_own)):
            result = lax.dot_general(mine[...], first[...], dims, preferred_element_type=F32)
            result += lax.dot_general(paired[...], second[...], dims, preferred_element_type=F32)
            out[:, offset : offset + columns] = result.astype(out.dtype)
        offset += columns


def in_parts(near, sent):
    parts = len(sent) // 2
    return [
        (near, parts * SLICES, part, (sent[part], 0), (sent[parts + part], 0))
        for part in range(parts)
    ]


def packed_pair(near, sent):
    return (near, SLICES, 0, (sent, 0), (sent, 1))


def weight_grads(left, ups, chunk, clock, first=0, depth=None, packed=None, place=0, base=None):
    rows = left[0] if isinstance(left, tuple) else left
    frames = ups[0][0].shape[0]
    depth = depth or rows.shape[1]
    skipped = first // chunk
    in_specs = []
    operands = []
    for core in range(2):
        if isinstance(left, tuple):
            operands.append(left[core])
            index = lambda step, spots: (0, step + skipped)
        else:
            operands.append(left)
            index = lambda step, spots, core=core: (spots[5 + core], step + skipped)
        in_specs.append(pl.BlockSpec((frames, chunk), index))
    widths = []
    for near, parts, part, *beside in ups:
        columns = near.shape[1] // parts
        for which, (item, block) in zip((0, 2), beside):
            operands += [near, item]
            stride = parts // SLICES
            mine = lambda step, spots, which=which, part=part, stride=stride: (
                0,
                spots[which] * stride + part,
            )
            theirs = lambda step, spots, block=block: (0, block)
            in_specs += [pl.BlockSpec((frames, columns), index) for index in (mine, theirs)]
        widths.append(columns)
    total = sum(widths)
    down = lambda step, spots: (step, place)
    count = len(operands)
    if base is not None:
        operands += base
        in_specs += [pl.BlockSpec(memory_space=pl.ANY)] * 2
    outs = pl.pallas_call(
        functools.partial(weight_kernel, len(ups)),
        input_output_aliases={} if base is None else {1 + count: 0, 2 + count: 1},
        out_shape=[jax.ShapeDtypeStruct((depth, packed or total), BF16)] * 2,
        grid_spec=pltpu.PrefetchScalarGridSpec(
            num_scalar_prefetch=1,
            grid=(depth // chunk,),
            in_specs=in_specs,
            out_specs=[pl.BlockSpec((chunk, total), down)] * 2,
        ),
        compiler_params=pltpu.CompilerParams(
            dimension_semantics=("arbitrary",), vmem_limit_bytes=VMEM_MOST
        ),
        cost_estimate=cost_of(
            8 * frames * depth * total, 4 * frames * depth + 8 * frames * total + 4 * depth * total
        ),
    )(clock.spots, *operands)
    return clock(*outs)


def attention_kernel(query, keys, values, across, along, mixed, summary):
    head = pl.program_id(0)
    scores = lax.dot_general(
        query[...], keys[...], (((1,), (1,)), ((), ())), preferred_element_type=F32
    )
    scores = jnp.where(across[...] == along[...], scores, MASKED)
    highest = jnp.max(scores, axis=-1, keepdims=True)
    raised = jnp.exp(scores - highest)
    totals = jnp.sum(raised, axis=-1, keepdims=True)
    probs = (raised * (1.0 / totals)).astype(BF16)
    mixed[...] = jnp.dot(probs, values[...], preferred_element_type=F32).astype(BF16)
    lane = lax.broadcasted_iota(jnp.int32, summary.shape, 1)
    kept = jnp.where(head == 0, jnp.zeros_like(summary), summary[...])
    summary[...] = jnp.where(lane == head, highest + jnp.log(totals), kept)


def attention(query, keys, values, across, along, clock):
    (query,) = clock(query)
    frames, width = query.shape
    head_block = pl.BlockSpec((frames, HEAD_DIM), lambda head: (0, head))
    fixed = lambda head: (0, 0)
    outs = pl.pallas_call(
        attention_kernel,
        out_shape=[
            jax.ShapeDtypeStruct((frames, width), BF16),
            jax.ShapeDtypeStruct((frames, HEAD_DIM), F32),
        ],
        grid=(width // HEAD_DIM,),
        in_specs=[head_block] * 3
        + [pl.BlockSpec((frames, 1), fixed), pl.BlockSpec((1, frames), fixed)],
        out_specs=[head_block, pl.BlockSpec((frames, HEAD_DIM), fixed)],
        compiler_params=pltpu.CompilerParams(
            dimension_semantics=("arbitrary",), vmem_limit_bytes=VMEM_LIMIT
        ),
        cost_estimate=cost_of(4 * frames * frames * width, 8 * frames * width),
    )(query, keys, values, across, along)
    return clock(*outs)


def attention_back_kernel(
    spots, query, keys, values, upstream, summary, across, along, cosine, sine, *outs
):
    head = pl.program_id(0)
    at = pl.ds(pl.multiple_of(head * HEAD_DIM, HEAD_DIM), HEAD_DIM)
    query_out, keys_out, values_out = outs[:3]
    contract_last = (((1,), (1,)), ((), ()))
    contract_first = (((0,), (0,)), ((), ()))
    scores = lax.dot_general(query[...], keys[...], contract_last, preferred_element_type=F32)
    scores = jnp.where(across[...] == along[...], scores, MASKED)
    lane = lax.broadcasted_iota(jnp.int32, summary.shape, 1)
    level = jnp.sum(jnp.where(lane == head, summary[...], 0.0), axis=-1, keepdims=True)
    probs = jnp.exp(scores - level)
    grads = lax.dot_general(upstream[...], values[...], contract_last, preferred_element_type=F32)
    balance = jnp.sum(probs * grads, axis=-1, keepdims=True)
    scores_grad = (probs * (grads - balance)).astype(BF16)
    values_out[:, at] = lax.dot_general(
        probs.astype(BF16), upstream[...], contract_first, preferred_element_type=F32
    ).astype(BF16)
    scale = HEAD_DIM ** (-0.5)
    query_back = jnp.dot(scores_grad, keys[...], preferred_element_type=F32)
    query_out[:, at] = (rotate(query_back, cosine[...], -sine[...]) * scale).astype(BF16)
    keys_back = lax.dot_general(scores_grad, query[...], contract_first, preferred_element_type=F32)
    keys_out[:, at] = rotate(keys_back, cosine[...], -sine[...]).astype(BF16)

    @pl.when(head == pl.num_programs(0) - 1)
    def _():
        for out, sent in zip(outs[:3], outs[3:]):
            send_slices(spots, out, sent)


def attention_back(query, keys, values, upstream, summary, across, along, cosine, sine, clock):
    frames, width = query.shape
    head_block = pl.BlockSpec((frames, HEAD_DIM), lambda head, spots: (0, head))
    fixed = lambda head, spots: (0, 0)
    whole = pl.BlockSpec((frames, HEAD_DIM), fixed)
    outs = pl.pallas_call(
        attention_back_kernel,
        out_shape=[jax.ShapeDtypeStruct((frames, width), BF16)] * 3
        + [jax.ShapeDtypeStruct((frames, width // 2), BF16)] * 3,
        grid_spec=pltpu.PrefetchScalarGridSpec(
            num_scalar_prefetch=1,
            grid=(width // HEAD_DIM,),
            in_specs=[head_block] * 4
            + [
                whole,
                pl.BlockSpec((frames, 1), fixed),
                pl.BlockSpec((1, frames), fixed),
                whole,
                whole,
            ],
            out_specs=[pl.BlockSpec((frames, width), fixed)] * 3
            + [pl.BlockSpec((frames, width // 2), fixed)] * 3,
        ),
        compiler_params=pltpu.CompilerParams(
            dimension_semantics=("arbitrary",), vmem_limit_bytes=VMEM_MOST
        ),
        cost_estimate=cost_of(10 * frames * frames * width, 14 * frames * width),
    )(clock.spots, query, keys, values, upstream, summary, across, along, cosine, sine)
    outs = clock(*outs)
    return outs[:3], outs[3:]


def bare_call(kernel, outs, operands, clock, flops=0):
    fixed = lambda spots: (0, 0)
    results = pl.pallas_call(
        kernel,
        out_shape=[jax.ShapeDtypeStruct(shape, kind) for shape, kind in outs],
        grid_spec=pltpu.PrefetchScalarGridSpec(
            num_scalar_prefetch=1,
            grid=(),
            in_specs=[
                pl.BlockSpec(item.shape, lambda spots, item=item: (0,) * item.ndim)
                for item in operands
            ],
            out_specs=[pl.BlockSpec(shape, fixed) for shape, _ in outs],
        ),
        compiler_params=pltpu.CompilerParams(vmem_limit_bytes=VMEM_MOST),
        cost_estimate=cost_of(flops, sum(size_of(item) for item in operands)),
    )(clock.spots, *operands)
    return clock(*results)


def final_kernel(spots, value, gain, valid, cotangent, out, grad_out, gain_out, low_out, sent):
    normed, scaled, inverse = normalize(value[...], gain[...])
    out[...] = (normed * valid[...]).astype(BF16)
    upstream = cotangent[...].astype(F32) * valid[...]
    grad, gain_grad = normalize_back(upstream, scaled, inverse, gain[...])
    grad_out[...] = grad
    gain_out[...] = gain_grad
    low_out[...] = (0.5 * grad).astype(BF16)
    send_slices(spots, low_out, sent)


def final(value, gain, valid, cotangent, clock):
    shape = value.shape
    return bare_call(
        final_kernel,
        [
            (shape, BF16),
            (shape, F32),
            (gain.shape, F32),
            (shape, BF16),
            ((shape[0], shape[1] // 2), BF16),
        ],
        [value, gain, valid, cotangent],
        clock,
    )


TAPS = 5
REACH = 2
CONV_BLOCK = 256


def convolve_kernel(spots, values, gates, taps, same, valid, mixed, shares):
    glued = values[...] * sigmoid(gates[...])
    frames = glued.shape[0]
    result = jnp.zeros_like(glued)
    for index in range(TAPS):
        moved = pltpu.roll(glued, (REACH - index) % frames, 0) if index != REACH else glued
        result += taps[index : index + 1, :] * moved * same[:, index : index + 1]
    mixed[...] = result
    counted = jnp.maximum(jnp.sum(valid[...]), 1.0)
    local_sum = jnp.sum(result * valid[...], axis=0, keepdims=True)
    spread = (result - local_sum / counted) * valid[...]
    shares[0:1, :] = local_sum
    shares[1:2, :] = jnp.sum(spread * spread, axis=0, keepdims=True)


def convolve(expand, taps, same, valid, clock):
    frames, width = expand.shape[0], expand.shape[1] // 2
    blocks = width // CONV_BLOCK
    along = lambda step, spots: (0, step)
    fixed = lambda step, spots: (0, 0)
    outs = pl.pallas_call(
        convolve_kernel,
        out_shape=[
            jax.ShapeDtypeStruct((frames, width), F32),
            jax.ShapeDtypeStruct((2, width), F32),
        ],
        grid_spec=pltpu.PrefetchScalarGridSpec(
            num_scalar_prefetch=1,
            grid=(blocks,),
            in_specs=[
                pl.BlockSpec((frames, CONV_BLOCK), along),
                pl.BlockSpec((frames, CONV_BLOCK), lambda step, spots: (0, step + blocks)),
                pl.BlockSpec((TAPS, CONV_BLOCK), along),
                pl.BlockSpec(same.shape, fixed),
                pl.BlockSpec(valid.shape, fixed),
            ],
            out_specs=[
                pl.BlockSpec((frames, CONV_BLOCK), along),
                pl.BlockSpec((2, CONV_BLOCK), along),
            ],
        ),
        compiler_params=pltpu.CompilerParams(
            dimension_semantics=("arbitrary",), vmem_limit_bytes=VMEM_LIMIT
        ),
        cost_estimate=cost_of(0, size_of(expand)),
    )(clock.spots, expand, expand, taps, same, valid)
    return clock(*outs)


def batch_prologue(wholes, full_outs):
    mixed, mean, inverse, gain, shift = (item[...] for item in wholes)
    normal = (mixed - mean) * inverse * gain + shift
    acted = (normal * sigmoid(normal)).astype(BF16)
    full_outs[0][...] = acted
    return acted


def projected(mixed, mean, inverse, gain, shift, value, pieces, first, columns, clock):
    return forward_product(
        clock,
        pieces,
        first,
        columns,
        [mixed, mean, inverse, gain, shift],
        [(value, columns)],
        [(mixed.shape, BF16)],
        [(F32, columns)],
        batch_prologue,
        functools.partial(add_epilogue, 1.0),
    )


def project_epilogue(spots, result, wholes, blocks, full_outs, block_outs):
    mixed, mean, inverse, gain, shift, valid = (item[...] for item in wholes)
    standard = (mixed - mean) * inverse
    grad = result * swish_slope(standard * gain + shift)
    full_outs[0][...] = grad
    counted = grad * valid
    full_outs[1][0:1, :] = jnp.sum(counted, axis=0, keepdims=True)
    full_outs[1][1:2, :] = jnp.sum(counted * standard, axis=0, keepdims=True)


def project_back(outer, mixed, mean, inverse, gain, shift, valid, pieces, first, clock):
    frames, width = mixed.shape
    return backward_product(
        clock,
        pieces,
        first,
        [outer],
        [mixed, mean, inverse, gain, shift, valid],
        [],
        width,
        [((frames, width), F32), ((2, width), F32)],
        [],
        project_epilogue,
    )


def convolve_back_kernel(
    spots, grad, mixed, values, gates, taps, same, valid, sums, mean, inverse, gain, count, out, taps_out, *sent
):
    step = pl.program_id(0)
    frames, columns = grad.shape
    width = out.shape[1] // 2
    standard = (mixed[...] - mean[...]) * inverse[...]
    share = (sums[0:1, :] + standard * sums[1:2, :]) / count[...]
    upstream = gain[...] * inverse[...] * (grad[...] - valid[...] * share)
    gate = sigmoid(gates[...])
    glued = values[...] * gate
    back = jnp.zeros_like(upstream)
    for index in range(TAPS):
        term = upstream * same[:, index : index + 1]
        if index == REACH:
            moved, returned = glued, term
        else:
            moved = pltpu.roll(glued, (REACH - index) % frames, 0)
            returned = pltpu.roll(term, (index - REACH) % frames, 0)
        taps_out[index : index + 1, :] = jnp.sum(term * moved, axis=0, keepdims=True)
        back += taps[index : index + 1, :] * returned
    low = pl.multiple_of(step * columns, 128)
    high = pl.multiple_of(width + step * columns, 128)
    out[:, pl.ds(low, columns)] = (back * gate).astype(BF16)
    out[:, pl.ds(high, columns)] = (back * glued * (1.0 - gate)).astype(BF16)

    @pl.when(step == pl.num_programs(0) - 1)
    def _():
        for part, place in zip(sent, (1, 3)):
            start = pl.multiple_of(spots[place] * part.shape[1], 128)
            part[...] = out[:, pl.ds(start, part.shape[1])]


def convolve_back(grad, mixed, expand, taps, same, valid, sums, mean, inverse, gain, count, clock):
    frames, width = mixed.shape
    blocks = width // CONV_BLOCK
    along = lambda step, spots: (0, step)
    fixed = lambda step, spots: (0, 0)
    wide = pl.BlockSpec((frames, CONV_BLOCK), along)
    row = pl.BlockSpec((1, CONV_BLOCK), along)
    outs = pl.pallas_call(
        convolve_back_kernel,
        out_shape=[
            jax.ShapeDtypeStruct((frames, 2 * width), BF16),
            jax.ShapeDtypeStruct((TAPS, width), F32),
        ]
        + [jax.ShapeDtypeStruct((frames, width // 2), BF16)] * 2,
        grid_spec=pltpu.PrefetchScalarGridSpec(
            num_scalar_prefetch=1,
            grid=(blocks,),
            in_specs=[
                wide,
                wide,
                wide,
                pl.BlockSpec((frames, CONV_BLOCK), lambda step, spots: (0, step + blocks)),
                pl.BlockSpec((TAPS, CONV_BLOCK), along),
                pl.BlockSpec(same.shape, fixed),
                pl.BlockSpec(valid.shape, fixed),
                pl.BlockSpec((2, CONV_BLOCK), along),
                row,
                row,
                row,
                pl.BlockSpec((1, 1), fixed),
            ],
            out_specs=[
                pl.BlockSpec((frames, 2 * width), fixed),
                pl.BlockSpec((TAPS, CONV_BLOCK), along),
            ]
            + [pl.BlockSpec((frames, width // 2), fixed)] * 2,
        ),
        compiler_params=pltpu.CompilerParams(
            dimension_semantics=("arbitrary",), vmem_limit_bytes=VMEM_MOST
        ),
        cost_estimate=cost_of(0, size_of(expand) * 2),
    )(clock.spots, grad, mixed, expand, expand, taps, same, valid, sums, mean, inverse, gain, count)
    return clock(*outs)


def folds_kernel(kinds, spots, *refs):
    refs = list(refs)

    def take(number):
        taken = refs[:number]
        del refs[:number]
        return taken

    inputs = [take(FOLD_INPUTS[kind]) for kind in kinds]
    for kind, items in zip(kinds, inputs):
        if kind == "blocks":
            (blocks,) = items
            (out,) = take(1)
            total = blocks[0].astype(F32)
            for index in range(1, blocks.shape[0]):
                total += blocks[index].astype(F32)
            out[...] = total.astype(BF16)
        else:
            for first in range(0, len(items), 2):
                (out,) = take(1)
                total = items[first][...].astype(F32) + items[first + 1][...].astype(F32)
                out[...] = total.astype(out.dtype)


FOLD_INPUTS = {"split": 4, "sum": 2, "blocks": 1}


def folds(items, clock):
    steps = 2
    for kind, operands in items:
        rows = operands[-1].shape[-2] // (2 if kind == "split" else 1)
        if rows % 32:
            steps = 1
    operands, in_specs, out_specs, out_shape = [], [], [], []

    def put(item, block, index):
        operands.append(item)
        in_specs.append(pl.BlockSpec(block, index))

    def give(shape, kind):
        out_shape.append(jax.ShapeDtypeStruct(shape, kind))
        block = (shape[0] // steps, shape[1])
        out_specs.append(pl.BlockSpec(block, lambda step, spots: (step, 0)))

    for kind, (*value, moving) in items:
        rows, columns = moving.shape[-2:]
        if kind == "split":
            block = (rows // 2 // steps, columns)
            kept = lambda step, spots: (spots[BITS] * steps + step, 0)
            sent = lambda step, spots: ((1 - spots[BITS]) * steps + step, 0)
            for index in (kept, sent):
                put(value[0], block, index)
                put(moving, block, index)
            give((rows // 2, columns), F32)
            give((rows // 2, columns), BF16)
        elif kind == "sum":
            for item in (value[0], moving):
                put(item, (rows // steps, columns), lambda step, spots: (step, 0))
            give((rows, columns), BF16)
        else:
            block = (moving.shape[0], rows // steps, columns)
            put(moving, block, lambda step, spots: (0, step, 0))
            give((rows, columns), BF16)
    outs = pl.pallas_call(
        functools.partial(folds_kernel, tuple(kind for kind, _ in items)),
        out_shape=out_shape,
        grid_spec=pltpu.PrefetchScalarGridSpec(
            num_scalar_prefetch=1,
            grid=(steps,),
            in_specs=in_specs,
            out_specs=out_specs,
        ),
        compiler_params=pltpu.CompilerParams(
            dimension_semantics=("arbitrary",), vmem_limit_bytes=VMEM_MOST
        ),
        cost_estimate=cost_of(0, sum(size_of(item) for item in operands)),
    )(clock.spots, *operands)
    return list(clock(*outs))


def unfold_kernel(widths, size, spots, value, *outs):
    step = pl.program_id(0)
    block = value.shape[0] // size
    for item in range(size // 2):
        place = 2 * item + step
        rows = value[pl.ds(pl.multiple_of(place * block, 16), block), :].astype(F32)
        offset = 0
        for out, width in zip(outs, widths):
            out[item * block : (item + 1) * block, :] = rows[:, offset : offset + width]
            offset += width


def unfold(value, size, widths, clock):
    rows, columns = value.shape
    outs = pl.pallas_call(
        functools.partial(unfold_kernel, widths, size),
        out_shape=[jax.ShapeDtypeStruct((rows, width), F32) for width in widths],
        grid_spec=pltpu.PrefetchScalarGridSpec(
            num_scalar_prefetch=1,
            grid=(2,),
            in_specs=[pl.BlockSpec((rows, columns), lambda step, spots: (0, 0))],
            out_specs=[
                pl.BlockSpec((rows // 2, width), lambda step, spots: (step, 0))
                for width in widths
            ],
        ),
        compiler_params=pltpu.CompilerParams(
            dimension_semantics=("arbitrary",), vmem_limit_bytes=VMEM_MOST
        ),
        cost_estimate=cost_of(0, size_of(value)),
    )(clock.spots, value)
    return clock(*outs)


class Clock:
    def __init__(self, spots):
        self.spots = spots

    def __call__(self, *values):
        self.spots, *values = lax.optimization_barrier((self.spots,) + values)
        return values

    def send(self, value, axis, mask):
        (value,) = self(value)
        return swapped(value, axis, mask)


class Gather:
    def __init__(self, slices, clock):
        self.own = slices[0] if len(slices) == 1 else jnp.concatenate(slices, axis=1)
        self.half = self.own.shape[0] // 2
        self.clock = clock
        self.crossing = lax.dynamic_slice_in_dim(
            self.own, half_sent() * self.half, self.half, axis=0
        )

    def cross(self):
        self.across = self.clock.send(self.crossing, "fsdp", 2)

    def beside(self):
        self.own_beside = joined(self.own)

    def forward(self):
        quarter = self.half // 2
        self.across, self.own_beside = self.clock(self.across, self.own_beside)
        self.first = swapped(self.across[:quarter], "dp", 1)
        self.second = swapped(self.across[quarter:], "dp", 2)
        self.across_beside = swapped(self.across, "fsdp", 1)

    def turn(self):
        self.first, self.second, self.across_beside = self.clock(
            self.first, self.second, self.across_beside
        )
        self.first_beside = swapped(self.first, "fsdp", 1)
        self.second_beside = swapped(self.second, "fsdp", 1)

    def finish(self):
        self.first_beside, self.second_beside = self.clock(
            self.first_beside, self.second_beside
        )
        self.pieces = (
            self.own,
            self.own_beside,
            self.across,
            self.first,
            self.second,
            self.across_beside,
            self.first_beside,
            self.second_beside,
        )


def half_sent():
    place = lax.axis_index("dp")
    return (place ^ (place >> 1)) & 1


class Reduction:
    def __init__(self, far, own, clock, wide=False):
        self.size = lax.axis_size("dp")
        self.clock = clock
        self.value = own
        self.sent = far
        self.stage = 0
        self.wide = wide
        self.moving = None
        self.whole = None

    def exchange(self, blocks):
        groups = [[i for i in range(self.size) if i % 2 == low] for low in range(2)]
        return lax.all_to_all(blocks, "dp", 0, 0, axis_index_groups=groups, tiled=True)

    def fold(self, moving):
        self.stage += 1
        if self.stage == 1:
            return "split", (self.value, moving)
        if self.stage == 2:
            return "sum", (self.value, moving)
        if self.stage == 3:
            return "blocks", (moving,)
        self.sent = moving.reshape(-1, moving.shape[2])
        return None

    def take(self, outs):
        if self.stage == 1:
            self.value = outs.pop(0)
        self.sent = outs.pop(0)
        if self.stage == 2:
            rows, columns = self.sent.shape
            members = self.size // 2
            self.sent = self.sent.reshape(members, rows // members, columns)

    def send(self, sent):
        if self.stage == 0:
            self.moving = swapped(sent, "fsdp", 2)
        elif self.stage == 1:
            self.moving = swapped(sent, "dp", 1)
        elif self.stage == 2:
            self.moving = self.exchange(sent)
        elif self.stage == 3 and self.wide:
            copies = (self.size // 2,) + sent.shape
            self.moving = self.exchange(jnp.broadcast_to(sent[None], copies))
        elif self.stage == 3:
            self.whole = lax.all_gather(sent, "dp", axis=0, tiled=True)
            self.moving = None
        else:
            self.value = sent
            self.moving = swapped(sent, "dp", 1)

    def ended(self):
        return self.whole is not None or self.stage == 4

    def result(self, widths=None):
        while not self.ended():
            turn(self.clock, self)
        if self.wide:
            (moving,) = self.clock(self.moving)
            return [
                jnp.where(
                    lax.axis_index("dp") & 1 == 0,
                    jnp.concatenate([self.value, moving], axis=0),
                    jnp.concatenate([moving, self.value], axis=0),
                ).astype(F32)
            ]
        (whole,) = self.clock(self.whole)
        return unfold(whole, self.size, widths or (whole.shape[1],), self.clock)


def turn(clock, *groups):
    groups = [group for group in groups if not group.ended()]
    waiting = [group for group in groups if group.moving is not None]
    fresh = [group for group in groups if group.moving is None]
    arrived = clock(*[group.moving for group in waiting], *[group.sent for group in fresh])
    for group, item in zip(fresh, arrived[len(waiting) :]):
        group.send(item)
    sums = [(group, group.fold(moving)) for group, moving in zip(waiting, arrived)]
    sums = [(group, item) for group, item in sums if item is not None]
    if sums:
        outs = folds([item for _, item in sums], clock)
        for group, _ in sums:
            group.take(outs)
    sent = clock(*[group.sent for group in waiting])
    for group, item in zip(waiting, sent):
        group.send(item)


def joined(value):
    groups = [[i, i + 1] for i in range(0, lax.axis_size("fsdp"), 2)]
    return lax.all_gather(value, "fsdp", axis=0, tiled=True, axis_index_groups=groups)


class Doubling:
    def __init__(self, value):
        self.sent = value
        self.moving = None
        self.left = [
            (axis, 1 << bit)
            for axis in ("fsdp", "dp")
            for bit in range(lax.axis_size(axis).bit_length() - 1)
        ]

    def fold(self, moving):
        self.sent = self.sent + moving

    def send(self, sent):
        self.sent = sent
        if self.left:
            axis, mask = self.left.pop(0)
            self.moving = swapped(sent, axis, mask)
        else:
            self.moving = None
            self.left = None

    def ended(self):
        return self.left is None

    def result(self, clock):
        while not self.ended():
            turn(clock, self)
        return self.sent


def swapped(value, axis, mask):
    size = lax.axis_size(axis)
    return lax.ppermute(value, axis, [(i, i ^ mask) for i in range(size)])


def spread_sum(rows):
    axes = ("dp", "fsdp")
    count = lax.axis_size(axes)
    copies = jnp.broadcast_to(rows[None], (count,) + rows.shape)
    return lax.all_to_all(copies, axes, 0, 0, tiled=True)


def neighbours(segment, taps):
    frames = segment.shape[0]
    reach = (taps - 1) // 2
    side = jnp.pad(segment, (reach, reach), constant_values=-1)
    columns = [side[index : index + frames] == segment for index in range(taps)]
    return jnp.pad(jnp.stack(columns, axis=1).astype(F32), ((0, 0), (0, 8 - taps)))


def body(
    frames_in,
    cotangent,
    lengths,
    first_gain,
    first_up,
    first_down,
    attend_gain,
    query_proj,
    key_proj,
    value_proj,
    output_proj,
    conv_gain,
    conv_expand,
    conv_kernel,
    batch_gain,
    batch_shift,
    conv_project,
    second_gain,
    second_up,
    second_down,
    final_gain,
):
    frames, width = frames_in.shape
    slot = lax.axis_index("fsdp")
    part = half_sent()
    row, rows = lax.axis_index("dp"), lax.axis_size("dp")
    bits = [(row >> which) & 1 for which in range(rows.bit_length() - 1)]
    spots = jnp.stack(
        [slot, slot ^ 1, slot ^ 2, slot ^ 3, part, slot & 1, 1 - (slot & 1)] + bits
    ).astype(jnp.int32)
    clock = Clock(spots)
    segment, position, valid = layout(lengths[0], frames)
    cosine, sine = rotation(position, HEAD_DIM // 2)
    column = valid[:, None]
    seg_across, seg_along = segment[:, None], segment[None, :]
    first_gain, attend_gain, conv_gain, second_gain, final_gain, batch_gain, batch_shift = (
        item[None]
        for item in (
            first_gain,
            attend_gain,
            conv_gain,
            second_gain,
            final_gain,
            batch_gain,
            batch_shift,
        )
    )
    same = neighbours(segment, conv_kernel.shape[0])
    narrow = query_proj.shape[1]
    wide = conv_expand.shape[1]

    def pair(value):
        return clock.send(value, "fsdp", 1)

    first_ups = Gather((first_up,), clock)
    first_ups.cross()
    first_ups.beside()
    first_downs = Gather((first_down,), clock)
    attends = Gather((query_proj, key_proj, value_proj), clock)
    convs = Gather((output_proj, conv_expand, conv_project), clock)
    second_ups = Gather((second_up,), clock)
    second_downs = Gather((second_down,), clock)
    later = (first_downs, attends, convs, second_ups, second_downs)
    for group, item in zip(later, clock(*[group.crossing for group in later])):
        group.crossing = item
        group.beside()
    first_ups.forward()
    first_downs.cross()
    attends.cross()
    first_ups.turn()
    first_ups.finish()
    first_normed, first_inner, first_acted = up(frames_in, first_gain, first_ups.pieces, clock)
    first_downs.forward()
    convs.cross()
    first_downs.turn()
    first_downs.finish()
    attends.forward()
    second_ups.cross()
    after_first = added(
        first_acted, frames_in, 0.5, first_downs.pieces, 0, first_down.shape[1], clock
    )
    attends.turn()
    attends.finish()
    attend_normed, query, keys, values = attend_front(
        after_first, attend_gain, cosine, sine, attends.pieces, narrow, clock
    )
    convs.forward()
    attended, summary = attention(query, keys, values, seg_across, seg_along, clock)
    convs.turn()
    convs.finish()
    after_attend = added(attended, after_first, 1.0, convs.pieces, 0, narrow, clock)
    conv_normed, expand = expanded(after_attend, conv_gain, convs.pieces, narrow, wide, clock)

    mixed, local = convolve(expand, conv_kernel, same, column, clock)
    local = jnp.concatenate([local, jnp.broadcast_to(jnp.sum(valid), (2, 128))], axis=1)
    shares = spread_sum(local)
    second_downs.cross()
    second_ups.forward()
    (shares,) = clock(shares)
    second_ups.turn()
    counts = shares[:, 0, width : width + 1]
    count = jnp.sum(counts)
    sums = shares[:, 0, :width]
    mean = jnp.sum(sums, axis=0) / count
    offsets = sums / jnp.maximum(counts, 1.0) - mean
    variance = jnp.sum(shares[:, 1, :width] + counts * offsets * offsets, axis=0) / count
    deviation_inverse = lax.rsqrt(variance + EPSILON)
    mean_row, inverse_row = mean[None], deviation_inverse[None]
    conv_acted, after_conv = projected(
        mixed,
        mean_row,
        inverse_row,
        batch_gain,
        batch_shift,
        after_attend,
        convs.pieces,
        narrow + wide,
        narrow,
        clock,
    )
    second_ups.finish()
    second_downs.forward()
    second_normed, second_inner, second_acted = up(
        after_conv, second_gain, second_ups.pieces, clock
    )
    second_downs.turn()
    second_downs.finish()
    pair_acted, pair_normed = pair(second_acted), pair(second_normed)
    after_second = added(
        second_acted, after_conv, 0.5, second_downs.pieces, 0, second_down.shape[1], clock
    )
    pair_acted, pair_normed = clock(pair_acted, pair_normed)
    layer_out, upstream, final_gain_grad, outer, sent = final(
        after_second, final_gain, column, cotangent, clock
    )
    (pair_outer,) = clock(pair(sent))
    both_conv_acted, both_conv, both_attended, both_attend, both_first_acted, both_first = (
        joined(item)
        for item in clock(
            conv_acted, conv_normed, attended, attend_normed, first_acted, first_normed
        )
    )

    second_down_sum = Reduction(
        *weight_grads((second_acted, pair_acted), [packed_pair(outer, pair_outer)], 1024, clock),
        clock,
    )
    turn(clock, second_down_sum)
    inner_grad, sent = down_back(outer, second_inner, second_downs.pieces, 2, clock)
    pair_inner = [pair(item) for item in sent]
    upstream, second_gain_grad, outer, sent = up_back(
        inner_grad, after_conv, second_gain, upstream, second_ups.pieces, 1.0, clock
    )
    pair_inner = clock(*pair_inner)
    pair_outer = pair(sent)
    normal_grad, local = project_back(
        outer,
        mixed,
        mean_row,
        inverse_row,
        batch_gain,
        batch_shift,
        column,
        convs.pieces,
        narrow + wide,
        clock,
    )
    (local,) = clock(local)
    pieces = spread_sum(local)
    second_up_sum = Reduction(
        *weight_grads((second_normed, pair_normed), in_parts(inner_grad, pair_inner), 512, clock),
        clock,
    )
    pair_outer, both_conv_acted = clock(pair_outer, both_conv_acted)
    conv_part = weight_grads(
        both_conv_acted,
        [packed_pair(outer, pair_outer)],
        512,
        clock,
        packed=wide + narrow,
        place=wide // narrow,
    )
    (pieces,) = clock(pieces)
    turn(clock, second_up_sum, second_down_sum)
    sums = jnp.sum(pieces, axis=0)
    expand_back, kernel_local, *sent = convolve_back(
        normal_grad,
        mixed,
        expand,
        conv_kernel,
        same,
        column,
        sums,
        mean_row,
        inverse_row,
        batch_gain,
        count.reshape(1, 1),
        clock,
    )
    pair_back = [pair(item) for item in sent]
    upstream, conv_gain_grad, outer, sent = norm_back_product(
        [expand_back], after_attend, conv_gain, upstream, convs.pieces, narrow, 1.0, clock
    )
    *pair_back, both_conv = clock(*pair_back, both_conv)
    pair_outer = pair(sent)
    conv_part = weight_grads(
        both_conv,
        [(expand_back, SLICES, 0, *((item, 0) for item in pair_back))],
        512,
        clock,
        packed=wide + narrow,
        base=conv_part,
    )
    conv_sum = Reduction(*conv_part, clock)
    mixed_back = plain_back(outer, BF16, convs.pieces, 0, clock)
    pair_outer, both_attended = clock(pair_outer, both_attended)
    turn(clock, conv_sum, second_up_sum, second_down_sum)
    backs, sent = attention_back(
        query, keys, values, mixed_back, summary, seg_across, seg_along, cosine, sine, clock
    )
    pair_backs = [pair(item) for item in sent]
    attend_part = weight_grads(
        both_attended, [packed_pair(outer, pair_outer)], 512, clock, packed=4 * narrow, place=3
    )
    *pair_backs, both_attend = clock(*pair_backs, both_attend)
    attend_part = weight_grads(
        both_attend,
        [packed_pair(item, other) for item, other in zip(backs, pair_backs)],
        512,
        clock,
        packed=4 * narrow,
        base=attend_part,
    )
    attend_sum = Reduction(*attend_part, clock)
    turn(clock, attend_sum, conv_sum, second_up_sum, second_down_sum)
    upstream, attend_gain_grad, outer, sent = norm_back_product(
        backs, after_first, attend_gain, upstream, attends.pieces, 0, 0.5, clock
    )
    (pair_outer,) = clock(pair(sent))
    (both_first_acted,) = clock(both_first_acted)
    first_down_sum = Reduction(
        *weight_grads(both_first_acted, [packed_pair(outer, pair_outer)], 1024, clock), clock
    )
    inner_grad, sent = down_back(outer, first_inner, first_downs.pieces, 1, clock)
    turn(clock, first_down_sum, attend_sum, conv_sum, second_up_sum)
    *pair_inner, both_first = clock(*[pair(item) for item in sent], both_first)
    first_up_sum = Reduction(
        *weight_grads(both_first, in_parts(inner_grad, pair_inner), 512, clock), clock, wide=True
    )
    turn(clock, first_up_sum)
    upstream, first_gain_grad, _, _ = up_back(
        inner_grad, frames_in, first_gain, upstream, first_ups.pieces, 1.0, clock
    )
    minor = jnp.concatenate(
        [
            first_gain_grad,
            attend_gain_grad,
            conv_gain_grad,
            second_gain_grad,
            final_gain_grad,
            kernel_local,
        ]
    )
    minors = Doubling(minor)
    turn(clock, minors, first_down_sum, attend_sum, conv_sum)
    (second_down_grad,) = second_down_sum.result()
    turn(clock, minors, first_down_sum, attend_sum)
    turn(clock, first_up_sum)
    (second_up_grad,) = second_up_sum.result()
    turn(clock, minors, first_up_sum)
    expand_grad, project_grad = conv_sum.result((wide, narrow))
    turn(clock, minors, first_up_sum, first_down_sum)
    query_grad, key_grad, value_grad, output_grad = attend_sum.result((narrow,) * 4)
    turn(clock, minors, first_up_sum)
    minor_sums = minors.result(clock)
    (first_up_grad,) = first_up_sum.result()
    (first_up_grad,) = clock(first_up_grad)
    (first_down_grad,) = first_down_sum.result()
    shift_grad, scale_grad = sums
    taps = conv_kernel.shape[0]
    return (
        layer_out,
        upstream,
        first_up_grad,
        first_down_grad,
        query_grad,
        key_grad,
        value_grad,
        output_grad,
        expand_grad,
        project_grad,
        second_up_grad,
        second_down_grad,
        minor_sums[0],
        minor_sums[1],
        minor_sums[2],
        minor_sums[3],
        minor_sums[4],
        minor_sums[5 : 5 + taps],
        scale_grad,
        shift_grad,
        mean,
        variance,
    )


def solution(mesh):
    placed = (
        P(("dp", "fsdp"), None),
        P(("dp", "fsdp"), None),
        P(("dp", "fsdp"), None),
        P(),
        P(None, "fsdp"),
        P(None, "fsdp"),
        P(),
        P(None, "fsdp"),
        P(None, "fsdp"),
        P(None, "fsdp"),
        P(None, "fsdp"),
        P(),
        P(None, "fsdp"),
        P(),
        P(),
        P(),
        P(None, "fsdp"),
        P(),
        P(None, "fsdp"),
        P(None, "fsdp"),
        P(),
    )
    return jax.shard_map(
        body,
        mesh=mesh,
        in_specs=placed,
        out_specs=(
            P(("dp", "fsdp"), None),
            P(("dp", "fsdp"), None),
            P(None, "fsdp"),
            P(None, "fsdp"),
            P(None, "fsdp"),
            P(None, "fsdp"),
            P(None, "fsdp"),
            P(None, "fsdp"),
            P(None, "fsdp"),
            P(None, "fsdp"),
            P(None, "fsdp"),
            P(None, "fsdp"),
            P(),
            P(),
            P(),
            P(),
            P(),
            P(),
            P(),
            P(),
            P(),
            P(),
        ),
        check_vma=False,
    )
```
